32 devices in a mesh: dp: 8 (over z, y), mp: 4 (over x, core).
Axes of the slice: x: 2, y: 2, z: 4, core: 2. Of those that a mesh axis runs over, the one named last changes fastest.
Arguments:
- layer_input: bfloat16 [8192, 768], P(('dp', 'mp')), may hold values from -6 to 6
- doc_ids: int32 [8192], P('dp'), may hold values from 0 to 8191, as said below
- type_ids: int32 [8192], P('dp'), may hold values from 0 to 1, as said below
- positions: int32 [8192], P('dp'), may hold values from 0 to 799, as said below
- query_weight: bfloat16 [768, 768], P('dp', 'mp'), may hold values from -0.21875 to 0.21875
- key_weight: bfloat16 [768, 768], P('dp', 'mp'), may hold values from -0.21875 to 0.21875
- value_weight: bfloat16 [768, 768], P('dp', 'mp'), may hold values from -0.21875 to 0.21875
- pos_kernel: bfloat16 [768, 768], P('dp', 'mp'), may hold values from -0.21875 to 0.21875
- out_weight: bfloat16 [768, 768], P('mp', 'dp'), may hold values from -1.25 to 1.25
- inner_weight: bfloat16 [768, 3072], P('dp', 'mp'), may hold values from -0.21875 to 0.21875
- outer_weight: bfloat16 [3072, 768], P('mp', 'dp'), may hold values from -0.109375 to 0.109375
- content_bias: float32 [12, 64], P('mp'), may hold values from -3 to 3
- pos_bias: float32 [12, 64], P('mp'), may hold values from -3 to 3
- type_bias: float32 [12, 64], P('mp'), may hold values from -3 to 3
- value_bias: float32 [12, 64], P('mp'), may hold values from -1.2 to 1.2
- type_embed: float32 [2, 12, 64], P(None, 'mp'), may hold values from -3 to 3
- inner_bias: float32 [3072], P('mp'), may hold values from -3 to 3
- attn_bias: float32 [768], replicated, may hold values from -3 to 3
- ffn_bias: float32 [768], replicated, may hold values from -3 to 3
- attn_gain: float32 [768], replicated, may hold values from 0.5 to 1.5
- attn_shift: float32 [768], replicated, may hold values from -3 to 3
- ffn_gain: float32 [768], replicated, may hold values from 0.5 to 1.5
- ffn_shift: float32 [768], replicated, may hold values from -3 to 3
- out_grad: bfloat16 [8192, 768], P(('dp', 'mp')), may hold values from -6 to 6
Outputs:
- layer_output: bfloat16 [8192, 768], P(('dp', 'mp'))
- input_grad: bfloat16 [8192, 768], P(('dp', 'mp'))
- query_weight_grad: float32 [768, 768], P('dp', 'mp')
- key_weight_grad: float32 [768, 768], P('dp', 'mp')
- value_weight_grad: float32 [768, 768], P('dp', 'mp')
- pos_kernel_grad: float32 [768, 768], P('dp', 'mp')
- out_weight_grad: float32 [768, 768], P('mp', 'dp')
- inner_weight_grad: float32 [768, 3072], P('dp', 'mp')
- outer_weight_grad: float32 [3072, 768], P('mp', 'dp')
- content_bias_grad: float32 [12, 64], P('mp')
- pos_bias_grad: float32 [12, 64], P('mp')
- type_bias_grad: float32 [12, 64], P('mp')
- value_bias_grad: float32 [12, 64], P('mp')
- type_embed_grad: float32 [2, 12, 64], P(None, 'mp')
- inner_bias_grad: float32 [3072], P('mp')
- attn_bias_grad: float32 [768], replicated
- ffn_bias_grad: float32 [768], replicated
- attn_gain_grad: float32 [768], replicated
- attn_shift_grad: float32 [768], replicated
- ffn_gain_grad: float32 [768], replicated
- ffn_shift_grad: float32 [768], replicated
The draws below stay inside these ranges and needn't reach their ends.
Inputs may be any that keep to these rules, and one draw needn't show every extreme that they name: `doc_ids`: a document's id is the index, among all tokens, of its last token, so ids never fall along the tokens; a document never crosses the boundary of a sequence of 1024 tokens; each document holds at most 800 tokens, and at least 60 unless it ends a sequence; some document holds exactly 800. `type_ids`: within each document, type 0 up to a point and type 1 from there. `positions`: a token's place within its document, counted from 0.
All inputs are finite; a program needn't handle non-finite values.
Results may differ from the reference program's by a relative error of at most 0.034.
Values may be sent and summed in bfloat16 or wider, within the bound.
A program may use at most 128 MiB of HBM per device.

```python
import math
import jax
import jax.numpy as jnp
from jax import lax

D = 768
H = 12
DH = 64
F = 3072
SEQ = 1024
DOC_MAX = 800
DOC_MIN = 60
TOKENS = 8192


def doc_layout(key):
    seq_count = TOKENS // SEQ
    doc_slots = SEQ // DOC_MIN + 1
    folded = jax.random.fold_in(key, 11)
    len_key, long_key, cut_key = jax.random.split(folded, 3)
    lengths = jax.random.randint(len_key, (seq_count, doc_slots), DOC_MIN, DOC_MAX + 1)
    chosen = jax.random.randint(long_key, (), 0, seq_count)
    leading = jnp.where(jnp.arange(seq_count) == chosen, DOC_MAX, lengths[:, 0])
    lengths = jnp.concatenate([leading[:, None], lengths[:, 1:]], axis=1)
    doc_ends = jnp.cumsum(lengths, axis=1)
    places = jnp.arange(SEQ)
    passed = (doc_ends[:, None, :] <= places[None, :, None]).astype(jnp.int32)
    local_ids = jnp.sum(passed, axis=-1)
    starts = jnp.sum(passed * lengths[:, None, :], axis=-1)
    offsets = places[None, :] - starts
    cut_points = jax.random.randint(cut_key, (seq_count, doc_slots), 1, lengths)
    slot_index = jnp.arange(doc_slots)
    own_slot = local_ids[:, :, None] == slot_index[None, None, :]
    cut_of = jnp.sum(jnp.where(own_slot, cut_points[:, None, :], 0), axis=-1)
    length_of = jnp.sum(jnp.where(own_slot, lengths[:, None, :], 0), axis=-1)
    type_rows = (offsets >= cut_of).astype(jnp.int32)
    last_place = jnp.minimum(starts + length_of, SEQ) - 1
    global_ids = last_place + (jnp.arange(seq_count) * SEQ)[:, None]
    return (global_ids.reshape(-1).astype(jnp.int32), type_rows.reshape(-1), offsets.reshape(-1).astype(jnp.int32))


def draw_doc_ids(key, part):
    return doc_layout(key)[0]


def draw_type_ids(key, part):
    return doc_layout(key)[1]


def draw_positions(key, part):
    return doc_layout(key)[2]


def spiked(drawn, key, source, target, parts, factor):
    def block_of(dim):
        return (jnp.arange(drawn.shape[dim]) // (drawn.shape[dim] // parts)).reshape((-1,) + (1,) * (drawn.ndim - 1 - dim))

    first = jax.random.permutation(key, parts)[block_of(target)]
    other_side = (block_of(target) + parts // 2) % parts
    return jnp.where((block_of(source) == first) | (block_of(source) == other_side), factor * drawn, drawn)


def block_levels(key, dims, cuts, least, top_value):
    def one(axis_at, shards_of):
        steps = jax.random.uniform(jax.random.fold_in(jax.random.fold_in(key, 6), axis_at), (shards_of,), jnp.float32, least / len(cuts), top_value / len(cuts))
        return jnp.repeat(jnp.exp(steps), dims[axis_at] // shards_of).reshape((-1,) + (1,) * (len(dims) - axis_at - 1))

    level = one(*cuts[0])
    for cut in cuts[1:]:
        level = level * one(*cut)
    return level


def noise(rng, extent, scale, bound, cuts=(), held_as=jnp.bfloat16):
    loudness = block_levels(rng, extent, cuts, -0.22, 0.18) if cuts else 1.0
    array = jax.random.normal(rng, extent, jnp.float32) * scale * loudness
    return jnp.minimum(jnp.maximum(array, -bound), bound).astype(held_as)


def gaussian_with(rng, dims, width, limit, cuts, heavy, kind=jnp.bfloat16):
    drawn = width * jax.random.normal(rng, dims, jnp.float32)
    if cuts:
        drawn = drawn * block_levels(rng, dims, cuts, -0.22, 0.18)
    return jnp.clip(spiked(drawn, jax.random.fold_in(rng, 3), *heavy), -limit, limit).astype(kind)


def setup_inputs(seed: int = 0) -> dict:
    key_of = jax.random.split(jax.random.key(seed), 25)
    return {
        "layer_input": gaussian_with(key_of[0], (TOKENS, D), 1.0, 6.0, ((0, 32),), (0, 1, 32, 2.75)),
        "doc_ids": draw_doc_ids(jax.random.fold_in(key_of[24], 71), 0),
        "type_ids": draw_type_ids(jax.random.fold_in(key_of[24], 71), 0),
        "positions": draw_positions(jax.random.fold_in(key_of[24], 71), 0),
        "query_weight": noise(key_of[4], (D, H * DH), D ** -0.5, 0.21875, ((0, 8), (1, 4))),
        "key_weight": noise(key_of[5], (D, H * DH), D ** -0.5, 0.21875, ((0, 8), (1, 4))),
        "value_weight": noise(key_of[6], (D, H * DH), D ** -0.5, 0.21875, ((0, 8), (1, 4))),
        "pos_kernel": noise(key_of[7], (D, H * DH), D ** -0.5, 0.21875, ((0, 8), (1, 4))),
        "out_weight": noise(key_of[8], (H * DH, D), (H * DH // 32) ** -0.5, 1.25, ((0, 4), (1, 8))),
        "inner_weight": noise(key_of[9], (D, F), D ** -0.5, 0.21875, ((0, 8), (1, 4))),
        "outer_weight": noise(key_of[10], (F, D), F ** -0.5, 0.109375, ((0, 4), (1, 8))),
        "content_bias": noise(key_of[11], (H, DH), 0.5, 3.0, ((0, 4),), jnp.float32),
        "pos_bias": noise(key_of[12], (H, DH), 0.5, 3.0, ((0, 4),), jnp.float32),
        "type_bias": noise(key_of[13], (H, DH), 0.5, 3.0, ((0, 4),), jnp.float32),
        "value_bias": noise(key_of[14], (H, DH), 0.2, 1.2, ((0, 4),), jnp.float32),
        "type_embed": noise(key_of[15], (2, H, DH), 0.5, 3.0, ((1, 4),), jnp.float32),
        "inner_bias": noise(key_of[16], (F,), 0.5, 3.0, ((0, 4),), jnp.float32),
        "attn_bias": noise(key_of[17], (D,), 0.5, 3.0, (), jnp.float32),
        "ffn_bias": noise(key_of[18], (D,), 0.5, 3.0, (), jnp.float32),
        "attn_gain": jnp.clip(1.0 + 0.1 * jax.random.normal(key_of[19], (D,), jnp.float32), 0.5, 1.5),
        "attn_shift": noise(key_of[20], (D,), 0.5, 3.0, (), jnp.float32),
        "ffn_gain": jnp.clip(1.0 + 0.1 * jax.random.normal(key_of[21], (D,), jnp.float32), 0.5, 1.5),
        "ffn_shift": noise(key_of[22], (D,), 0.5, 3.0, (), jnp.float32),
        "out_grad": gaussian_with(key_of[23], (TOKENS, D), 1.0, 6.0, ((0, 32),), (0, 1, 32, 2.75)),
    }


@jax.custom_vjp
def low(v):
    return lax.optimization_barrier(v.astype(jnp.bfloat16)).astype(jnp.float32)

@jax.custom_vjp
def low_back(v):
    return v

def low_keep(v):
    return (low(v), None)

def low_pass(kept, grad):
    return (grad,)

def back_keep(v):
    return (v, None)

def back_low(kept, grad):
    return (low(grad),)
low.defvjp(low_keep, low_pass)
low_back.defvjp(back_keep, back_low)
precise = lax.Precision.HIGHEST

def row_norm(summed, gain_vec, shift_vec):
    center = summed - lax.optimization_barrier(jnp.mean(summed, axis=-1, keepdims=True))
    spread = lax.optimization_barrier(jnp.mean(center * center, axis=-1, keepdims=True))
    return center * lax.rsqrt(spread + 1e-06) * gain_vec + shift_vec

def gelu_tanh(values):
    return 0.5 * values * (1.0 + jnp.tanh(0.7978845608028654 * (values + 0.044715 * values * values * values)))

def frequencies(half_count, model_width):
    return 1.0 / 10000.0 ** (jnp.arange(half_count, dtype=jnp.float32) * (2.0 / model_width))

def one_sequence(params, seq_input, doc_row, type_row, place_row):
    w_query, w_key, w_value, w_pos, w_out, w_inner, w_outer, c_bias, p_bias, t_bias, v_bias, t_embed, i_bias, a_bias, f_bias, a_gain, a_shift, f_gain, f_shift = params
    seq_len = seq_input.shape[0]
    half_width = D // 2
    score_scale = 1.0 / math.sqrt(DH)
    query_full = low_back(jnp.dot(seq_input, w_query, precision=precise)).reshape(seq_len, H, DH)
    key_rows = low_back(low(jnp.dot(seq_input, w_key, precision=precise))).reshape(seq_len, H, DH)
    value_rows = low_back(low(jnp.dot(seq_input, w_value, precision=precise) + v_bias.reshape(-1))).reshape(seq_len, H, DH)
    q_content = low(query_full + c_bias)
    q_pos = low(query_full + p_bias)
    q_type = query_full + t_bias
    type_terms = jnp.einsum('shd,bhd->bhs', q_type, t_embed, precision=precise)
    angles = place_row.astype(jnp.float32)[:, None] * frequencies(half_width, D)[None, :]
    sine_rows = jnp.sin(angles)
    cosines = jnp.cos(angles)
    z_full = low_back(jnp.einsum('shd,ehd->hse', q_pos, w_pos.reshape(D, H, DH), precision=precise))
    z_sin = z_full[..., :half_width]
    z_cos = z_full[..., half_width:]
    query_rot = low(jnp.concatenate([z_sin * sine_rows + z_cos * cosines, z_cos * sine_rows - z_sin * cosines], axis=-1))
    key_rot = low(jnp.concatenate([cosines, sine_rows], axis=-1))
    content = jnp.einsum('qhd,khd->hqk', q_content, key_rows, precision=precise)
    position = jnp.einsum('hqe,ke->hqk', query_rot, key_rot, precision=precise)
    same_type = (type_row[:, None] == type_row[None, :])[None]
    type_part = jnp.where(same_type, type_terms[1][:, :, None], type_terms[0][:, :, None])
    scores = low_back(score_scale * (content + position + type_part))
    same_doc = (doc_row[:, None] == doc_row[None, :])[None]
    masked = jnp.where(same_doc, scores, -1e+30)
    probs = jax.nn.softmax(masked, axis=-1)
    attended = low_back(low(jnp.einsum('hqk,khd->qhd', low(probs), value_rows, precision=precise))).reshape(seq_len, H * DH)
    branch = low_back(jnp.dot(attended, w_out, precision=precise))
    hidden_one = row_norm(seq_input + branch + a_bias, a_gain, a_shift)
    inner_act = low_back(jnp.dot(low(hidden_one), w_inner, precision=precise) + i_bias)
    activation = low(gelu_tanh(inner_act))
    ffn_out = low_back(jnp.dot(activation, w_outer, precision=precise))
    return row_norm(hidden_one + ffn_out + f_bias, f_gain, f_shift)

def reference(layer_input, doc_ids, type_ids, positions, query_weight, key_weight, value_weight, pos_kernel, out_weight, inner_weight, outer_weight, content_bias, pos_bias, type_bias, value_bias, type_embed, inner_bias, attn_bias, ffn_bias, attn_gain, attn_shift, ffn_gain, ffn_shift, out_grad):
    params = tuple((source.astype(jnp.float32) for source in (query_weight, key_weight, value_weight, pos_kernel, out_weight, inner_weight, outer_weight, content_bias, pos_bias, type_bias, value_bias, type_embed, inner_bias, attn_bias, ffn_bias, attn_gain, attn_shift, ffn_gain, ffn_shift)))
    seq_count = TOKENS // SEQ
    inputs = layer_input.astype(jnp.float32).reshape(seq_count, SEQ, D)
    doc_rows = doc_ids.reshape(seq_count, SEQ)
    type_rows = type_ids.reshape(seq_count, SEQ)
    place_rows = positions.reshape(seq_count, SEQ)

    def forward(weights, seq_inputs):
        checked = jax.checkpoint(one_sequence)

        def scan_step(carry, pieces):
            return (carry, checked(weights, pieces[0], pieces[1], pieces[2], pieces[3]))
        unused, outputs = lax.scan(scan_step, jnp.zeros((), jnp.float32), (seq_inputs, doc_rows, type_rows, place_rows))
        return outputs
    outputs, pullback = jax.vjp(forward, params, inputs)
    grads, input_grad = pullback(out_grad.astype(jnp.float32).reshape(seq_count, SEQ, D))
    return (outputs.reshape(TOKENS, D).astype(jnp.bfloat16), input_grad.reshape(TOKENS, D).astype(jnp.bfloat16), grads[0], grads[1], grads[2], grads[3], grads[4], grads[5], grads[6], grads[7], grads[8], grads[9], grads[10], grads[11], grads[12], grads[13], grads[14], grads[15], grads[16], grads[17], grads[18])
```

```python
import math

import jax
import jax.numpy as jnp
import numpy as np
from jax import lax
from jax.experimental import pallas as pl
from jax.experimental.pallas import tpu as pltpu
from jax.sharding import PartitionSpec as P

f32 = jnp.float32
bf16 = jnp.bfloat16
MESH = pl.DeviceIdType.MESH
MASK = -1e30
DOC_LEAST = 60
NN = (((1,), (0,)), ((), ()))
NT = (((1,), (1,)), ((), ()))
TN = (((0,), (0,)), ((), ()))


def mm(a, b, dims):
    return lax.dot_general(a, b, dims, preferred_element_type=f32)


def lane_of(rows):
    return lax.broadcasted_iota(jnp.int32, (rows, 128), 1)


def low_half(value):
    return jnp.where(lane_of(value.shape[0]) < 64, value, 0.0)


def swap(value):
    return pltpu.roll(value, 64, 1)


class Links:
    def __init__(self, send_sems, recv_sems):
        self.send_sems = send_sems
        self.recv_sems = recv_sems
        self.used = 0
        self.sent = []

    def start(self, src, dst, where):
        copy = pltpu.make_async_remote_copy(
            src_ref=src,
            dst_ref=dst,
            send_sem=self.send_sems.at[self.used],
            recv_sem=self.recv_sems.at[self.used],
            device_id=where,
            device_id_type=MESH,
        )
        self.used += 1
        self.sent.append(copy)
        copy.start()
        return copy

    def drain(self, some=None):
        for copy in some or self.sent:
            copy.wait_send()
            self.sent = [other for other in self.sent if other is not copy]


def norm_stats(summed):
    center = summed - jnp.mean(summed, axis=-1, keepdims=True)
    spread = jnp.mean(center * center, axis=-1, keepdims=True)
    inv_std = lax.rsqrt(spread + 1e-06)
    return center * inv_std, inv_std


def norm_back(grad, normed, inv_std, gain):
    scaled = grad * gain
    return inv_std * (
        scaled
        - jnp.mean(scaled, axis=-1, keepdims=True)
        - normed * jnp.mean(scaled * normed, axis=-1, keepdims=True)
    )


def col_sum(value):
    return jnp.sum(value, axis=0, keepdims=True)


def layer_kernel(
    x_ref, og_ref, qmeta_ref, kmeta_ref, w1_ref, wo_ref, wi_ref, wu_ref, small_ref, ln_ref, ib_ref,
    ta_ref, tb_ref,
    out_ref, ig_ref, dw1_ref, dwo_ref, dwi_ref, dwu_ref, vec_ref, hs_ref,
    xs, hb, eb2, eb1, part_a, part_b, r1a, r1b, r2a, r2b, sxa, sxb, own_f,
    table, rel, qa, qr, ka, va, q32, es, a32, attnp, act, slope, igr,
    h1, n1, e2, inv1, e1, dkv, drt, dqkv, flip,
    send_sems, recv_sems,
):
    rows = x_ref.shape[0]
    width = x_ref.shape[1]
    hidden = wi_ref.shape[1]
    members = xs.shape[0]
    seq = members * rows
    heads = es.shape[0]
    half = width // 2
    scale = 0.125
    me = lax.axis_index("mp")
    core = lax.rem(me, 2)
    side = lax.div(me, 2)
    mate = me + 1 - 2 * core
    across = lax.rem(me + 2, 4)
    diag = lax.rem(mate + 2, 4)
    links = Links(send_sems, recv_sems)
    to_mate = {"mp": mate}
    to_across = {"mp": across}

    barrier = pltpu.get_barrier_semaphore()
    for where in (to_mate, to_across):
        pl.semaphore_signal(barrier, inc=1, device_id=where, device_id_type=MESH)
    pl.semaphore_wait(barrier, 2)

    def gather_start(buf):
        a = links.start(buf.at[me], buf.at[me], to_across)
        b = links.start(buf.at[me], buf.at[me], to_mate)
        return a, b

    def gather_forward(buf, first):
        first.wait_recv()
        return links.start(buf.at[across], buf.at[across], to_mate)

    xs[me] = x_ref[...]
    x_a, x_b = gather_start(xs)

    steps = tb_ref.shape[1]

    def table_step(u, carry):
        sa = ta_ref[0, pl.ds(u, 1), :]
        ca = ta_ref[1, pl.ds(u, 1), :]
        at = pl.multiple_of(u * steps, steps)
        table[pl.ds(at, steps), :half] = (sa * tb_ref[1] - ca * tb_ref[0]).astype(bf16)
        table[pl.ds(at, steps), half:] = (ca * tb_ref[1] + sa * tb_ref[0]).astype(bf16)
        return carry

    lax.fori_loop(0, ta_ref.shape[1], table_step, 0)

    ri = lax.broadcasted_iota(jnp.int32, (rows, rows), 0)
    ci = lax.broadcasted_iota(jnp.int32, (rows, rows), 1)
    flip[...] = jnp.where(ri + ci == rows - 1, 1.0, 0.0).astype(bf16)

    def rel_step(i, carry):
        at = pl.ds(pl.multiple_of(i * 256, 256), 256)
        got = mm(table[at, :], w1_ref[:, 512:768], NN)
        rel[0, at, :] = low_half(swap(got[:, :128])).astype(bf16)
        rel[1, at, :] = low_half(got[:, 128:]).astype(bf16)
        rel[2, at, :] = low_half(swap(got[:, 128:])).astype(bf16)
        return carry

    lax.fori_loop(0, 2 * seq // 256, rel_step, 0)

    def project(o):
        at = pl.ds(pl.multiple_of(o * rows, rows), rows)
        got = mm(xs[o], w1_ref[:, :640], NN)
        lane = lane_of(rows)
        qmeta = qmeta_ref[at, :].astype(f32)
        kmeta = kmeta_ref[at, :].astype(f32)
        typed = qmeta[:, 64:65]
        for h in range(heads):
            kv = got[:, 128 * h : 128 * h + 128]
            ka[h, at, :] = jnp.where(lane < 64, kv, kmeta).astype(bf16)
            vrow = swap(kv) + small_ref[8 * h + 5 : 8 * h + 6, :]
            va[h, at, :] = jnp.where(lane < 64, vrow, jnp.where(lane < 66, 1.0, 0.0)).astype(bf16)
            q = got[:, 384:512] if h < 2 else got[:, 512:640]
            if h == 1:
                q = swap(q)
            q = low_half(q)
            q32[h, at, :] = q
            qt = q + small_ref[8 * h + 2 : 8 * h + 3, :]
            ct0 = jnp.sum(qt * small_ref[8 * h + 3 : 8 * h + 4, :], axis=1, keepdims=True)
            ct1 = jnp.sum(qt * small_ref[8 * h + 4 : 8 * h + 5, :], axis=1, keepdims=True)
            diff = (ct1 - ct0) * scale
            base = ct0 * scale + diff * (1.0 - typed)
            tilt = diff * (2.0 * typed - 1.0)
            base_hi = base.astype(bf16).astype(f32)
            tilt_hi = tilt.astype(bf16).astype(f32)
            extra = jnp.where(
                lane == 64,
                base_hi,
                jnp.where(
                    lane == 65,
                    base - base_hi,
                    jnp.where(lane == 66, tilt_hi, jnp.where(lane == 67, tilt - tilt_hi, qmeta)),
                ),
            )
            qc = (q + small_ref[8 * h : 8 * h + 1, :]) * scale
            qa[h, at, :] = jnp.where(lane < 64, qc, extra).astype(bf16)
            qr[h, at, :] = low_half((q + small_ref[8 * h + 1 : 8 * h + 2, :]) * scale).astype(bf16)

    project(me)
    x_f = gather_forward(xs, x_a)
    x_b.wait_recv()
    project(mate)
    project(across)
    x_f.wait_recv()
    project(diag)

    wide = seq + rows

    def attend(o):
        at = pl.ds(pl.multiple_of(o * rows, rows), rows)
        window = pl.ds(pl.multiple_of((members - 1 - o) * rows, rows), wide)

        def one_head(h, carry):
            s = mm(qa[h, at, :], ka[h], NT)
            g = mm(qr[h, at, :], rel[h, window, :], NT)
            g = pltpu.roll(g, wide + 1 - rows, 1, stride=1, stride_axis=0)
            s = s + g[:, :seq]
            top = jnp.max(s, axis=1, keepdims=True)
            e = jnp.exp(s - top).astype(bf16)
            es[h, at, :] = e
            o_full = mm(e, va[h], NN)
            inv = 1.0 / o_full[:, 64:65]
            a32[h, at, :] = jnp.where(lane_of(rows) < 64, o_full * inv, inv)
            return carry

        lax.fori_loop(0, heads, one_head, 0)
        first = low_half(a32[0, at, :]) + swap(low_half(a32[1, at, :]))
        attnp[at, :128] = first.astype(bf16)
        attnp[at, 128:] = low_half(a32[2, at, :]).astype(bf16)
        return mm(attnp[at, :], wo_ref[...], NT)

    class Scatter:
        def __init__(self, part, r1, r2, sx):
            self.part, self.r1, self.r2, self.sx = part, r1, r2, sx

        def give(self, kind, value):
            if kind == "diag":
                self.part[diag] = value.astype(bf16)
                self.c_far = links.start(self.part.at[diag], self.r1.at[1 - side], to_mate)
            elif kind == "mate":
                self.part[mate] = value.astype(bf16)
                self.c_near = links.start(self.part.at[mate], self.r1.at[side], to_mate)
            elif kind == "across":
                self.part[across] = value.astype(bf16)
            else:
                own_f[...] = value

        def pass_on(self):
            self.c_far.wait_recv()
            self.sx[...] = (self.part[across].astype(f32) + self.r1[1 - side].astype(f32)).astype(bf16)
            self.c_over = links.start(self.sx, self.r2, to_across)

        def release(self):
            links.drain([self.c_far, self.c_near, self.c_over])

        def take(self):
            self.c_near.wait_recv()
            near = own_f[...] + self.r1[side].astype(f32)
            self.c_over.wait_recv()
            return near + self.r2[...].astype(f32)

    first_red = red = Scatter(part_a, r1a, r2a, sxa)
    red.give("diag", attend(diag))
    red.give("across", attend(across))
    red.pass_on()
    red.give("mate", attend(mate))
    red.give("own", attend(me))
    summed = x_ref[...].astype(f32) + red.take() + ln_ref[0:1, :]
    normed, inv_std = norm_stats(summed)
    n1[...] = normed
    inv1[...] = jnp.broadcast_to(inv_std, inv1.shape)
    h1[...] = normed * ln_ref[1:2, :] + ln_ref[2:3, :]
    hb[me] = h1[...].astype(bf16)
    g_a, g_b = gather_start(hb)

    def ffn(o):
        inner = mm(hb[o], wi_ref[...], NN) + ib_ref[...]
        square = inner * inner
        t = jnp.tanh(0.7978845608028654 * (inner + 0.044715 * square * inner))
        act[o] = (0.5 * inner * (1.0 + t)).astype(bf16)
        slope[o] = (
            0.5 * (1.0 + t)
            + 0.5 * inner * (1.0 - t * t) * 0.7978845608028654 * (1.0 + 3.0 * 0.044715 * square)
        ).astype(bf16)
        return mm(act[o], wu_ref[...], NT)

    def gathered(buf, first, second, block, reducer):
        reducer.give("own", block(me))
        second.wait_recv()
        reducer.give("mate", block(mate))
        forward = gather_forward(buf, first)
        reducer.give("across", block(across))
        forward.wait_recv()
        reducer.give("diag", block(diag))
        reducer.pass_on()

    second_red = red = Scatter(part_b, r1b, r2b, sxb)
    gathered(hb, g_a, g_b, ffn, red)
    summed = h1[...] + red.take() + ln_ref[3:4, :]
    normed, inv_std = norm_stats(summed)
    out_ref[...] = (normed * ln_ref[4:5, :] + ln_ref[5:6, :]).astype(bf16)
    grad = og_ref[...].astype(f32)
    vec_ref[4:5, :] = col_sum(grad * normed)
    vec_ref[5:6, :] = col_sum(grad)
    e2[...] = norm_back(grad, normed, inv_std, ln_ref[4:5, :])
    vec_ref[1:2, :] = col_sum(e2[...])
    eb2[me] = e2[...].astype(bf16)
    g_a, g_b = gather_start(eb2)

    vec_ref[6:8, :] = jnp.zeros((2, width), f32)
    hs_ref[...] = jnp.zeros(hs_ref.shape, f32)

    def ffn_back(o):
        grad_inner = (mm(eb2[o], wu_ref[...], NN) * slope[o].astype(f32)).astype(bf16)
        igr[o] = grad_inner
        vec_ref[6:7, :hidden] += col_sum(grad_inner.astype(f32))
        return mm(grad_inner, wi_ref[...], NT)

    first_red.release()
    red = Scatter(part_a, r1a, r2a, sxa)
    gathered(eb2, g_a, g_b, ffn_back, red)
    flat = lambda ref: ref[...].reshape(seq, ref.shape[2])
    dwu_ref[...] = mm(flat(eb2), flat(act), TN).astype(bf16)
    dwi_ref[...] = mm(flat(hb), flat(igr), TN).astype(bf16)

    grad = e2[...] + red.take()
    vec_ref[2:3, :] = col_sum(grad * n1[...])
    vec_ref[3:4, :] = col_sum(grad)
    e1[...] = norm_back(grad, n1[...], inv1[:, :1], ln_ref[1:2, :])
    vec_ref[0:1, :] = col_sum(e1[...])
    eb1[me] = e1[...].astype(bf16)
    g_a, g_b = gather_start(eb1)

    dkv[...] = jnp.zeros(dkv.shape, f32)
    drt[...] = jnp.zeros(drt.shape, f32)

    def attend_back(o):
        at = pl.ds(pl.multiple_of(o * rows, rows), rows)
        lo = pl.multiple_of((members - 1 - o) * rows, rows)
        window = pl.ds(lo, wide)
        d_all = mm(eb1[o], wo_ref[...], NN).astype(bf16).astype(f32)
        lane = lane_of(rows)
        typed = qmeta_ref[at, :].astype(f32)[:, 64:65]
        packed = []
        for h in range(heads):
            d_out = d_all[:, :128] if h < 2 else d_all[:, 128:]
            if h == 1:
                d_out = swap(d_out)
            kept = a32[h, at, :]
            d_out = low_half(d_out * kept[:, 64:65]).astype(bf16).astype(f32)
            d_row = -jnp.sum(d_out * kept, axis=1, keepdims=True)
            d_hi = d_row.astype(bf16).astype(f32)
            d_aug = jnp.where(lane == 64, d_hi, jnp.where(lane == 65, d_row - d_hi, d_out)).astype(bf16)
            e = es[h, at, :]
            ds = (e.astype(f32) * mm(d_aug, va[h], NT)).astype(bf16)
            dkv[h, 64:128, :] += mm(d_aug, e, TN)[:64]
            dkv[h, 0:64, :] += mm(qa[h, at, :], ds, TN)[:64]
            dq = mm(ds, ka[h], NN) * scale
            turned = mm(flip[...], ds, NN)
            turned = jnp.concatenate([turned, jnp.zeros((rows, rows), f32)], axis=1)
            dg = pltpu.roll(turned, 0, 1, stride=1, stride_axis=0).astype(bf16)
            dqr = mm(dg, rel[h, window, :], NN) * scale
            qr_turned = mm(flip[...], qr[h, at, :], NN).astype(bf16)
            drt[64 * h + 64 : 64 * h + 128, window] += mm(qr_turned, dg, TN)[:64]
            hs_ref[8 * h + 1 : 8 * h + 2, :] += col_sum(dqr)
            dqr_hi = dqr.astype(bf16)
            dqr_lo = (dqr - dqr_hi.astype(f32)).astype(bf16)
            dqr = mm(flip[...], dqr_hi, NN) + mm(flip[...], dqr_lo, NN)
            total = dq[:, 64:65]
            ones = dq[:, 66:67]
            same = jnp.where(typed > 0.5, ones, total - ones)
            other = total - same
            dqt = other * small_ref[8 * h + 3 : 8 * h + 4, :] + same * small_ref[8 * h + 4 : 8 * h + 5, :]
            qt = q32[h, at, :] + small_ref[8 * h + 2 : 8 * h + 3, :]
            hs_ref[8 * h : 8 * h + 1, :] += col_sum(dq)
            hs_ref[8 * h + 2 : 8 * h + 3, :] += col_sum(dqt)
            hs_ref[8 * h + 3 : 8 * h + 4, :] += col_sum(other * qt)
            hs_ref[8 * h + 4 : 8 * h + 5, :] += col_sum(same * qt)
            packed.append(low_half(dq + dqr + dqt))
        dqkv[at, 384:512] = (packed[0] + swap(packed[1])).astype(bf16)
        dqkv[at, 512:640] = packed[2].astype(bf16)

    attend_back(me)
    g_b.wait_recv()
    attend_back(mate)
    g_f = gather_forward(eb1, g_a)
    attend_back(across)
    g_f.wait_recv()
    attend_back(diag)
    dwo_ref[...] = mm(flat(eb1), attnp[...], TN).astype(bf16)

    for h in range(heads):
        turned = jnp.transpose(dkv[h], (1, 0)).astype(bf16)
        dqkv[:, 128 * h : 128 * h + 128] = turned
        hs_ref[8 * h + 5 : 8 * h + 6, :] = swap(col_sum(turned.astype(f32)))

    def input_back(o):
        at = pl.ds(pl.multiple_of(o * rows, rows), rows)
        return mm(dqkv[at, :], w1_ref[:, :640], NT)

    second_red.release()
    red = Scatter(part_b, r1b, r2b, sxb)
    red.give("diag", input_back(diag))
    red.give("across", input_back(across))
    red.pass_on()
    red.give("mate", input_back(mate))
    red.give("own", input_back(me))
    dw1_ref[:, :512] = mm(flat(xs), dqkv[:, :512], TN).astype(bf16)
    tail = mm(flat(xs), dqkv[:, 512:640], TN)
    d_rel = jnp.transpose(drt[...], (1, 0)).astype(bf16)
    d_pos = mm(table[...], d_rel, TN)
    dw1_ref[:, 512:640] = (tail + d_pos[:, :128]).astype(bf16)
    dw1_ref[:, 640:768] = d_pos[:, 128:].astype(bf16)
    ig_ref[...] = (e1[...] + red.take()).astype(bf16)
    links.drain()


def angle_tables(seq, width):
    half = width // 2
    freq = 1.0 / 10000.0 ** (np.arange(half, dtype=np.float64) * (2.0 / width))
    steps = 32
    coarse = (seq - 1 - steps * np.arange(2 * seq // steps, dtype=np.float64))[:, None] * freq[None, :]
    fine = np.arange(steps, dtype=np.float64)[:, None] * freq[None, :]
    return (
        np.stack([np.sin(coarse), np.cos(coarse)]).astype(np.float32),
        np.stack([np.sin(fine), np.cos(fine)]).astype(np.float32),
    )


def per_device(
    layer_input, doc_ids, type_ids, positions, query_weight, key_weight, value_weight, pos_kernel,
    out_weight, inner_weight, outer_weight, content_bias, pos_bias, type_bias, value_bias, type_embed,
    inner_bias, attn_bias, ffn_bias, attn_gain, attn_shift, ffn_gain, ffn_shift, out_grad,
):
    rows, width = layer_input.shape
    seq = doc_ids.shape[0]
    heads, depth = content_bias.shape
    hidden = inner_weight.shape[1]
    shard = query_weight.shape[0]
    members = seq // rows

    q3, k3, v3, p3 = (w.reshape(shard, heads, depth) for w in (query_weight, key_weight, value_weight, pos_kernel))
    kv = jnp.stack([k3, v3], axis=2).reshape(shard, 2 * heads * depth)
    out_t = jnp.pad(out_weight.T, ((0, 0), (0, 256 - heads * depth)))
    mine = jnp.concatenate([kv, query_weight, pos_kernel, out_t, inner_weight, outer_weight.T], axis=1)
    full = lax.all_gather(mine, "dp", axis=0, tiled=True)
    w1 = full[:, :768]
    wo = full[:, 768:1024]
    wi = full[:, 1024 : 1024 + hidden]
    wu = full[:, 1024 + hidden :]

    slots = seq // DOC_LEAST + 2
    ends = doc_ids - lax.axis_index("dp") * seq
    slot = jnp.where(ends == seq - 1, slots - 1, ends // DOC_LEAST)
    lane = jnp.arange(128, dtype=jnp.int32)[None, :]
    hit = lane == slot[:, None] + 68
    kind = type_ids[:, None].astype(f32)
    qmeta = jnp.where(lane == 64, kind, jnp.where(hit, 1.0, 0.0)).astype(bf16)
    kmeta = jnp.where(
        (lane == 64) | (lane == 65),
        1.0,
        jnp.where(
            (lane == 66) | (lane == 67),
            kind,
            jnp.where((lane >= 68) & (lane < 68 + slots) & ~hit, MASK, 0.0),
        ),
    ).astype(bf16)
    zero = jnp.zeros_like(content_bias)
    small = jnp.stack(
        [content_bias, pos_bias, type_bias, type_embed[0], type_embed[1], value_bias, zero, zero], axis=1
    ).reshape(8 * heads, depth)
    small = jnp.pad(small, ((0, 0), (0, 128 - depth)))
    ln = jnp.stack([attn_bias, attn_gain, attn_shift, ffn_bias, ffn_gain, ffn_shift])
    ta, tb = angle_tables(seq, width)

    vm = pltpu.VMEM
    block = (members, rows, width)
    scratch = [
        vm(block, bf16), vm(block, bf16), vm(block, bf16), vm(block, bf16),
        vm(block, bf16), vm(block, bf16),
        vm((2, rows, width), bf16), vm((2, rows, width), bf16),
        vm((rows, width), bf16), vm((rows, width), bf16),
        vm((rows, width), bf16), vm((rows, width), bf16),
        vm((rows, width), f32),
        vm((2 * seq, width), bf16),
        vm((heads, 2 * seq, 128), bf16),
        vm((heads, seq, 128), bf16), vm((heads, seq, 128), bf16),
        vm((heads, seq, 128), bf16), vm((heads, seq, 128), bf16),
        vm((heads, seq, 128), f32),
        vm((heads, seq, seq), bf16),
        vm((heads, seq, 128), f32),
        vm((seq, 256), bf16),
        vm((members, rows, hidden), bf16), vm((members, rows, hidden), bf16),
        vm((members, rows, hidden), bf16),
        vm((rows, width), f32), vm((rows, width), f32), vm((rows, width), f32),
        vm((rows, 128), f32), vm((rows, width), f32),
        vm((heads, 128, seq), f32),
        vm((256, 2 * seq), f32),
        vm((seq, 640), bf16),
        vm((rows, rows), bf16),
        pltpu.SemaphoreType.DMA((32,)), pltpu.SemaphoreType.DMA((32,)),
    ]
    sds = jax.ShapeDtypeStruct
    out, in_grad, dw1, dwo, dwi, dwu, vec, hs = pl.pallas_call(
        layer_kernel,
        out_shape=[
            sds((rows, width), bf16), sds((rows, width), bf16), sds((width, 768), bf16),
            sds((width, 256), bf16), sds((width, hidden), bf16), sds((width, hidden), bf16),
            sds((8, width), f32), sds((8 * heads, 128), f32),
        ],
        in_specs=[pl.BlockSpec(memory_space=pltpu.VMEM)] * 13,
        out_specs=[pl.BlockSpec(memory_space=pltpu.VMEM)] * 8,
        scratch_shapes=scratch,
        compiler_params=pltpu.CompilerParams(
            collective_id=0, has_side_effects=True, vmem_limit_bytes=67043328
        ),
        name="layer",
    )(layer_input, out_grad, qmeta, kmeta, w1, wo, wi, wu, small, ln, inner_bias.reshape(1, hidden), ta, tb)

    grads = jnp.concatenate([dw1, dwo, dwi, dwu], axis=1)
    grads = lax.psum_scatter(grads, "dp", scatter_dimension=0, tiled=True).astype(f32)
    hs = hs.reshape(heads, 8, 128)[:, :, :depth]
    vecs = lax.psum(lax.psum(vec[:6], "mp"), "dp")
    head_sums, inner_sum = lax.psum((hs, vec[6, :hidden]), "dp")
    dkv3 = grads[:, : 2 * heads * depth].reshape(shard, heads, 2, depth)
    cols = heads * depth
    return (
        out,
        in_grad,
        grads[:, 2 * cols : 3 * cols],
        dkv3[:, :, 0].reshape(shard, cols),
        dkv3[:, :, 1].reshape(shard, cols),
        grads[:, 3 * cols : 4 * cols],
        grads[:, 768 : 768 + cols].T,
        grads[:, 1024 : 1024 + hidden],
        grads[:, 1024 + hidden :].T,
        head_sums[:, 0],
        head_sums[:, 1],
        head_sums[:, 2],
        head_sums[:, 5],
        jnp.stack([head_sums[:, 3], head_sums[:, 4]]),
        inner_sum,
        vecs[0], vecs[1], vecs[2], vecs[3], vecs[4], vecs[5],
    )


def solution(mesh):
    rows = P(("dp", "mp"), None)
    token = P("dp")
    placed = (
        (rows, token, token, token)
        + (P("dp", "mp"),) * 4
        + (P("mp", "dp"), P("dp", "mp"), P("mp", "dp"))
        + (P("mp", None),) * 4
        + (P(None, "mp", None), P("mp"))
        + (P(),) * 6
        + (rows,)
    )
    given = (
        (rows, rows)
        + (P("dp", "mp"),) * 4
        + (P("mp", "dp"), P("dp", "mp"), P("mp", "dp"))
        + (P("mp", None),) * 4
        + (P(None, "mp", None), P("mp"))
        + (P(),) * 6
    )
    return jax.shard_map(per_device, mesh=mesh, in_specs=placed, out_specs=given, check_vma=False)
```

```python
import functools
import math

import jax
import jax.numpy as jnp
import numpy as np
from jax import lax
from jax.experimental import pallas as pl
from jax.experimental.pallas import tpu as pltpu
from jax.sharding import PartitionSpec as P

f32 = jnp.float32
bf16 = jnp.bfloat16
MESH = pl.DeviceIdType.MESH
MASK = -1e30
DOC_LEAST = 60
NN = (((1,), (0,)), ((), ()))
NT = (((1,), (1,)), ((), ()))
TN = (((0,), (0,)), ((), ()))


def mm(a, b, dims):
    return lax.dot_general(a, b, dims, preferred_element_type=f32)


def lane_of(rows):
    return lax.broadcasted_iota(jnp.int32, (rows, 128), 1)


def low_half(value):
    return jnp.where(lane_of(value.shape[0]) < 64, value, 0.0)


def swap(value):
    return pltpu.roll(value, 64, 1)


class Links:
    def __init__(self, send_sems, recv_sems):
        self.send_sems = send_sems
        self.recv_sems = recv_sems
        self.used = 0
        self.sent = []

    def start(self, src, dst, where):
        copy = pltpu.make_async_remote_copy(
            src_ref=src,
            dst_ref=dst,
            send_sem=self.send_sems.at[self.used],
            recv_sem=self.recv_sems.at[self.used],
            device_id=where,
            device_id_type=MESH,
        )
        self.used += 1
        self.sent.append(copy)
        copy.start()
        return copy

    def drain(self, some=None):
        for copy in some or self.sent:
            copy.wait_send()
            self.sent = [other for other in self.sent if other is not copy]


def norm_stats(summed):
    center = summed - jnp.mean(summed, axis=-1, keepdims=True)
    spread = jnp.mean(center * center, axis=-1, keepdims=True)
    inv_std = lax.rsqrt(spread + 1e-06)
    return center * inv_std, inv_std


def norm_back(grad, normed, inv_std, gain):
    scaled = grad * gain
    return inv_std * (
        scaled
        - jnp.mean(scaled, axis=-1, keepdims=True)
        - normed * jnp.mean(scaled * normed, axis=-1, keepdims=True)
    )


def col_sum(value):
    return jnp.sum(value, axis=0, keepdims=True)


class Ring:
    def __init__(self, count):
        mine = lax.axis_index("dp")
        row = lax.rem(mine, 2)
        along = lax.div(mine, 2)
        self.count = count
        self.place = (1 - row) * along + row * (count - 1 - along)

    def at(self, offset):
        place = lax.rem(self.place + (offset + self.count), self.count)
        back = lax.div(place, self.count // 2)
        return (1 - back) * 2 * place + back * (2 * (self.count - 1 - place) + 1)


class Flow:
    def __init__(self, sign, hops, rows, slot):
        self.sign, self.hops, self.rows, self.slot = sign, hops, rows, slot


def flows_of(count, rows):
    near = count // 2 - 1
    if rows % 32:
        return [Flow(1, near + 1, pl.ds(0, rows), 0), Flow(-1, near, pl.ds(0, rows), near + 1)]
    first, second = pl.ds(0, rows // 2), pl.ds(rows // 2, rows // 2)
    return [
        Flow(1, near + 1, first, 0),
        Flow(-1, near + 1, second, near),
        Flow(-1, near, first, near + 1),
        Flow(1, near, second, 0),
    ]


class Spread:
    def __init__(self, links, ring, bufs):
        self.links, self.ring, self.bufs = links, ring, bufs
        self.done = 0
        self.last = max(f.hops for f in flows_of(ring.count, bufs[0].shape[1]))
        self.moves = {}

    def begin(self):
        self.send(0)

    def send(self, s):
        for b, buf in enumerate(self.bufs):
            for f, flow in enumerate(flows_of(self.ring.count, buf.shape[1])):
                if s > 0 and s <= flow.hops:
                    self.moves[b, f].wait_recv()
                if s < flow.hops:
                    ref = buf.at[self.ring.at(-flow.sign * s), flow.rows]
                    self.moves[b, f] = self.links.start(ref, ref, {"dp": self.ring.at(flow.sign)})

    def step(self):
        if self.done < self.last:
            self.done += 1
            self.send(self.done)

    def finish(self):
        while self.done < self.last:
            self.step()


class Collect:
    def __init__(self, links, ring, bufs, gots):
        self.links, self.ring = links, ring
        self.bufs, self.gots = bufs, gots
        self.done = 0
        self.last = max(f.hops for f in flows_of(ring.count, bufs[0].shape[1]))
        self.moves = {}

    def begin(self):
        self.send(0)

    def send(self, s):
        for b, (buf, got) in enumerate(zip(self.bufs, self.gots)):
            for f, flow in enumerate(flows_of(self.ring.count, buf.shape[1])):
                if s > 0 and s <= flow.hops:
                    self.moves[b, f].wait_recv()
                if s < flow.hops:
                    owner = self.ring.at(flow.sign * (flow.hops - s))
                    if s > 0:
                        both = buf[owner, flow.rows].astype(f32) + got[flow.slot + s - 1, flow.rows].astype(f32)
                        buf[owner, flow.rows] = both.astype(bf16)
                    self.moves[b, f] = self.links.start(
                        buf.at[owner, flow.rows], got.at[flow.slot + s, flow.rows], {"dp": self.ring.at(flow.sign)}
                    )

    def step(self):
        if self.done < self.last:
            self.done += 1
            self.send(self.done)

    def finish(self):
        while self.done < self.last:
            self.step()

    def take(self, b, out_ref, columns):
        buf, got = self.bufs[b], self.gots[b]
        mine = self.ring.at(0)
        flows = flows_of(self.ring.count, buf.shape[1])
        for start in sorted({flow.rows.start for flow in flows}):
            total = None
            for flow in flows:
                if flow.rows.start == start:
                    part = got[flow.slot + flow.hops - 1, flow.rows].astype(f32)
                    total = buf[mine, flow.rows].astype(f32) + part if total is None else total + part
                    rows = flow.rows
            out_ref[rows, columns] = total


IN_BOTH = (
    "x_ref", "og_ref", "doc_ref", "kind_ref", "cb_ref", "pb_ref", "tbias_ref", "vb_ref", "te_ref", "ib_ref", "ab_ref",
    "fb_ref", "ag_ref", "as_ref", "fg_ref", "fs_ref", "ta_ref", "tb_ref",
)
IN_RING = (
    "wq_ref", "wk_ref", "wv_ref", "wp_ref", "wo_ref", "wi_ref", "wu_ref",
)
IN_WHOLE = (
    "w1g", "wog", "wig", "wug",
)
OUT_WHOLE = (
    "dwa", "dwb", "dwo", "dwi", "dwu",
)


def layer_kernel(ring_on, names, *refs):
    r = dict(zip(names, refs, strict=True))
    (x_ref, og_ref, doc_ref, kind_ref, cb_ref, pb_ref, tbias_ref, vb_ref, te_ref, ib_ref,
     ab_ref, fb_ref, ag_ref, as_ref, fg_ref, fs_ref, ta_ref, tb_ref) = (r[n] for n in IN_BOTH)
    w1g, wog, wig, wug = (r[n] for n in IN_WHOLE)
    dwa, dwb, dwo, dwi, dwu = (r[n] for n in OUT_WHOLE)
    out_ref, ig_ref = r["out_ref"], r["ig_ref"]
    vec_ref, hs_ref = r["vec"], r["hs"]
    (xs, hb, eb2, eb1, part_a, part_b, r1a, r1b, r2a, r2b, sxa, sxb, own_f,
     table, rel, qa, qr, ka, va, q32, es, a32, attnp, act, slope, igr,
     h1, n1, e2, inv1, e1, dkv, drt, dqkv, flip, qmeta_ref, kmeta_ref, small_ref, ln_ref, ibs,
     send_sems, recv_sems) = (r[n] for n in SCRATCH)
    rows = x_ref.shape[0]
    width = x_ref.shape[1]
    hidden = wig.shape[2]
    members = xs.shape[0]
    seq = members * rows
    heads = es.shape[0]
    half = width // 2
    scale = 0.125
    me = lax.axis_index("mp")
    core = lax.rem(me, 2)
    side = lax.div(me, 2)
    mate = me + 1 - 2 * core
    across = lax.rem(me + 2, 4)
    diag = lax.rem(mate + 2, 4)
    links = Links(send_sems, recv_sems)
    to_mate = {"mp": mate}
    to_across = {"mp": across}

    barrier = pltpu.get_barrier_semaphore()
    peers = [to_mate, to_across]
    if ring_on:
        ring = Ring(w1g.shape[0])
        peers += [{"dp": ring.at(1)}, {"dp": ring.at(-1)}]
    for where in peers:
        pl.semaphore_signal(barrier, inc=1, device_id=where, device_id_type=MESH)
    pl.semaphore_wait(barrier, len(peers))

    def whole(ref):
        return ref[...].reshape(width, ref.shape[2])

    def gather_start(buf):
        a = links.start(buf.at[me], buf.at[me], to_across)
        b = links.start(buf.at[me], buf.at[me], to_mate)
        return a, b

    def gather_forward(buf, first):
        first.wait_recv()
        return links.start(buf.at[across], buf.at[across], to_mate)

    xs[me] = x_ref[...]
    x_a, x_b = gather_start(xs)

    if ring_on:
        shard = w1g.shape[1]
        mine = ring.at(0)
        own_f[...] = jnp.zeros(own_f.shape, f32)
        tiles = []
        for i, name in enumerate(IN_RING[:4]):
            r0, c0 = 128 * (i // 2), 256 * (i % 2)
            own_f[r0 : r0 + shard, c0 : c0 + r[name].shape[1]] = r[name][...].astype(f32)
            tiles.append((own_f[r0 : r0 + shard, c0 : c0 + 128], own_f[r0 : r0 + shard, c0 + 128 : c0 + 256]))
        (qx, qy), (kx, ky), (vx, vy), (px, py) = tiles
        low = lane_of(shard) < 64
        joined = [
            jnp.where(low, kx, swap(vx)),
            jnp.where(low, swap(kx), vx),
            jnp.where(low, ky, swap(vy)),
            qx,
            jnp.where(low, qy, swap(px)),
            jnp.where(low, swap(px), swap(py)),
        ]
        for i, tile in enumerate(joined):
            w1g[mine, :, 128 * i : 128 * i + 128] = tile.astype(bf16)
        spread_1 = Spread(links, ring, [w1g])
        spread_1.begin()
        wo_ref = r["wo_ref"]
        own_f[:, :128] = jnp.zeros((256, 128), f32)
        own_f[: wo_ref.shape[0], :shard] = wo_ref[...].astype(f32)
        wog[mine] = jnp.transpose(own_f[:, :128], (1, 0))[:shard].astype(bf16)
        wig[mine] = r["wi_ref"][...]
        wug[mine] = r["wu_ref"][...]
        spread_2 = Spread(links, ring, [wog, wig])
        spread_3 = Spread(links, ring, [wug])

    small_ref[...] = jnp.zeros(small_ref.shape, f32)
    for h in range(heads):
        for i, ref in enumerate((cb_ref, pb_ref, tbias_ref)):
            small_ref[8 * h + i : 8 * h + i + 1, 0:64] = ref[h : h + 1, :]
        small_ref[8 * h + 3 : 8 * h + 5, 0:64] = te_ref[h]
        small_ref[8 * h + 5 : 8 * h + 6, 0:64] = vb_ref[h : h + 1, :]
    for i, ref in enumerate((ab_ref, ag_ref, as_ref, fb_ref, fg_ref, fs_ref)):
        ln_ref[i : i + 1, :] = ref[...].reshape(1, width)
    ibs[0:1, :] = ib_ref[...].reshape(1, hidden)

    slots = seq // DOC_LEAST + 2
    ends = (doc_ref[...].reshape(1, seq) - lax.axis_index("dp") * seq).astype(f32)
    slot = jnp.where(ends > seq - 1.5, slots - 1.0, jnp.floor((ends + 0.5) * (1.0 / DOC_LEAST)))
    slot = jnp.transpose(jnp.broadcast_to(slot, (128, seq)), (1, 0))
    kind = jnp.transpose(jnp.broadcast_to(kind_ref[...].reshape(1, seq).astype(f32), (128, seq)), (1, 0))
    lane = lane_of(seq)
    hit = jnp.abs(slot + 68.0 - lane.astype(f32)) < 0.5
    qmeta_ref[...] = jnp.where(lane == 64, kind, jnp.where(hit, 1.0, 0.0)).astype(bf16)
    miss = jnp.where(hit, 0.0, MASK)
    kmeta_ref[...] = jnp.where(
        lane < 66, 1.0, jnp.where(lane < 68, kind, jnp.where(lane < 68 + slots, miss, 0.0))
    ).astype(bf16)
    x_f = gather_forward(xs, x_a)
    if ring_on:
        spread_1.step()

    steps = tb_ref.shape[1]

    def table_step(u, carry):
        sa = ta_ref[0, pl.ds(u, 1), :]
        ca = ta_ref[1, pl.ds(u, 1), :]
        at = pl.multiple_of(u * steps, steps)
        table[pl.ds(at, steps), :half] = (sa * tb_ref[1] - ca * tb_ref[0]).astype(bf16)
        table[pl.ds(at, steps), half:] = (ca * tb_ref[1] + sa * tb_ref[0]).astype(bf16)
        return carry

    lax.fori_loop(0, ta_ref.shape[1] // 2, table_step, 0)
    if ring_on:
        spread_1.step()
    lax.fori_loop(ta_ref.shape[1] // 2, ta_ref.shape[1], table_step, 0)

    ri = lax.broadcasted_iota(jnp.int32, (rows, rows), 0)
    ci = lax.broadcasted_iota(jnp.int32, (rows, rows), 1)
    flip[...] = jnp.where(ri + ci == rows - 1, 1.0, 0.0).astype(bf16)
    if ring_on:
        spread_1.finish()
        spread_2.begin()

    def rel_step(i, carry):
        at = pl.ds(pl.multiple_of(i * 256, 256), 256)
        got = mm(table[at, :], w1g[:, :, 512:768].reshape(width, 256), NN)
        rel[0, at, :] = low_half(swap(got[:, :128])).astype(bf16)
        rel[1, at, :] = low_half(got[:, 128:]).astype(bf16)
        rel[2, at, :] = low_half(swap(got[:, 128:])).astype(bf16)
        return carry

    lax.fori_loop(0, 2 * seq // 256, rel_step, 0)

    def project(o):
        at = pl.ds(pl.multiple_of(o * rows, rows), rows)
        got = mm(xs[o], w1g[:, :, :640].reshape(width, 640), NN)
        lane = lane_of(rows)
        qmeta = qmeta_ref[at, :].astype(f32)
        kmeta = kmeta_ref[at, :].astype(f32)
        typed = qmeta[:, 64:65]
        for h in range(heads):
            kv = got[:, 128 * h : 128 * h + 128]
            ka[h, at, :] = jnp.where(lane < 64, kv, kmeta).astype(bf16)
            vrow = swap(kv) + small_ref[8 * h + 5 : 8 * h + 6, :]
            va[h, at, :] = jnp.where(lane < 64, vrow, jnp.where(lane < 66, 1.0, 0.0)).astype(bf16)
            q = got[:, 384:512] if h < 2 else got[:, 512:640]
            if h == 1:
                q = swap(q)
            q = low_half(q)
            q32[h, at, :] = q
            qt = q + small_ref[8 * h + 2 : 8 * h + 3, :]
            ct0 = jnp.sum(qt * small_ref[8 * h + 3 : 8 * h + 4, :], axis=1, keepdims=True)
            ct1 = jnp.sum(qt * small_ref[8 * h + 4 : 8 * h + 5, :], axis=1, keepdims=True)
            diff = (ct1 - ct0) * scale
            base = ct0 * scale + diff * (1.0 - typed)
            tilt = diff * (2.0 * typed - 1.0)
            base_hi = base.astype(bf16).astype(f32)
            tilt_hi = tilt.astype(bf16).astype(f32)
            extra = jnp.where(
                lane == 64,
                base_hi,
                jnp.where(
                    lane == 65,
                    base - base_hi,
                    jnp.where(lane == 66, tilt_hi, jnp.where(lane == 67, tilt - tilt_hi, qmeta)),
                ),
            )
            qc = (q + small_ref[8 * h : 8 * h + 1, :]) * scale
            qa[h, at, :] = jnp.where(lane < 64, qc, extra).astype(bf16)
            qr[h, at, :] = low_half((q + small_ref[8 * h + 1 : 8 * h + 2, :]) * scale).astype(bf16)

    def poll(*steppers):
        for stepper in steppers:
            stepper.step()

    project(me)
    x_b.wait_recv()
    if ring_on:
        poll(spread_2)
    project(mate)
    if ring_on:
        poll(spread_2)
    project(across)
    x_f.wait_recv()
    if ring_on:
        poll(spread_2)
    project(diag)
    if ring_on:
        spread_2.finish()
        spread_3.begin()

    wide = seq + rows

    def attend(o):
        at = pl.ds(pl.multiple_of(o * rows, rows), rows)
        window = pl.ds(pl.multiple_of((members - 1 - o) * rows, rows), wide)

        def one_head(h, carry):
            s = mm(qa[h, at, :], ka[h], NT)
            g = mm(qr[h, at, :], rel[h, window, :], NT)
            g = pltpu.roll(g, wide + 1 - rows, 1, stride=1, stride_axis=0)
            s = s + g[:, :seq]
            top = jnp.max(s, axis=1, keepdims=True)
            e = jnp.exp(s - top).astype(bf16)
            es[h, at, :] = e
            o_full = mm(e, va[h], NN)
            inv = 1.0 / o_full[:, 64:65]
            a32[h, at, :] = jnp.where(lane_of(rows) < 64, o_full * inv, inv)
            return carry

        lax.fori_loop(0, heads, one_head, 0)
        first = low_half(a32[0, at, :]) + swap(low_half(a32[1, at, :]))
        attnp[at, :128] = first.astype(bf16)
        attnp[at, 128:] = low_half(a32[2, at, :]).astype(bf16)
        return mm(attnp[at, :], whole(wog), NT)

    class Scatter:
        def __init__(self, part, r1, r2, sx):
            self.part, self.r1, self.r2, self.sx = part, r1, r2, sx

        def give(self, kind, value):
            if kind == "diag":
                self.part[diag] = value.astype(bf16)
                self.c_far = links.start(self.part.at[diag], self.r1.at[1 - side], to_mate)
            elif kind == "mate":
                self.part[mate] = value.astype(bf16)
                self.c_near = links.start(self.part.at[mate], self.r1.at[side], to_mate)
            elif kind == "across":
                self.part[across] = value.astype(bf16)
            else:
                own_f[...] = value

        def pass_on(self):
            self.c_far.wait_recv()
            self.sx[...] = (self.part[across].astype(f32) + self.r1[1 - side].astype(f32)).astype(bf16)
            self.c_over = links.start(self.sx, self.r2, to_across)

        def release(self):
            links.drain([self.c_far, self.c_near, self.c_over])

        def take(self):
            self.c_near.wait_recv()
            near = own_f[...] + self.r1[side].astype(f32)
            self.c_over.wait_recv()
            return near + self.r2[...].astype(f32)

    first_red = red = Scatter(part_a, r1a, r2a, sxa)
    red.give("diag", attend(diag))
    if ring_on:
        poll(spread_3)
    red.give("across", attend(across))
    red.pass_on()
    if ring_on:
        poll(spread_3)
    red.give("mate", attend(mate))
    if ring_on:
        poll(spread_3)
    red.give("own", attend(me))
    if ring_on:
        spread_3.finish()
    summed = x_ref[...].astype(f32) + red.take() + ln_ref[0:1, :]
    normed, inv_std = norm_stats(summed)
    n1[...] = normed
    inv1[...] = jnp.broadcast_to(inv_std, inv1.shape)
    h1[...] = normed * ln_ref[1:2, :] + ln_ref[2:3, :]
    hb[me] = h1[...].astype(bf16)
    g_a, g_b = gather_start(hb)

    def ffn(o):
        inner = mm(hb[o], whole(wig), NN) + ibs[0:1, :]
        square = inner * inner
        t = jnp.tanh(0.7978845608028654 * (inner + 0.044715 * square * inner))
        act[o] = (0.5 * inner * (1.0 + t)).astype(bf16)
        slope[o] = (
            0.5 * (1.0 + t)
            + 0.5 * inner * (1.0 - t * t) * 0.7978845608028654 * (1.0 + 3.0 * 0.044715 * square)
        ).astype(bf16)
        return mm(act[o], whole(wug), NT)

    def gathered(buf, first, second, block, reducer):
        reducer.give("own", block(me))
        second.wait_recv()
        reducer.give("mate", block(mate))
        forward = gather_forward(buf, first)
        reducer.give("across", block(across))
        forward.wait_recv()
        reducer.give("diag", block(diag))
        reducer.pass_on()

    second_red = red = Scatter(part_b, r1b, r2b, sxb)
    gathered(hb, g_a, g_b, ffn, red)
    summed = h1[...] + red.take() + ln_ref[3:4, :]
    normed, inv_std = norm_stats(summed)
    out_ref[...] = (normed * ln_ref[4:5, :] + ln_ref[5:6, :]).astype(bf16)
    grad = og_ref[...].astype(f32)
    vec_ref[4:5, :] = col_sum(grad * normed)
    vec_ref[5:6, :] = col_sum(grad)
    e2[...] = norm_back(grad, normed, inv_std, ln_ref[4:5, :])
    vec_ref[1:2, :] = col_sum(e2[...])
    eb2[me] = e2[...].astype(bf16)
    g_a, g_b = gather_start(eb2)

    vec_ref[6:8, :] = jnp.zeros((2, width), f32)
    hs_ref[...] = jnp.zeros(hs_ref.shape, f32)

    def ffn_back(o):
        grad_inner = (mm(eb2[o], whole(wug), NN) * slope[o].astype(f32)).astype(bf16)
        igr[o] = grad_inner
        vec_ref[6:7, :hidden] += col_sum(grad_inner.astype(f32))
        return mm(grad_inner, whole(wig), NT)

    first_red.release()
    red = Scatter(part_a, r1a, r2a, sxa)
    gathered(eb2, g_a, g_b, ffn_back, red)
    flat = lambda ref: ref[...].reshape(seq, ref.shape[2])

    def put(ref, value):
        ref[...] = value.astype(bf16).reshape(ref.shape)

    put(dwu, mm(flat(eb2), flat(act), TN))
    put(dwi, mm(flat(hb), flat(igr), TN))
    if ring_on:
        collect_1 = Collect(links, ring, [dwu, dwi], [r["gwu"], r["gwi"]])
        collect_1.begin()

    grad = e2[...] + red.take()
    vec_ref[2:3, :] = col_sum(grad * n1[...])
    vec_ref[3:4, :] = col_sum(grad)
    e1[...] = norm_back(grad, n1[...], inv1[:, :1], ln_ref[1:2, :])
    vec_ref[0:1, :] = col_sum(e1[...])
    eb1[me] = e1[...].astype(bf16)
    g_a, g_b = gather_start(eb1)
    if ring_on:
        vec_all, vec_mp = r["vec_all"], r["vec_mp"]
        vec_all[mine] = vec_ref[...]
        spread_4 = Spread(links, ring, [vec_all])
        spread_4.begin()

    dkv[...] = jnp.zeros(dkv.shape, f32)
    drt[...] = jnp.zeros(drt.shape, f32)

    def attend_back(o):
        at = pl.ds(pl.multiple_of(o * rows, rows), rows)
        lo = pl.multiple_of((members - 1 - o) * rows, rows)
        window = pl.ds(lo, wide)
        d_all = mm(eb1[o], whole(wog), NN).astype(bf16).astype(f32)
        lane = lane_of(rows)
        typed = qmeta_ref[at, :].astype(f32)[:, 64:65]
        packed = []
        for h in range(heads):
            d_out = d_all[:, :128] if h < 2 else d_all[:, 128:]
            if h == 1:
                d_out = swap(d_out)
            kept = a32[h, at, :]
            d_out = low_half(d_out * kept[:, 64:65]).astype(bf16).astype(f32)
            d_row = -jnp.sum(d_out * kept, axis=1, keepdims=True)
            d_hi = d_row.astype(bf16).astype(f32)
            d_aug = jnp.where(lane == 64, d_hi, jnp.where(lane == 65, d_row - d_hi, d_out)).astype(bf16)
            e = es[h, at, :]
            ds = (e.astype(f32) * mm(d_aug, va[h], NT)).astype(bf16)
            dkv[h, 64:128, :] += mm(d_aug, e, TN)[:64]
            dkv[h, 0:64, :] += mm(qa[h, at, :], ds, TN)[:64]
            dq = mm(ds, ka[h], NN) * scale
            turned = mm(flip[...], ds, NN)
            turned = jnp.concatenate([turned, jnp.zeros((rows, rows), f32)], axis=1)
            dg = pltpu.roll(turned, 0, 1, stride=1, stride_axis=0).astype(bf16)
            dqr = mm(dg, rel[h, window, :], NN) * scale
            qr_turned = mm(flip[...], qr[h, at, :], NN).astype(bf16)
            drt[64 * h + 64 : 64 * h + 128, window] += mm(qr_turned, dg, TN)[:64]
            hs_ref[8 * h + 1 : 8 * h + 2, :] += col_sum(dqr)
            dqr_hi = dqr.astype(bf16)
            dqr_lo = (dqr - dqr_hi.astype(f32)).astype(bf16)
            dqr = mm(flip[...], dqr_hi, NN) + mm(flip[...], dqr_lo, NN)
            total = dq[:, 64:65]
            ones = dq[:, 66:67]
            same = jnp.where(typed > 0.5, ones, total - ones)
            other = total - same
            dqt = other * small_ref[8 * h + 3 : 8 * h + 4, :] + same * small_ref[8 * h + 4 : 8 * h + 5, :]
            qt = q32[h, at, :] + small_ref[8 * h + 2 : 8 * h + 3, :]
            hs_ref[8 * h : 8 * h + 1, :] += col_sum(dq)
            hs_ref[8 * h + 2 : 8 * h + 3, :] += col_sum(dqt)
            hs_ref[8 * h + 3 : 8 * h + 4, :] += col_sum(other * qt)
            hs_ref[8 * h + 4 : 8 * h + 5, :] += col_sum(same * qt)
            packed.append(low_half(dq + dqr + dqt))
        dqkv[at, 384:512] = (packed[0] + swap(packed[1])).astype(bf16)
        dqkv[at, 512:640] = packed[2].astype(bf16)

    attend_back(me)
    g_b.wait_recv()
    if ring_on:
        poll(spread_4, collect_1)
    attend_back(mate)
    g_f = gather_forward(eb1, g_a)
    if ring_on:
        poll(spread_4, collect_1)
    attend_back(across)
    g_f.wait_recv()
    if ring_on:
        spread_4.finish()
        collect_1.step()
        total = vec_all[0]
        for i in range(1, ring.count):
            total = total + vec_all[i]
        vec_mp[me] = total
        v_a, v_b = gather_start(vec_mp)
    attend_back(diag)
    put(dwo, mm(flat(eb1), attnp[...], TN))
    if ring_on:
        collect_1.finish()
        v_b.wait_recv()
        v_f = gather_forward(vec_mp, v_a)
        collect_2 = Collect(links, ring, [dwo], [r["gwo"]])
        collect_2.begin()

    for h in range(heads):
        turned = jnp.transpose(dkv[h], (1, 0)).astype(bf16)
        dqkv[:, 128 * h : 128 * h + 128] = turned
        hs_ref[8 * h + 5 : 8 * h + 6, :] = swap(col_sum(turned.astype(f32)))
    put(dwa, mm(flat(xs), dqkv[:, :512], TN))
    if ring_on:
        hs_all = r["hs_all"]
        hs_all[mine] = hs_ref[...]
        spread_5 = Spread(links, ring, [hs_all])
        spread_5.begin()
        collect_3 = Collect(links, ring, [dwa], [r["gwa"]])
        collect_3.begin()

    def input_back(o):
        at = pl.ds(pl.multiple_of(o * rows, rows), rows)
        return mm(dqkv[at, :], w1g[:, :, :640].reshape(width, 640), NT)

    second_red.release()
    red = Scatter(part_b, r1b, r2b, sxb)
    red.give("diag", input_back(diag))
    red.give("across", input_back(across))
    if ring_on:
        poll(collect_2, spread_5)
    tail = mm(flat(xs), dqkv[:, 512:640], TN)
    d_rel = jnp.transpose(drt[...], (1, 0)).astype(bf16)
    d_pos = mm(table[...], d_rel, TN)
    put(dwb, jnp.concatenate([tail + d_pos[:, :128], d_pos[:, 128:]], axis=1))
    if ring_on:
        collect_4 = Collect(links, ring, [dwb], [r["gwb"]])
        collect_4.begin()
    red.pass_on()
    if ring_on:
        poll(collect_3, collect_2)
    red.give("mate", input_back(mate))
    red.give("own", input_back(me))
    if ring_on:
        poll(spread_5, collect_3, collect_4, collect_2)
    ig_ref[...] = (e1[...] + red.take()).astype(bf16)
    if ring_on:
        grad_ref = r["grad_ref"]
        poll(spread_5, collect_3, collect_4, collect_2)
        v_f.wait_recv()
        r["vec_ref"][...] = vec_mp[0] + vec_mp[1] + vec_mp[2] + vec_mp[3]
        r["vec_ref"][6:7, :] = vec_mp[me][6:7, :]
        collect_1.take(0, grad_ref, pl.ds(1024 + hidden, hidden))
        collect_1.take(1, grad_ref, pl.ds(1024, hidden))
        poll(spread_5, collect_3, collect_4)
        collect_2.finish()
        collect_2.take(0, grad_ref, pl.ds(768, 256))
        spread_5.finish()
        total = hs_all[0]
        for i in range(1, ring.count):
            total = total + hs_all[i]
        r["hs_ref"][...] = total
        collect_3.finish()
        collect_3.take(0, grad_ref, pl.ds(0, 512))
        collect_4.finish()
        collect_4.take(0, grad_ref, pl.ds(512, 256))
    else:
        r["vec_ref"][...] = vec_ref[...]
        r["hs_ref"][...] = hs_ref[...]
    links.drain()


SCRATCH = (
    "xs", "hb", "eb2", "eb1", "part_a", "part_b", "r1a", "r1b", "r2a", "r2b", "sxa", "sxb", "own_f", "table", "rel",
    "qa", "qr", "ka", "va", "q32", "es", "a32", "attnp", "act", "slope", "igr", "h1", "n1", "e2", "inv1", "e1", "dkv",
    "drt", "dqkv", "flip", "qmeta", "kmeta", "small", "ln", "ibs", "send_sems", "recv_sems",
)


def finish_kernel(
    out_ref, ig_ref, grad_ref, vec_ref, hs_ref,
    out, in_grad, wq, wk, wv, wp, wo, wi, wu, cb, pb, tbias, vb, te, ib, ab, fb, ag, ash, fg, fs, turn,
):
    out[...] = out_ref[...]
    in_grad[...] = ig_ref[...]
    shard, hidden = wi.shape
    t = [grad_ref[:, 128 * i : 128 * i + 128].astype(f32) for i in range(6)]
    low = lane_of(shard) < 64
    wk[:, :128] = jnp.where(low, t[0], swap(t[1]))
    wk[:, 128:] = t[2][:, :64]
    wv[:, :128] = jnp.where(low, swap(t[0]), t[1])
    wv[:, 128:] = swap(t[2])[:, :64]
    wq[:, :128] = t[3]
    wq[:, 128:] = t[4][:, :64]
    wp[:, :128] = jnp.where(low, swap(t[4]), swap(t[5]))
    wp[:, 128:] = swap(t[5])[:, :64]
    turn[...] = jnp.zeros(turn.shape, f32)
    turn[:shard, :] = grad_ref[:, 768:1024].astype(f32)
    wo[...] = jnp.transpose(turn[...], (1, 0))[: wo.shape[0], :shard]
    wi[...] = grad_ref[:, 1024 : 1024 + hidden].astype(f32)
    wu[...] = grad_ref[:, 1024 + hidden :].astype(f32)
    for h in range(cb.shape[0]):
        for i, ref in ((0, cb), (1, pb), (2, tbias), (5, vb)):
            ref[h : h + 1, :] = hs_ref[8 * h + i : 8 * h + i + 1, :64]
        te[h] = hs_ref[8 * h + 3 : 8 * h + 5, :64]
    ib[...] = vec_ref[6:7, :hidden].reshape(hidden)
    for i, ref in enumerate((ab, fb, ag, ash, fg, fs)):
        ref[...] = vec_ref[i : i + 1, :].reshape(ref.shape[0])


def angle_tables(seq, width):
    half = width // 2
    freq = 1.0 / 10000.0 ** (np.arange(half, dtype=np.float64) * (2.0 / width))
    steps = 32
    coarse = (seq - 1 - steps * np.arange(2 * seq // steps, dtype=np.float64))[:, None] * freq[None, :]
    fine = np.arange(steps, dtype=np.float64)[:, None] * freq[None, :]
    return (
        np.stack([np.sin(coarse), np.cos(coarse)]).astype(np.float32),
        np.stack([np.sin(fine), np.cos(fine)]).astype(np.float32),
    )


def per_device(
    layer_input, doc_ids, type_ids, positions, query_weight, key_weight, value_weight, pos_kernel,
    out_weight, inner_weight, outer_weight, content_bias, pos_bias, type_bias, value_bias, type_embed,
    inner_bias, attn_bias, ffn_bias, attn_gain, attn_shift, ffn_gain, ffn_shift, out_grad,
):
    rows, width = layer_input.shape
    seq = doc_ids.shape[0]
    heads, depth = content_bias.shape
    hidden = inner_weight.shape[1]
    shard = query_weight.shape[0]
    members = seq // rows
    count = width // shard
    cols = heads * depth
    ring_on = shard % 16 == 0 and count % 2 == 0 and count > 2

    type_rows = jnp.transpose(type_embed, (1, 0, 2))
    ta, tb = angle_tables(seq, width)
    given = [
        layer_input, out_grad, doc_ids, type_ids, content_bias, pos_bias, type_bias, value_bias, type_rows, inner_bias,
        attn_bias, ffn_bias, attn_gain, attn_shift, ffn_gain, ffn_shift, ta, tb,
    ]
    sds = jax.ShapeDtypeStruct
    vm = pltpu.VMEM
    blocks = count if ring_on else 1
    deep = width // blocks
    full = {
        "w1g": 768, "wog": 256, "wig": hidden, "wug": hidden,
        "dwa": 512, "dwb": 256, "dwo": 256, "dwi": hidden, "dwu": hidden,
    }
    outs = {
        "out_ref": sds((rows, width), bf16), "ig_ref": sds((rows, width), bf16),
        "vec_ref": sds((8, width), f32), "hs_ref": sds((8 * heads, 128), f32),
    }
    extra = {"vec": vm((8, width), f32), "hs": vm((8 * heads, 128), f32)}
    if ring_on:
        given += [query_weight, key_weight, value_weight, pos_kernel, out_weight, inner_weight, outer_weight.T]
        names = IN_BOTH + IN_RING
        outs["grad_ref"] = sds((shard, 1024 + 2 * hidden), f32)
        extra |= {name: vm((blocks, deep, wide), bf16) for name, wide in full.items()}
        for name in OUT_WHOLE:
            extra["g" + name[1:]] = vm((blocks - 1, deep, full[name]), bf16)
        extra["vec_all"] = vm((blocks, 8, width), f32)
        extra["vec_mp"] = vm((members, 8, width), f32)
        extra["hs_all"] = vm((blocks, 8 * heads, 128), f32)
    else:
        q3, k3, v3 = (w.reshape(shard, heads, depth) for w in (query_weight, key_weight, value_weight))
        kv = jnp.stack([k3, v3], axis=2).reshape(shard, 2 * cols)
        out_t = jnp.pad(out_weight.T, ((0, 0), (0, 256 - cols)))
        mine = jnp.concatenate([kv, query_weight, pos_kernel, out_t, inner_weight, outer_weight.T], axis=1)
        gathered = lax.all_gather(mine, "dp", axis=0, tiled=True)[None]
        bounds = np.cumsum([0] + [full[name] for name in IN_WHOLE])
        given += [gathered[:, :, lo:hi] for lo, hi in zip(bounds[:-1], bounds[1:])]
        names = IN_BOTH + IN_WHOLE
        outs |= {name: sds((1, width, full[name]), bf16) for name in OUT_WHOLE}

    block = (members, rows, width)
    per_head = (heads, seq, 128)
    scratch = {
        "xs": vm(block, bf16), "hb": vm(block, bf16), "eb2": vm(block, bf16), "eb1": vm(block, bf16),
        "part_a": vm(block, bf16), "part_b": vm(block, bf16),
        "r1a": vm((2, rows, width), bf16), "r1b": vm((2, rows, width), bf16),
        "r2a": vm((rows, width), bf16), "r2b": vm((rows, width), bf16),
        "sxa": vm((rows, width), bf16), "sxb": vm((rows, width), bf16),
        "own_f": vm((rows, width), f32), "table": vm((2 * seq, width), bf16), "rel": vm((heads, 2 * seq, 128), bf16),
        "qa": vm(per_head, bf16), "qr": vm(per_head, bf16), "ka": vm(per_head, bf16), "va": vm(per_head, bf16),
        "q32": vm(per_head, f32), "es": vm((heads, seq, seq), bf16), "a32": vm(per_head, f32),
        "attnp": vm((seq, 256), bf16), "act": vm((members, rows, hidden), bf16),
        "slope": vm((members, rows, hidden), bf16), "igr": vm((members, rows, hidden), bf16),
        "h1": vm((rows, width), f32), "n1": vm((rows, width), f32), "e2": vm((rows, width), f32),
        "inv1": vm((rows, 128), f32), "e1": vm((rows, width), f32), "dkv": vm((heads, 128, seq), f32),
        "drt": vm((256, 2 * seq), f32), "dqkv": vm((seq, 640), bf16), "flip": vm((rows, rows), bf16),
        "qmeta": vm((seq, 128), bf16), "kmeta": vm((seq, 128), bf16), "small": vm((8 * heads, 128), f32),
        "ln": vm((8, width), f32), "ibs": vm((8, hidden), f32),
        "send_sems": pltpu.SemaphoreType.DMA((192,)), "recv_sems": pltpu.SemaphoreType.DMA((192,)),
    }
    scratch |= extra
    inside = pl.BlockSpec(memory_space=pltpu.VMEM)
    made = pl.pallas_call(
        functools.partial(layer_kernel, ring_on, [*names, *outs, *scratch]),
        out_shape=list(outs.values()),
        in_specs=[inside] * len(given),
        out_specs=[inside] * len(outs),
        scratch_shapes=list(scratch.values()),
        compiler_params=pltpu.CompilerParams(collective_id=0, has_side_effects=True, vmem_limit_bytes=67043328),
        name="layer",
    )(*given)
    made = dict(zip(outs, made))

    if ring_on:
        grads, vec, hs = made["grad_ref"], made["vec_ref"], made["hs_ref"]
    else:
        grads = jnp.concatenate([made[name][0] for name in ("dwa", "dwb", "dwo", "dwi", "dwu")], axis=1)
        grads = lax.psum_scatter(grads, "dp", scatter_dimension=0, tiled=True).astype(f32)
        vec, hs = lax.psum((made["vec_ref"], made["hs_ref"]), "dp")
        vec = jnp.concatenate([lax.psum(vec[:6], "mp"), vec[6:]], axis=0)
    small = sds((heads, depth), f32)
    line = sds((width,), f32)
    results = pl.pallas_call(
        finish_kernel,
        out_shape=[
            made["out_ref"], made["ig_ref"], *[sds((shard, cols), f32)] * 4, sds((cols, shard), f32),
            sds((shard, hidden), f32), sds((shard, hidden), f32), *[small] * 4, sds((heads, 2, depth), f32),
            sds((hidden,), f32), *[line] * 6,
        ],
        in_specs=[inside] * 5,
        out_specs=[inside] * 21,
        scratch_shapes=[vm((128, 256), f32)],
        name="finish",
    )(made["out_ref"], made["ig_ref"], grads, vec, hs)
    results = list(results)
    results[8] = results[8].T
    results[13] = jnp.transpose(results[13], (1, 0, 2))
    return tuple(results)


def solution(mesh):
    rows = P(("dp", "mp"), None)
    token = P("dp")
    placed = (
        (rows, token, token, token)
        + (P("dp", "mp"),) * 4
        + (P("mp", "dp"), P("dp", "mp"), P("mp", "dp"))
        + (P("mp", None),) * 4
        + (P(None, "mp", None), P("mp"))
        + (P(),) * 6
        + (rows,)
    )
    given = (
        (rows, rows)
        + (P("dp", "mp"),) * 4
        + (P("mp", "dp"), P("dp", "mp"), P("mp", "dp"))
        + (P("mp", None),) * 4
        + (P(None, "mp", None), P("mp"))
        + (P(),) * 6
    )
    return jax.shard_map(per_device, mesh=mesh, in_specs=placed, out_specs=given, check_vma=False)
```

```python
import functools
import math

import jax
import jax.numpy as jnp
import numpy as np
from jax import lax
from jax.experimental import pallas as pl
from jax.experimental.pallas import tpu as pltpu
from jax.sharding import PartitionSpec as P

f32 = jnp.float32
bf16 = jnp.bfloat16
MESH = pl.DeviceIdType.MESH
MASK = -1e30
DOC_LEAST = 60
NN = (((1,), (0,)), ((), ()))
NT = (((1,), (1,)), ((), ()))
TN = (((0,), (0,)), ((), ()))


def mm(a, b, dims):
    return lax.dot_general(a, b, dims, preferred_element_type=f32)


def lane_of(rows):
    return lax.broadcasted_iota(jnp.int32, (rows, 128), 1)


def low_half(value):
    return jnp.where(lane_of(value.shape[0]) < 64, value, 0.0)


def swap(value):
    return pltpu.roll(value, 64, 1)


class Links:
    def __init__(self, send_sems, recv_sems):
        self.send_sems = send_sems
        self.recv_sems = recv_sems
        self.used = 0
        self.sent = []

    def start(self, src, dst, where):
        copy = pltpu.make_async_remote_copy(
            src_ref=src,
            dst_ref=dst,
            send_sem=self.send_sems.at[self.used],
            recv_sem=self.recv_sems.at[self.used],
            device_id=where,
            device_id_type=MESH,
        )
        self.used += 1
        self.sent.append(copy)
        copy.start()
        return copy

    def drain(self, some=None):
        for copy in some or self.sent:
            copy.wait_send()
            self.sent = [other for other in self.sent if other is not copy]


def norm_stats(summed):
    center = summed - jnp.mean(summed, axis=-1, keepdims=True)
    spread = jnp.mean(center * center, axis=-1, keepdims=True)
    inv_std = lax.rsqrt(spread + 1e-06)
    return center * inv_std, inv_std


def norm_back(grad, normed, inv_std, gain):
    scaled = grad * gain
    return inv_std * (
        scaled
        - jnp.mean(scaled, axis=-1, keepdims=True)
        - normed * jnp.mean(scaled * normed, axis=-1, keepdims=True)
    )


def col_sum(value):
    return jnp.sum(value, axis=0, keepdims=True)


class Ring:
    def __init__(self, count):
        mine = lax.axis_index("dp")
        row = lax.rem(mine, 2)
        along = lax.div(mine, 2)
        self.count = count
        self.place = (1 - row) * along + row * (count - 1 - along)

    def at(self, offset):
        place = lax.rem(self.place + (offset + self.count), self.count)
        back = lax.div(place, self.count // 2)
        return (1 - back) * 2 * place + back * (2 * (self.count - 1 - place) + 1)


class Flow:
    def __init__(self, sign, hops, rows, slot):
        self.sign, self.hops, self.rows, self.slot = sign, hops, rows, slot


def flows_of(count, rows):
    near = count // 2 - 1
    if rows % 32:
        return [Flow(1, near + 1, pl.ds(0, rows), 0), Flow(-1, near, pl.ds(0, rows), near + 1)]
    first, second = pl.ds(0, rows // 2), pl.ds(rows // 2, rows // 2)
    return [
        Flow(1, near + 1, first, 0),
        Flow(-1, near + 1, second, near),
        Flow(-1, near, first, near + 1),
        Flow(1, near, second, 0),
    ]


class Spread:
    def __init__(self, links, ring, bufs):
        self.links, self.ring, self.bufs = links, ring, bufs
        self.done = 0
        self.last = max(f.hops for f in flows_of(ring.count, bufs[0].shape[1]))
        self.moves = {}

    def begin(self):
        self.send(0)

    def send(self, s):
        for b, buf in enumerate(self.bufs):
            for f, flow in enumerate(flows_of(self.ring.count, buf.shape[1])):
                if s > 0 and s <= flow.hops:
                    self.moves[b, f].wait_recv()
                if s < flow.hops:
                    ref = buf.at[self.ring.at(-flow.sign * s), flow.rows]
                    self.moves[b, f] = self.links.start(ref, ref, {"dp": self.ring.at(flow.sign)})

    def step(self):
        if self.done < self.last:
            self.done += 1
            self.send(self.done)

    def finish(self):
        while self.done < self.last:
            self.step()


class Collect:
    def __init__(self, links, ring, bufs, gots):
        self.links, self.ring = links, ring
        self.bufs, self.gots = bufs, gots
        self.done = 0
        self.last = max(f.hops for f in flows_of(ring.count, bufs[0].shape[1]))
        self.moves = {}

    def begin(self):
        self.send(0)

    def send(self, s):
        for b, (buf, got) in enumerate(zip(self.bufs, self.gots)):
            for f, flow in enumerate(flows_of(self.ring.count, buf.shape[1])):
                if s > 0 and s <= flow.hops:
                    self.moves[b, f].wait_recv()
                if s < flow.hops:
                    owner = self.ring.at(flow.sign * (flow.hops - s))
                    if s > 0:
                        both = buf[owner, flow.rows].astype(f32) + got[flow.slot + s - 1, flow.rows].astype(f32)
                        buf[owner, flow.rows] = both.astype(bf16)
                    self.moves[b, f] = self.links.start(
                        buf.at[owner, flow.rows], got.at[flow.slot + s, flow.rows], {"dp": self.ring.at(flow.sign)}
                    )

    def step(self):
        if self.done < self.last:
            self.done += 1
            self.send(self.done)

    def finish(self):
        while self.done < self.last:
            self.step()

    def take(self, b, out_ref, columns):
        buf, got = self.bufs[b], self.gots[b]
        mine = self.ring.at(0)
        flows = flows_of(self.ring.count, buf.shape[1])
        for start in sorted({flow.rows.start for flow in flows}):
            total = None
            for flow in flows:
                if flow.rows.start == start:
                    part = got[flow.slot + flow.hops - 1, flow.rows].astype(f32)
                    total = buf[mine, flow.rows].astype(f32) + part if total is None else total + part
                    rows = flow.rows
            out_ref[rows, columns] = total


IN_BOTH = (
    "x_ref", "og_ref", "doc_ref", "kind_ref", "cb_ref", "pb_ref", "tbias_ref", "vb_ref", "te_ref", "ib_ref", "ab_ref",
    "fb_ref", "ag_ref", "as_ref", "fg_ref", "fs_ref", "ta_ref", "tb_ref",
)
IN_RING = (
    "wq_ref", "wk_ref", "wv_ref", "wp_ref", "wo_ref", "wi_ref", "wu_ref",
)
IN_WHOLE = (
    "w1g", "wog", "wig", "wug",
)
OUT_WHOLE = (
    "dwa", "dwb", "dwo", "dwi", "dwu",
)


def layer_kernel(ring_on, names, *refs):
    r = dict(zip(names, refs, strict=True))
    (x_ref, og_ref, doc_ref, kind_ref, cb_ref, pb_ref, tbias_ref, vb_ref, te_ref, ib_ref,
     ab_ref, fb_ref, ag_ref, as_ref, fg_ref, fs_ref, ta_ref, tb_ref) = (r[n] for n in IN_BOTH)
    w1g, wog, wig, wug = (r[n] for n in IN_WHOLE)
    dwa, dwb, dwo, dwi, dwu = (r[n] for n in OUT_WHOLE)
    out_ref, ig_ref = r["out_ref"], r["ig_ref"]
    vec_ref, hs_ref = r["vec"], r["hs"]
    (xs, hb, eb2, eb1, part_a, part_b, r1a, r1b, r2a, r2b, sxa, sxb, own_f,
     table, rel, qa, qr, ka, va, q32, es, a32, attnp, act, slope, igr,
     h1, n1, e2, inv1, e1, dkv, drt, dqkv, flip, qmeta_ref, kmeta_ref, small_ref, ln_ref, ibs,
     send_sems, recv_sems) = (r[n] for n in SCRATCH)
    rows = x_ref.shape[0]
    width = x_ref.shape[1]
    hidden = wig.shape[2]
    members = xs.shape[0]
    seq = members * rows
    heads = es.shape[0]
    half = width // 2
    scale = 0.125
    me = lax.axis_index("mp")
    core = lax.rem(me, 2)
    side = lax.div(me, 2)
    mate = me + 1 - 2 * core
    across = lax.rem(me + 2, 4)
    diag = lax.rem(mate + 2, 4)
    links = Links(send_sems, recv_sems)
    to_mate = {"mp": mate}
    to_across = {"mp": across}

    barrier = pltpu.get_barrier_semaphore()
    peers = [to_mate, to_across]
    if ring_on:
        ring = Ring(w1g.shape[0])
        peers += [{"dp": ring.at(1)}, {"dp": ring.at(-1)}]
    for where in peers:
        pl.semaphore_signal(barrier, inc=1, device_id=where, device_id_type=MESH)
    pl.semaphore_wait(barrier, len(peers))

    def whole(ref):
        return ref[...].reshape(width, ref.shape[2])

    def gather_start(buf):
        a = links.start(buf.at[me], buf.at[me], to_across)
        b = links.start(buf.at[me], buf.at[me], to_mate)
        return a, b

    def gather_forward(buf, first):
        first.wait_recv()
        return links.start(buf.at[across], buf.at[across], to_mate)

    part_rows = rows // 2
    halves = [pl.ds(0, part_rows), pl.ds(part_rows, part_rows)]
    near_pair, far_pair = pl.ds(2 * side, 2), pl.ds(2 * (1 - side), 2)

    class Gather:
        def __init__(self, buf, x):
            self.buf, self.x = buf, x
            mine_x = buf.at[me, halves[x]]
            self.over = links.start(mine_x, mine_x, to_across)
            self.beside = links.start(mine_x, mine_x, to_mate)

        def forward(self):
            self.over.wait_recv()
            theirs = self.buf.at[across, halves[self.x]]
            self.last = links.start(theirs, theirs, to_mate)

    xs[me] = x_ref[...]
    x_a, x_b = gather_start(xs)

    if ring_on:
        shard = w1g.shape[1]
        mine = ring.at(0)
        own_f[...] = jnp.zeros(own_f.shape, f32)
        tiles = []
        for i, name in enumerate(IN_RING[:4]):
            r0, c0 = 128 * (i // 2), 256 * (i % 2)
            own_f[r0 : r0 + shard, c0 : c0 + r[name].shape[1]] = r[name][...].astype(f32)
            tiles.append((own_f[r0 : r0 + shard, c0 : c0 + 128], own_f[r0 : r0 + shard, c0 + 128 : c0 + 256]))
        (qx, qy), (kx, ky), (vx, vy), (px, py) = tiles
        low = lane_of(shard) < 64
        joined = [
            jnp.where(low, kx, swap(vx)),
            jnp.where(low, swap(kx), vx),
            jnp.where(low, ky, swap(vy)),
            qx,
            jnp.where(low, qy, swap(px)),
            jnp.where(low, swap(px), swap(py)),
        ]
        for i, tile in enumerate(joined):
            w1g[mine, :, 128 * i : 128 * i + 128] = tile.astype(bf16)
        spread_1 = Spread(links, ring, [w1g])
        spread_1.begin()
        wo_ref = r["wo_ref"]
        own_f[:, :128] = jnp.zeros((256, 128), f32)
        own_f[: wo_ref.shape[0], :shard] = wo_ref[...].astype(f32)
        wog[mine] = jnp.transpose(own_f[:, :128], (1, 0))[:shard].astype(bf16)
        wig[mine] = r["wi_ref"][...]
        wug[mine] = r["wu_ref"][...]
        spread_o, spread_i, spread_u = (Spread(links, ring, [ref]) for ref in (wog, wig, wug))

    small_ref[...] = jnp.zeros(small_ref.shape, f32)
    for h in range(heads):
        for i, ref in enumerate((cb_ref, pb_ref, tbias_ref)):
            small_ref[8 * h + i : 8 * h + i + 1, 0:64] = ref[h : h + 1, :]
        small_ref[8 * h + 3 : 8 * h + 5, 0:64] = te_ref[h]
        small_ref[8 * h + 5 : 8 * h + 6, 0:64] = vb_ref[h : h + 1, :]
    for i, ref in enumerate((ab_ref, ag_ref, as_ref, fb_ref, fg_ref, fs_ref)):
        ln_ref[i : i + 1, :] = ref[...].reshape(1, width)
    ibs[0:1, :] = ib_ref[...].reshape(1, hidden)

    slots = seq // DOC_LEAST + 2
    ends = (doc_ref[...].reshape(1, seq) - lax.axis_index("dp") * seq).astype(f32)
    slot = jnp.where(ends > seq - 1.5, slots - 1.0, jnp.floor((ends + 0.5) * (1.0 / DOC_LEAST)))
    slot = jnp.transpose(jnp.broadcast_to(slot, (128, seq)), (1, 0))
    kind = jnp.transpose(jnp.broadcast_to(kind_ref[...].reshape(1, seq).astype(f32), (128, seq)), (1, 0))
    lane = lane_of(seq)
    hit = jnp.abs(slot + 68.0 - lane.astype(f32)) < 0.5
    qmeta_ref[...] = jnp.where(lane == 64, kind, jnp.where(hit, 1.0, 0.0)).astype(bf16)
    miss = jnp.where(hit, 0.0, MASK)
    kmeta_ref[...] = jnp.where(
        lane < 66, 1.0, jnp.where(lane < 68, kind, jnp.where(lane < 68 + slots, miss, 0.0))
    ).astype(bf16)
    x_f = gather_forward(xs, x_a)
    if ring_on:
        spread_1.step()

    steps = tb_ref.shape[1]

    def table_step(u, carry):
        sa = ta_ref[0, pl.ds(u, 1), :]
        ca = ta_ref[1, pl.ds(u, 1), :]
        at = pl.multiple_of(u * steps, steps)
        table[pl.ds(at, steps), :half] = (sa * tb_ref[1] - ca * tb_ref[0]).astype(bf16)
        table[pl.ds(at, steps), half:] = (ca * tb_ref[1] + sa * tb_ref[0]).astype(bf16)
        return carry

    lax.fori_loop(0, ta_ref.shape[1] // 2, table_step, 0)
    if ring_on:
        spread_1.step()
    lax.fori_loop(ta_ref.shape[1] // 2, ta_ref.shape[1], table_step, 0)

    ri = lax.broadcasted_iota(jnp.int32, (rows, rows), 0)
    ci = lax.broadcasted_iota(jnp.int32, (rows, rows), 1)
    flip[...] = jnp.where(ri + ci == rows - 1, 1.0, 0.0).astype(bf16)
    if ring_on:
        spread_1.step()
        spread_o.begin()
        spread_1.finish()

    def rel_step(i, carry):
        at = pl.ds(pl.multiple_of(i * 256, 256), 256)
        got = mm(table[at, :], w1g[:, :, 512:768].reshape(width, 256), NN)
        rel[0, at, :] = low_half(swap(got[:, :128])).astype(bf16)
        rel[1, at, :] = low_half(got[:, 128:]).astype(bf16)
        rel[2, at, :] = low_half(swap(got[:, 128:])).astype(bf16)
        return carry

    lax.fori_loop(0, 2 * seq // 256, rel_step, 0)

    def project(o):
        at = pl.ds(pl.multiple_of(o * rows, rows), rows)
        got = mm(xs[o], w1g[:, :, :640].reshape(width, 640), NN)
        lane = lane_of(rows)
        qmeta = qmeta_ref[at, :].astype(f32)
        kmeta = kmeta_ref[at, :].astype(f32)
        typed = qmeta[:, 64:65]
        for h in range(heads):
            kv = got[:, 128 * h : 128 * h + 128]
            ka[h, at, :] = jnp.where(lane < 64, kv, kmeta).astype(bf16)
            vrow = swap(kv) + small_ref[8 * h + 5 : 8 * h + 6, :]
            va[h, at, :] = jnp.where(lane < 64, vrow, jnp.where(lane < 66, 1.0, 0.0)).astype(bf16)
            q = got[:, 384:512] if h < 2 else got[:, 512:640]
            if h == 1:
                q = swap(q)
            q = low_half(q)
            q32[h, at, :] = q
            qt = q + small_ref[8 * h + 2 : 8 * h + 3, :]
            ct0 = jnp.sum(qt * small_ref[8 * h + 3 : 8 * h + 4, :], axis=1, keepdims=True)
            ct1 = jnp.sum(qt * small_ref[8 * h + 4 : 8 * h + 5, :], axis=1, keepdims=True)
            diff = (ct1 - ct0) * scale
            base = ct0 * scale + diff * (1.0 - typed)
            tilt = diff * (2.0 * typed - 1.0)
            base_hi = base.astype(bf16).astype(f32)
            tilt_hi = tilt.astype(bf16).astype(f32)
            extra = jnp.where(
                lane == 64,
                base_hi,
                jnp.where(
                    lane == 65,
                    base - base_hi,
                    jnp.where(lane == 66, tilt_hi, jnp.where(lane == 67, tilt - tilt_hi, qmeta)),
                ),
            )
            qc = (q + small_ref[8 * h : 8 * h + 1, :]) * scale
            qa[h, at, :] = jnp.where(lane < 64, qc, extra).astype(bf16)
            qr[h, at, :] = low_half((q + small_ref[8 * h + 1 : 8 * h + 2, :]) * scale).astype(bf16)

    def poll(*steppers):
        for stepper in steppers:
            stepper.step()

    if ring_on:
        spread_o.step()
    project(me)
    x_b.wait_recv()
    project(mate)
    project(across)
    x_f.wait_recv()
    project(diag)
    if ring_on:
        poll(spread_o)
        spread_i.begin()

    wide = seq + rows

    def attend(o, between=None):
        at = pl.ds(pl.multiple_of(o * rows, rows), rows)
        window = pl.ds(pl.multiple_of((members - 1 - o) * rows, rows), wide)

        def one_head(h, carry):
            s = mm(qa[h, at, :], ka[h], NT)
            g = mm(qr[h, at, :], rel[h, window, :], NT)
            g = pltpu.roll(g, wide + 1 - rows, 1, stride=1, stride_axis=0)
            s = s + g[:, :seq]
            top = jnp.max(s, axis=1, keepdims=True)
            e = jnp.exp(s - top).astype(bf16)
            es[h, at, :] = e
            o_full = mm(e, va[h], NN)
            inv = 1.0 / o_full[:, 64:65]
            a32[h, at, :] = jnp.where(lane_of(rows) < 64, o_full * inv, inv)
            return carry

        if between:
            lax.fori_loop(0, 1, one_head, 0)
            between()
        lax.fori_loop(1 if between else 0, heads, one_head, 0)
        first = low_half(a32[0, at, :]) + swap(low_half(a32[1, at, :]))
        attnp[at, :128] = first.astype(bf16)
        attnp[at, 128:] = low_half(a32[2, at, :]).astype(bf16)

    def branch_of(o):
        return mm(attnp[pl.ds(pl.multiple_of(o * rows, rows), rows), :], whole(wog), NT)

    class Scatter:
        def __init__(self, part, r1, r2, sx):
            self.part, self.r1, self.r2, self.sx = part, r1, r2, sx
            self.far, self.near, self.over = [None, None], [None, None], [None, None]

        def give_diag(self, x, value):
            self.part[diag, halves[x]] = value.astype(bf16)
            self.far[x] = links.start(self.part.at[diag, halves[x]], self.r1.at[1 - side, halves[x]], to_mate)

        def give_across(self, x, value):
            self.part[across, halves[x]] = value.astype(bf16)

        def give_mate(self, x, value):
            self.part[mate, halves[x]] = value.astype(bf16)
            self.near[x] = links.start(self.part.at[mate, halves[x]], self.r1.at[side, halves[x]], to_mate)

        def give_own(self, x, value):
            own_f[halves[x]] = value

        def give_near(self, x, pair):
            self.give_mate(x, jnp.where(core == 0, pair[1], pair[0]))
            self.give_own(x, jnp.where(core == 0, pair[0], pair[1]))

        def give_far(self, x, pair):
            self.give_diag(x, jnp.where(core == 0, pair[1], pair[0]))
            self.give_across(x, jnp.where(core == 0, pair[0], pair[1]))

        def pass_on(self, x):
            self.far[x].wait_recv()
            both = self.part[across, halves[x]].astype(f32) + self.r1[1 - side, halves[x]].astype(f32)
            self.sx[halves[x]] = both.astype(bf16)
            self.over[x] = links.start(self.sx.at[halves[x]], self.r2.at[halves[x]], to_across)

        def release(self):
            links.drain(self.far + self.near + self.over)

        def take(self, x):
            self.near[x].wait_recv()
            near = own_f[halves[x]] + self.r1[side, halves[x]].astype(f32)
            self.over[x].wait_recv()
            return near + self.r2[halves[x]].astype(f32)

    def split(value):
        return value[:part_rows], value[part_rows:]

    first_red = red = Scatter(part_a, r1a, r2a, sxa)
    attend(diag)
    if ring_on:
        poll(spread_o, spread_i)
        spread_u.begin()
    attend(across)
    if ring_on:
        spread_o.finish()
    for x, (there, here) in enumerate(zip(split(branch_of(diag)), split(branch_of(across)))):
        red.give_diag(x, there)
        red.give_across(x, here)
    if ring_on:
        poll(spread_i, spread_u)

    def first_pass():
        red.pass_on(0)
        red.pass_on(1)

    attend(mate, first_pass)
    for x, value in enumerate(split(branch_of(mate))):
        red.give_mate(x, value)
    if ring_on:
        poll(spread_i, spread_u)
    attend(me)
    for x, value in enumerate(split(branch_of(me))):
        red.give_own(x, value)
    vec_ref[...] = jnp.zeros((8, width), f32)
    hs_ref[...] = jnp.zeros(hs_ref.shape, f32)

    def first_norm(x):
        at = halves[x]
        summed = x_ref[at, :].astype(f32) + first_red.take(x) + ln_ref[0:1, :]
        normed, inv_std = norm_stats(summed)
        n1[at, :] = normed
        inv1[at, :] = jnp.broadcast_to(inv_std, (part_rows, 128))
        h1[at, :] = normed * ln_ref[1:2, :] + ln_ref[2:3, :]
        hb[me, at] = h1[at, :].astype(bf16)
        return Gather(hb, x)

    def ffn(pair, x):
        inner = mm(hb[pair, halves[x]].reshape(rows, width), whole(wig), NN) + ibs[0:1, :]
        square = inner * inner
        t = jnp.tanh(0.7978845608028654 * (inner + 0.044715 * square * inner))
        made = (0.5 * inner * (1.0 + t)).astype(bf16)
        act[pair, halves[x]] = made.reshape(2, part_rows, hidden)
        steep = (
            0.5 * (1.0 + t)
            + 0.5 * inner * (1.0 - t * t) * 0.7978845608028654 * (1.0 + 3.0 * 0.044715 * square)
        ).astype(bf16)
        slope[pair, halves[x]] = steep.reshape(2, part_rows, hidden)
        return mm(made, whole(wug), NT).reshape(2, part_rows, width)

    def stage(start, block, reducer, ready=None):
        moves = [start(0), start(1)]
        if ready:
            ready()
        for x in (0, 1):
            moves[x].beside.wait_recv()
            reducer.give_near(x, block(near_pair, x))
        moves[0].forward()
        moves[0].last.wait_recv()
        reducer.give_far(0, block(far_pair, 0))
        moves[1].forward()
        reducer.pass_on(0)
        moves[1].last.wait_recv()
        reducer.give_far(1, block(far_pair, 1))
        reducer.pass_on(1)

    def weights_ready():
        spread_i.finish()
        spread_u.finish()

    if ring_on:
        poll(spread_i, spread_u)
    second_red = red = Scatter(part_b, r1b, r2b, sxb)
    stage(first_norm, ffn, second_red, weights_ready if ring_on else None)

    def second_norm(x):
        at = halves[x]
        summed = h1[at, :] + second_red.take(x) + ln_ref[3:4, :]
        normed, inv_std = norm_stats(summed)
        out_ref[at, :] = (normed * ln_ref[4:5, :] + ln_ref[5:6, :]).astype(bf16)
        grad = og_ref[at, :].astype(f32)
        back = norm_back(grad, normed, inv_std, ln_ref[4:5, :])
        e2[at, :] = back
        eb2[me, at] = back.astype(bf16)
        move = Gather(eb2, x)
        vec_ref[4:5, :] += col_sum(grad * normed)
        vec_ref[5:6, :] += col_sum(grad)
        vec_ref[1:2, :] += col_sum(back)
        return move

    def ffn_back(pair, x):
        steep = slope[pair, halves[x]].reshape(rows, hidden).astype(f32)
        grad_inner = (mm(eb2[pair, halves[x]].reshape(rows, width), whole(wug), NN) * steep).astype(bf16)
        igr[pair, halves[x]] = grad_inner.reshape(2, part_rows, hidden)
        vec_ref[6:7, :hidden] += col_sum(grad_inner.astype(f32))
        return mm(grad_inner, whole(wig), NT).reshape(2, part_rows, width)

    third_red = Scatter(part_a, r1a, r2a, sxa)
    stage(second_norm, ffn_back, third_red, first_red.release)
    flat = lambda ref: ref[...].reshape(seq, ref.shape[2])

    def put(ref, value):
        ref[...] = value.astype(bf16).reshape(ref.shape)

    def third_norm(x):
        at = halves[x]
        grad = e2[at, :] + third_red.take(x)
        back = norm_back(grad, n1[at, :], inv1[at, :1], ln_ref[1:2, :])
        e1[at, :] = back
        eb1[me, at] = back.astype(bf16)
        move = Gather(eb1, x)
        vec_ref[2:3, :] += col_sum(grad * n1[at, :])
        vec_ref[3:4, :] += col_sum(grad)
        vec_ref[0:1, :] += col_sum(back)
        return move

    put(dwu, mm(flat(eb2), flat(act), TN))
    if ring_on:
        collect_u = Collect(links, ring, [dwu], [r["gwu"]])
        collect_u.begin()
    g_0 = third_norm(0)
    put(dwi, mm(flat(hb), flat(igr), TN))
    if ring_on:
        collect_i = Collect(links, ring, [dwi], [r["gwi"]])
        collect_i.begin()
    g_1 = third_norm(1)
    if ring_on:
        vec_all, vec_mp = r["vec_all"], r["vec_mp"]
        vec_all[mine] = vec_ref[...]
        spread_4 = Spread(links, ring, [vec_all])
        spread_4.begin()

    dkv[...] = jnp.zeros(dkv.shape, f32)
    drt[...] = jnp.zeros(drt.shape, f32)

    def attend_back(o):
        at = pl.ds(pl.multiple_of(o * rows, rows), rows)
        lo = pl.multiple_of((members - 1 - o) * rows, rows)
        window = pl.ds(lo, wide)
        d_all = mm(eb1[o], whole(wog), NN).astype(bf16).astype(f32)
        lane = lane_of(rows)
        typed = qmeta_ref[at, :].astype(f32)[:, 64:65]
        packed = []
        for h in range(heads):
            d_out = d_all[:, :128] if h < 2 else d_all[:, 128:]
            if h == 1:
                d_out = swap(d_out)
            kept = a32[h, at, :]
            d_out = low_half(d_out * kept[:, 64:65]).astype(bf16).astype(f32)
            d_row = -jnp.sum(d_out * kept, axis=1, keepdims=True)
            d_hi = d_row.astype(bf16).astype(f32)
            d_aug = jnp.where(lane == 64, d_hi, jnp.where(lane == 65, d_row - d_hi, d_out)).astype(bf16)
            e = es[h, at, :]
            ds = (e.astype(f32) * mm(d_aug, va[h], NT)).astype(bf16)
            dkv[h, 64:128, :] += mm(d_aug, e, TN)[:64]
            dkv[h, 0:64, :] += mm(qa[h, at, :], ds, TN)[:64]
            dq = mm(ds, ka[h], NN) * scale
            turned = mm(flip[...], ds, NN)
            turned = jnp.concatenate([turned, jnp.zeros((rows, rows), f32)], axis=1)
            dg = pltpu.roll(turned, 0, 1, stride=1, stride_axis=0).astype(bf16)
            dqr = mm(dg, rel[h, window, :], NN) * scale
            qr_turned = mm(flip[...], qr[h, at, :], NN).astype(bf16)
            drt[64 * h + 64 : 64 * h + 128, window] += mm(qr_turned, dg, TN)[:64]
            hs_ref[8 * h + 1 : 8 * h + 2, :] += col_sum(dqr)
            dqr_hi = dqr.astype(bf16)
            dqr_lo = (dqr - dqr_hi.astype(f32)).astype(bf16)
            dqr = mm(flip[...], dqr_hi, NN) + mm(flip[...], dqr_lo, NN)
            total = dq[:, 64:65]
            ones = dq[:, 66:67]
            same = jnp.where(typed > 0.5, ones, total - ones)
            other = total - same
            dqt = other * small_ref[8 * h + 3 : 8 * h + 4, :] + same * small_ref[8 * h + 4 : 8 * h + 5, :]
            qt = q32[h, at, :] + small_ref[8 * h + 2 : 8 * h + 3, :]
            hs_ref[8 * h : 8 * h + 1, :] += col_sum(dq)
            hs_ref[8 * h + 2 : 8 * h + 3, :] += col_sum(dqt)
            hs_ref[8 * h + 3 : 8 * h + 4, :] += col_sum(other * qt)
            hs_ref[8 * h + 4 : 8 * h + 5, :] += col_sum(same * qt)
            packed.append(low_half(dq + dqr + dqt))
        dqkv[at, 384:512] = (packed[0] + swap(packed[1])).astype(bf16)
        dqkv[at, 512:640] = packed[2].astype(bf16)

    attend_back(me)
    g_0.beside.wait_recv()
    g_1.beside.wait_recv()
    g_0.forward()
    g_1.forward()
    if ring_on:
        poll(spread_4, collect_u, collect_i)
    attend_back(mate)
    if ring_on:
        poll(spread_4, collect_u, collect_i)
    attend_back(across)
    g_0.last.wait_recv()
    g_1.last.wait_recv()
    put(dwo, mm(flat(eb1), attnp[...], TN))
    if ring_on:
        spread_4.finish()
        total = vec_all[0]
        for i in range(1, ring.count):
            total = total + vec_all[i]
        vec_mp[me] = total
        v_a, v_b = gather_start(vec_mp)
        poll(collect_u, collect_i)
        collect_2 = Collect(links, ring, [dwo], [r["gwo"]])
        collect_2.begin()
    attend_back(diag)
    if ring_on:
        poll(collect_u, collect_i, collect_2)
        v_b.wait_recv()
        v_f = gather_forward(vec_mp, v_a)

    for h in range(heads):
        turned = jnp.transpose(dkv[h], (1, 0)).astype(bf16)
        dqkv[:, 128 * h : 128 * h + 128] = turned
        hs_ref[8 * h + 5 : 8 * h + 6, :] = swap(col_sum(turned.astype(f32)))
    put(dwa, mm(flat(xs), dqkv[:, :512], TN))
    if ring_on:
        hs_all = r["hs_all"]
        hs_all[mine] = hs_ref[...]
        spread_5 = Spread(links, ring, [hs_all])
        spread_5.begin()
        collect_3 = Collect(links, ring, [dwa], [r["gwa"]])
        collect_3.begin()

    def input_back(o):
        at = pl.ds(pl.multiple_of(o * rows, rows), rows)
        return mm(dqkv[at, :], w1g[:, :, :640].reshape(width, 640), NT)

    second_red.release()
    red = Scatter(part_b, r1b, r2b, sxb)
    for x, value in enumerate(split(input_back(diag))):
        red.give_diag(x, value)
    for x, value in enumerate(split(input_back(across))):
        red.give_across(x, value)
    if ring_on:
        poll(collect_2)
    red.pass_on(0)
    red.pass_on(1)
    if ring_on:
        poll(collect_3, spread_5)
    tail = mm(flat(xs), dqkv[:, 512:640], TN)
    d_rel = jnp.transpose(drt[...], (1, 0)).astype(bf16)
    d_pos = mm(table[...], d_rel, TN)
    put(dwb, jnp.concatenate([tail + d_pos[:, :128], d_pos[:, 128:]], axis=1))
    if ring_on:
        collect_4 = Collect(links, ring, [dwb], [r["gwb"]])
        collect_4.begin()
        poll(collect_2, collect_3, spread_5)
    for x, value in enumerate(split(input_back(mate))):
        red.give_mate(x, value)
    for x, value in enumerate(split(input_back(me))):
        red.give_own(x, value)
    if ring_on:
        grad_ref = r["grad_ref"]
        poll(collect_3, collect_4, spread_5)
        collect_u.finish()
        collect_i.finish()
        collect_u.take(0, grad_ref, pl.ds(1024 + hidden, hidden))
        collect_i.take(0, grad_ref, pl.ds(1024, hidden))
        poll(collect_4)
    for x in (0, 1):
        ig_ref[halves[x], :] = (e1[halves[x], :] + red.take(x)).astype(bf16)
    if ring_on:
        poll(collect_3, collect_4, spread_5)
        v_f.wait_recv()
        r["vec_ref"][...] = vec_mp[0] + vec_mp[1] + vec_mp[2] + vec_mp[3]
        r["vec_ref"][6:7, :] = vec_mp[me][6:7, :]
        collect_2.finish()
        collect_2.take(0, grad_ref, pl.ds(768, 256))
        spread_5.finish()
        total = hs_all[0]
        for i in range(1, ring.count):
            total = total + hs_all[i]
        r["hs_ref"][...] = total
        collect_3.finish()
        collect_3.take(0, grad_ref, pl.ds(0, 512))
        collect_4.finish()
        collect_4.take(0, grad_ref, pl.ds(512, 256))
    else:
        r["vec_ref"][...] = vec_ref[...]
        r["hs_ref"][...] = hs_ref[...]
    links.drain()


SCRATCH = (
    "xs", "hb", "eb2", "eb1", "part_a", "part_b", "r1a", "r1b", "r2a", "r2b", "sxa", "sxb", "own_f", "table", "rel",
    "qa", "qr", "ka", "va", "q32", "es", "a32", "attnp", "act", "slope", "igr", "h1", "n1", "e2", "inv1", "e1", "dkv",
    "drt", "dqkv", "flip", "qmeta", "kmeta", "small", "ln", "ibs", "send_sems", "recv_sems",
)


def finish_kernel(
    out_ref, ig_ref, grad_ref, vec_ref, hs_ref,
    out, in_grad, wq, wk, wv, wp, wo, wi, wu, cb, pb, tbias, vb, te, ib, ab, fb, ag, ash, fg, fs, turn,
):
    out[...] = out_ref[...]
    in_grad[...] = ig_ref[...]
    shard, hidden = wi.shape
    t = [grad_ref[:, 128 * i : 128 * i + 128].astype(f32) for i in range(6)]
    low = lane_of(shard) < 64
    wk[:, :128] = jnp.where(low, t[0], swap(t[1]))
    wk[:, 128:] = t[2][:, :64]
    wv[:, :128] = jnp.where(low, swap(t[0]), t[1])
    wv[:, 128:] = swap(t[2])[:, :64]
    wq[:, :128] = t[3]
    wq[:, 128:] = t[4][:, :64]
    wp[:, :128] = jnp.where(low, swap(t[4]), swap(t[5]))
    wp[:, 128:] = swap(t[5])[:, :64]
    turn[...] = jnp.zeros(turn.shape, f32)
    turn[:shard, :] = grad_ref[:, 768:1024].astype(f32)
    wo[...] = jnp.transpose(turn[...], (1, 0))[: wo.shape[0], :shard]
    wi[...] = grad_ref[:, 1024 : 1024 + hidden].astype(f32)
    wu[...] = grad_ref[:, 1024 + hidden :].astype(f32)
    for h in range(cb.shape[0]):
        for i, ref in ((0, cb), (1, pb), (2, tbias), (5, vb)):
            ref[h : h + 1, :] = hs_ref[8 * h + i : 8 * h + i + 1, :64]
        te[h] = hs_ref[8 * h + 3 : 8 * h + 5, :64]
    ib[...] = vec_ref[6:7, :hidden].reshape(hidden)
    for i, ref in enumerate((ab, fb, ag, ash, fg, fs)):
        ref[...] = vec_ref[i : i + 1, :].reshape(ref.shape[0])


def angle_tables(seq, width):
    half = width // 2
    freq = 1.0 / 10000.0 ** (np.arange(half, dtype=np.float64) * (2.0 / width))
    steps = 32
    coarse = (seq - 1 - steps * np.arange(2 * seq // steps, dtype=np.float64))[:, None] * freq[None, :]
    fine = np.arange(steps, dtype=np.float64)[:, None] * freq[None, :]
    return (
        np.stack([np.sin(coarse), np.cos(coarse)]).astype(np.float32),
        np.stack([np.sin(fine), np.cos(fine)]).astype(np.float32),
    )


def per_device(
    layer_input, doc_ids, type_ids, positions, query_weight, key_weight, value_weight, pos_kernel,
    out_weight, inner_weight, outer_weight, content_bias, pos_bias, type_bias, value_bias, type_embed,
    inner_bias, attn_bias, ffn_bias, attn_gain, attn_shift, ffn_gain, ffn_shift, out_grad,
):
    rows, width = layer_input.shape
    seq = doc_ids.shape[0]
    heads, depth = content_bias.shape
    hidden = inner_weight.shape[1]
    shard = query_weight.shape[0]
    members = seq // rows
    count = width // shard
    cols = heads * depth
    ring_on = shard % 16 == 0 and count % 2 == 0 and count > 2

    type_rows = jnp.transpose(type_embed, (1, 0, 2))
    ta, tb = angle_tables(seq, width)
    given = [
        layer_input, out_grad, doc_ids, type_ids, content_bias, pos_bias, type_bias, value_bias, type_rows, inner_bias,
        attn_bias, ffn_bias, attn_gain, attn_shift, ffn_gain, ffn_shift, ta, tb,
    ]
    sds = jax.ShapeDtypeStruct
    vm = pltpu.VMEM
    blocks = count if ring_on else 1
    deep = width // blocks
    full = {
        "w1g": 768, "wog": 256, "wig": hidden, "wug": hidden,
        "dwa": 512, "dwb": 256, "dwo": 256, "dwi": hidden, "dwu": hidden,
    }
    outs = {
        "out_ref": sds((rows, width), bf16), "ig_ref": sds((rows, width), bf16),
        "vec_ref": sds((8, width), f32), "hs_ref": sds((8 * heads, 128), f32),
    }
    extra = {"vec": vm((8, width), f32), "hs": vm((8 * heads, 128), f32)}
    if ring_on:
        given += [query_weight, key_weight, value_weight, pos_kernel, out_weight, inner_weight, outer_weight.T]
        names = IN_BOTH + IN_RING
        outs["grad_ref"] = sds((shard, 1024 + 2 * hidden), f32)
        extra |= {name: vm((blocks, deep, wide), bf16) for name, wide in full.items()}
        for name in OUT_WHOLE:
            extra["g" + name[1:]] = vm((blocks - 1, deep, full[name]), bf16)
        extra["vec_all"] = vm((blocks, 8, width), f32)
        extra["vec_mp"] = vm((members, 8, width), f32)
        extra["hs_all"] = vm((blocks, 8 * heads, 128), f32)
    else:
        q3, k3, v3 = (w.reshape(shard, heads, depth) for w in (query_weight, key_weight, value_weight))
        kv = jnp.stack([k3, v3], axis=2).reshape(shard, 2 * cols)
        out_t = jnp.pad(out_weight.T, ((0, 0), (0, 256 - cols)))
        mine = jnp.concatenate([kv, query_weight, pos_kernel, out_t, inner_weight, outer_weight.T], axis=1)
        gathered = lax.all_gather(mine, "dp", axis=0, tiled=True)[None]
        bounds = np.cumsum([0] + [full[name] for name in IN_WHOLE])
        given += [gathered[:, :, lo:hi] for lo, hi in zip(bounds[:-1], bounds[1:])]
        names = IN_BOTH + IN_WHOLE
        outs |= {name: sds((1, width, full[name]), bf16) for name in OUT_WHOLE}

    block = (members, rows, width)
    per_head = (heads, seq, 128)
    scratch = {
        "xs": vm(block, bf16), "hb": vm(block, bf16), "eb2": vm(block, bf16), "eb1": vm(block, bf16),
        "part_a": vm(block, bf16), "part_b": vm(block, bf16),
        "r1a": vm((2, rows, width), bf16), "r1b": vm((2, rows, width), bf16),
        "r2a": vm((rows, width), bf16), "r2b": vm((rows, width), bf16),
        "sxa": vm((rows, width), bf16), "sxb": vm((rows, width), bf16),
        "own_f": vm((rows, width), f32), "table": vm((2 * seq, width), bf16), "rel": vm((heads, 2 * seq, 128), bf16),
        "qa": vm(per_head, bf16), "qr": vm(per_head, bf16), "ka": vm(per_head, bf16), "va": vm(per_head, bf16),
        "q32": vm(per_head, f32), "es": vm((heads, seq, seq), bf16), "a32": vm(per_head, f32),
        "attnp": vm((seq, 256), bf16), "act": vm((members, rows, hidden), bf16),
        "slope": vm((members, rows, hidden), bf16), "igr": vm((members, rows, hidden), bf16),
        "h1": vm((rows, width), f32), "n1": vm((rows, width), f32), "e2": vm((rows, width), f32),
        "inv1": vm((rows, 128), f32), "e1": vm((rows, width), f32), "dkv": vm((heads, 128, seq), f32),
        "drt": vm((256, 2 * seq), f32), "dqkv": vm((seq, 640), bf16), "flip": vm((rows, rows), bf16),
        "qmeta": vm((seq, 128), bf16), "kmeta": vm((seq, 128), bf16), "small": vm((8 * heads, 128), f32),
        "ln": vm((8, width), f32), "ibs": vm((8, hidden), f32),
        "send_sems": pltpu.SemaphoreType.DMA((192,)), "recv_sems": pltpu.SemaphoreType.DMA((192,)),
    }
    scratch |= extra
    inside = pl.BlockSpec(memory_space=pltpu.VMEM)
    made = pl.pallas_call(
        functools.partial(layer_kernel, ring_on, [*names, *outs, *scratch]),
        out_shape=list(outs.values()),
        in_specs=[inside] * len(given),
        out_specs=[inside] * len(outs),
        scratch_shapes=list(scratch.values()),
        compiler_params=pltpu.CompilerParams(collective_id=0, has_side_effects=True, vmem_limit_bytes=67043328),
        name="layer",
    )(*given)
    made = dict(zip(outs, made))

    if ring_on:
        grads, vec, hs = made["grad_ref"], made["vec_ref"], made["hs_ref"]
    else:
        grads = jnp.concatenate([made[name][0] for name in ("dwa", "dwb", "dwo", "dwi", "dwu")], axis=1)
        grads = lax.psum_scatter(grads, "dp", scatter_dimension=0, tiled=True).astype(f32)
        vec, hs = lax.psum((made["vec_ref"], made["hs_ref"]), "dp")
        vec = jnp.concatenate([lax.psum(vec[:6], "mp"), vec[6:]], axis=0)
    small = sds((heads, depth), f32)
    line = sds((width,), f32)
    results = pl.pallas_call(
        finish_kernel,
        out_shape=[
            made["out_ref"], made["ig_ref"], *[sds((shard, cols), f32)] * 4, sds((cols, shard), f32),
            sds((shard, hidden), f32), sds((shard, hidden), f32), *[small] * 4, sds((heads, 2, depth), f32),
            sds((hidden,), f32), *[line] * 6,
        ],
        in_specs=[inside] * 5,
        out_specs=[inside] * 21,
        scratch_shapes=[vm((128, 256), f32)],
        name="finish",
    )(made["out_ref"], made["ig_ref"], grads, vec, hs)
    results = list(results)
    results[8] = results[8].T
    results[13] = jnp.transpose(results[13], (1, 0, 2))
    return tuple(results)


def solution(mesh):
    rows = P(("dp", "mp"), None)
    token = P("dp")
    placed = (
        (rows, token, token, token)
        + (P("dp", "mp"),) * 4
        + (P("mp", "dp"), P("dp", "mp"), P("mp", "dp"))
        + (P("mp", None),) * 4
        + (P(None, "mp", None), P("mp"))
        + (P(),) * 6
        + (rows,)
    )
    given = (
        (rows, rows)
        + (P("dp", "mp"),) * 4
        + (P("mp", "dp"), P("dp", "mp"), P("mp", "dp"))
        + (P("mp", None),) * 4
        + (P(None, "mp", None), P("mp"))
        + (P(),) * 6
    )
    return jax.shard_map(per_device, mesh=mesh, in_specs=placed, out_specs=given, check_vma=False)
```

```python
import functools
import math

import jax
import jax.numpy as jnp
import numpy as np
from jax import lax
from jax.experimental import pallas as pl
from jax.experimental.pallas import tpu as pltpu
from jax.sharding import PartitionSpec as P

f32 = jnp.float32
bf16 = jnp.bfloat16
MESH = pl.DeviceIdType.MESH
MASK = -1e30
DOC_LEAST = 60
NN = (((1,), (0,)), ((), ()))
NT = (((1,), (1,)), ((), ()))
TN = (((0,), (0,)), ((), ()))


def mm(a, b, dims):
    return lax.dot_general(a, b, dims, preferred_element_type=f32)


def lane_of(rows):
    return lax.broadcasted_iota(jnp.int32, (rows, 128), 1)


def low_half(value):
    return jnp.where(lane_of(value.shape[0]) < 64, value, 0.0)


def swap(value):
    return pltpu.roll(value, 64, 1)


class Links:
    def __init__(self, send_sems, recv_sems):
        self.send_sems = send_sems
        self.recv_sems = recv_sems
        self.used = 0
        self.sent = []

    def start(self, src, dst, where):
        copy = pltpu.make_async_remote_copy(
            src_ref=src,
            dst_ref=dst,
            send_sem=self.send_sems.at[self.used],
            recv_sem=self.recv_sems.at[self.used],
            device_id=where,
            device_id_type=MESH,
        )
        self.used += 1
        self.sent.append(copy)
        copy.start()
        return copy

    def drain(self, some=None):
        for copy in some or self.sent:
            copy.wait_send()
            self.sent = [other for other in self.sent if other is not copy]


def norm_stats(summed):
    center = summed - jnp.mean(summed, axis=-1, keepdims=True)
    spread = jnp.mean(center * center, axis=-1, keepdims=True)
    inv_std = lax.rsqrt(spread + 1e-06)
    return center * inv_std, inv_std


def norm_back(grad, normed, inv_std, gain):
    scaled = grad * gain
    return inv_std * (
        scaled
        - jnp.mean(scaled, axis=-1, keepdims=True)
        - normed * jnp.mean(scaled * normed, axis=-1, keepdims=True)
    )


def col_sum(value):
    return jnp.sum(value, axis=0, keepdims=True)


class Ring:
    def __init__(self, count):
        mine = lax.axis_index("dp")
        row = lax.rem(mine, 2)
        along = lax.div(mine, 2)
        self.count = count
        self.place = (1 - row) * along + row * (count - 1 - along)

    def at(self, offset):
        place = lax.rem(self.place + (offset + self.count), self.count)
        back = lax.div(place, self.count // 2)
        return (1 - back) * 2 * place + back * (2 * (self.count - 1 - place) + 1)


class Flow:
    def __init__(self, sign, hops, rows, slot):
        self.sign, self.hops, self.rows, self.slot = sign, hops, rows, slot


def flows_of(count, rows):
    near = count // 2 - 1
    if rows % 32:
        return [Flow(1, near + 1, pl.ds(0, rows), 0), Flow(-1, near, pl.ds(0, rows), near + 1)]
    first, second = pl.ds(0, rows // 2), pl.ds(rows // 2, rows // 2)
    return [
        Flow(1, near + 1, first, 0),
        Flow(-1, near + 1, second, near),
        Flow(-1, near, first, near + 1),
        Flow(1, near, second, 0),
    ]


class Spread:
    def __init__(self, links, ring, bufs):
        self.links, self.ring, self.bufs = links, ring, bufs
        self.done = 0
        self.last = max(f.hops for f in flows_of(ring.count, bufs[0].shape[1]))
        self.moves = {}

    def begin(self):
        self.send(0)

    def send(self, s):
        for b, buf in enumerate(self.bufs):
            for f, flow in enumerate(flows_of(self.ring.count, buf.shape[1])):
                if s > 0 and s <= flow.hops:
                    self.moves[b, f].wait_recv()
                if s < flow.hops:
                    ref = buf.at[self.ring.at(-flow.sign * s), flow.rows]
                    self.moves[b, f] = self.links.start(ref, ref, {"dp": self.ring.at(flow.sign)})

    def step(self):
        if self.done < self.last:
            self.done += 1
            self.send(self.done)

    def finish(self):
        while self.done < self.last:
            self.step()


class Collect:
    def __init__(self, links, ring, bufs, gots):
        self.links, self.ring = links, ring
        self.bufs, self.gots = bufs, gots
        self.done = 0
        self.last = max(f.hops for f in flows_of(ring.count, bufs[0].shape[1]))
        self.moves = {}

    def begin(self):
        self.send(0)

    def send(self, s):
        for b, (buf, got) in enumerate(zip(self.bufs, self.gots)):
            for f, flow in enumerate(flows_of(self.ring.count, buf.shape[1])):
                if s > 0 and s <= flow.hops:
                    self.moves[b, f].wait_recv()
                if s < flow.hops:
                    owner = self.ring.at(flow.sign * (flow.hops - s))
                    if s > 0:
                        both = buf[owner, flow.rows].astype(f32) + got[flow.slot + s - 1, flow.rows].astype(f32)
                        buf[owner, flow.rows] = both.astype(bf16)
                    self.moves[b, f] = self.links.start(
                        buf.at[owner, flow.rows], got.at[flow.slot + s, flow.rows], {"dp": self.ring.at(flow.sign)}
                    )

    def step(self):
        if self.done < self.last:
            self.done += 1
            self.send(self.done)

    def finish(self):
        while self.done < self.last:
            self.step()

    def take(self, b, out_ref, columns):
        buf, got = self.bufs[b], self.gots[b]
        mine = self.ring.at(0)
        flows = flows_of(self.ring.count, buf.shape[1])
        for start in sorted({flow.rows.start for flow in flows}):
            total = None
            for flow in flows:
                if flow.rows.start == start:
                    part = got[flow.slot + flow.hops - 1, flow.rows].astype(f32)
                    total = buf[mine, flow.rows].astype(f32) + part if total is None else total + part
                    rows = flow.rows
            out_ref[rows, columns] = total


IN_BOTH = (
    "x_ref", "og_ref", "doc_ref", "kind_ref", "cb_ref", "pb_ref", "tbias_ref", "vb_ref", "te_ref", "ib_ref", "ab_ref",
    "fb_ref", "ag_ref", "as_ref", "fg_ref", "fs_ref", "ta_ref", "tb_ref",
)
IN_RING = (
    "wq_ref", "wk_ref", "wv_ref", "wp_ref", "wo_ref", "wi_ref", "wu_ref",
)
IN_WHOLE = (
    "w1g", "wog", "wig", "wug",
)
OUT_WHOLE = (
    "dwa", "dwb", "dwo", "dwi", "dwu",
)


def layer_kernel(ring_on, names, *refs):
    r = dict(zip(names, refs, strict=True))
    (x_ref, og_ref, doc_ref, kind_ref, cb_ref, pb_ref, tbias_ref, vb_ref, te_ref, ib_ref,
     ab_ref, fb_ref, ag_ref, as_ref, fg_ref, fs_ref, ta_ref, tb_ref) = (r[n] for n in IN_BOTH)
    w1g, wog, wig, wug = (r[n] for n in IN_WHOLE)
    dwa, dwb, dwo, dwi, dwu = (r[n] for n in OUT_WHOLE)
    out_ref, ig_ref = r["out_ref"], r["ig_ref"]
    vec_ref, hs_ref = r["vec"], r["hs"]
    (xs, hb, eb2, eb1, part_a, part_b, r1a, r1b, r2a, r2b, sxa, sxb, own_f,
     table, rel, qa, qr, ka, va, q32, es, a32, attnp, act, slope, igr,
     h1, n1, e2, inv1, e1, dkv, drt, dqkv, flip, qmeta_ref, kmeta_ref, small_ref, per_head, ln_ref, ibs,
     send_sems, recv_sems) = (r[n] for n in SCRATCH)
    rows = x_ref.shape[0]
    width = x_ref.shape[1]
    hidden = wig.shape[2]
    members = xs.shape[0]
    seq = members * rows
    heads = es.shape[0]
    half = width // 2
    scale = 0.125
    me = lax.axis_index("mp")
    core = lax.rem(me, 2)
    side = lax.div(me, 2)
    mate = me + 1 - 2 * core
    across = lax.rem(me + 2, 4)
    diag = lax.rem(mate + 2, 4)
    links = Links(send_sems, recv_sems)
    to_mate = {"mp": mate}
    to_across = {"mp": across}

    barrier = pltpu.get_barrier_semaphore()
    peers = [to_mate, to_across]
    if ring_on:
        ring = Ring(w1g.shape[0])
        peers += [{"dp": ring.at(1)}, {"dp": ring.at(-1)}]
    for where in peers:
        pl.semaphore_signal(barrier, inc=1, device_id=where, device_id_type=MESH)
    pl.semaphore_wait(barrier, len(peers))

    def whole(ref):
        return ref[...].reshape(width, ref.shape[2])

    def gather_start(buf):
        a = links.start(buf.at[me], buf.at[me], to_across)
        b = links.start(buf.at[me], buf.at[me], to_mate)
        return a, b

    def gather_forward(buf, first):
        first.wait_recv()
        return links.start(buf.at[across], buf.at[across], to_mate)

    part_rows = rows // 2
    halves = [pl.ds(0, part_rows), pl.ds(part_rows, part_rows)]
    near_pair, far_pair = pl.ds(2 * side, 2), pl.ds(2 * (1 - side), 2)

    class Gather:
        def __init__(self, buf, x):
            self.buf, self.x = buf, x
            mine_x = buf.at[me, halves[x]]
            self.over = links.start(mine_x, mine_x, to_across)
            self.beside = links.start(mine_x, mine_x, to_mate)

        def forward(self):
            self.over.wait_recv()
            theirs = self.buf.at[across, halves[self.x]]
            self.last = links.start(theirs, theirs, to_mate)

    xs[me] = x_ref[...]
    x_a, x_b = gather_start(xs)

    if ring_on:
        shard = w1g.shape[1]
        mine = ring.at(0)
        own_f[...] = jnp.zeros(own_f.shape, f32)
        tiles = []
        for i, name in enumerate(IN_RING[:4]):
            r0, c0 = 128 * (i // 2), 256 * (i % 2)
            own_f[r0 : r0 + shard, c0 : c0 + r[name].shape[1]] = r[name][...].astype(f32)
            tiles.append((own_f[r0 : r0 + shard, c0 : c0 + 128], own_f[r0 : r0 + shard, c0 + 128 : c0 + 256]))
        (qx, qy), (kx, ky), (vx, vy), (px, py) = tiles
        low = lane_of(shard) < 64
        joined = [
            jnp.where(low, kx, swap(vx)),
            jnp.where(low, swap(kx), vx),
            jnp.where(low, ky, swap(vy)),
            qx,
            jnp.where(low, qy, swap(px)),
            jnp.where(low, swap(px), swap(py)),
        ]
        for i, tile in enumerate(joined):
            w1g[mine, :, 128 * i : 128 * i + 128] = tile.astype(bf16)
        spread_1 = Spread(links, ring, [w1g])
        spread_1.begin()
        wo_ref = r["wo_ref"]
        own_f[:, :128] = jnp.zeros((256, 128), f32)
        own_f[: wo_ref.shape[0], :shard] = wo_ref[...].astype(f32)
        wog[mine] = jnp.transpose(own_f[:, :128], (1, 0))[:shard].astype(bf16)
        wig[mine] = r["wi_ref"][...]
        wug[mine] = r["wu_ref"][...]
        spread_o, spread_i, spread_u = (Spread(links, ring, [ref]) for ref in (wog, wig, wug))

    small_ref[...] = jnp.zeros(small_ref.shape, f32)
    for h in range(heads):
        for i, ref in enumerate((cb_ref, pb_ref, tbias_ref)):
            small_ref[h, i : i + 1, 0:64] = ref[h : h + 1, :]
        small_ref[h, 3:5, 0:64] = te_ref[h]
        small_ref[h, 5:6, 0:64] = vb_ref[h : h + 1, :]
    for i, ref in enumerate((ab_ref, ag_ref, as_ref, fb_ref, fg_ref, fs_ref)):
        ln_ref[i : i + 1, :] = ref[...].reshape(1, width)
    ibs[0:1, :] = ib_ref[...].reshape(1, hidden)

    slots = seq // DOC_LEAST + 2
    ends = (doc_ref[...].reshape(1, seq) - lax.axis_index("dp") * seq).astype(f32)
    slot = jnp.where(ends > seq - 1.5, slots - 1.0, jnp.floor((ends + 0.5) * (1.0 / DOC_LEAST)))
    slot = jnp.transpose(jnp.broadcast_to(slot, (128, seq)), (1, 0))
    kind = jnp.transpose(jnp.broadcast_to(kind_ref[...].reshape(1, seq).astype(f32), (128, seq)), (1, 0))
    lane = lane_of(seq)
    hit = jnp.abs(slot + 68.0 - lane.astype(f32)) < 0.5
    qmeta_ref[...] = jnp.where(lane == 64, kind, jnp.where(hit, 1.0, 0.0)).astype(bf16)
    miss = jnp.where(hit, 0.0, MASK)
    kmeta_ref[...] = jnp.where(
        lane < 66, 1.0, jnp.where(lane < 68, kind, jnp.where(lane < 68 + slots, miss, 0.0))
    ).astype(bf16)
    x_f = gather_forward(xs, x_a)
    if ring_on:
        spread_1.step()

    steps = tb_ref.shape[1]

    def table_step(u, carry):
        sa = ta_ref[0, pl.ds(u, 1), :]
        ca = ta_ref[1, pl.ds(u, 1), :]
        at = pl.multiple_of(u * steps, steps)
        table[pl.ds(at, steps), :half] = (sa * tb_ref[1] - ca * tb_ref[0]).astype(bf16)
        table[pl.ds(at, steps), half:] = (ca * tb_ref[1] + sa * tb_ref[0]).astype(bf16)
        return carry

    lax.fori_loop(0, ta_ref.shape[1] // 2, table_step, 0)
    if ring_on:
        spread_1.step()
    lax.fori_loop(ta_ref.shape[1] // 2, ta_ref.shape[1], table_step, 0)

    ri = lax.broadcasted_iota(jnp.int32, (rows, rows), 0)
    ci = lax.broadcasted_iota(jnp.int32, (rows, rows), 1)
    flip[...] = jnp.where(ri + ci == rows - 1, 1.0, 0.0).astype(bf16)
    if ring_on:
        spread_1.step()
        spread_o.begin()
        spread_1.finish()

    def rel_step(i, carry):
        at = pl.ds(pl.multiple_of(i * 256, 256), 256)
        got = mm(table[at, :], w1g[:, :, 512:768].reshape(width, 256), NN)
        rel[0, at, :] = low_half(swap(got[:, :128])).astype(bf16)
        rel[1, at, :] = low_half(got[:, 128:]).astype(bf16)
        rel[2, at, :] = low_half(swap(got[:, 128:])).astype(bf16)
        return carry

    lax.fori_loop(0, 2 * seq // 256, rel_step, 0)

    def project(o, carry):
        at = pl.ds(pl.multiple_of(o * rows, rows), rows)
        got = mm(xs[o], w1g[:, :, :640].reshape(width, 640), NN)
        lane = lane_of(rows)
        qmeta = qmeta_ref[at, :].astype(f32)
        kmeta = kmeta_ref[at, :].astype(f32)
        typed = qmeta[:, 64:65]
        for h in range(heads):
            kv = got[:, 128 * h : 128 * h + 128]
            ka[h, at, :] = jnp.where(lane < 64, kv, kmeta).astype(bf16)
            vrow = swap(kv) + small_ref[h, 5:6, :]
            va[h, at, :] = jnp.where(lane < 64, vrow, jnp.where(lane < 66, 1.0, 0.0)).astype(bf16)
            q = got[:, 384:512] if h < 2 else got[:, 512:640]
            if h == 1:
                q = swap(q)
            q = low_half(q)
            q32[h, at, :] = q
            qt = q + small_ref[h, 2:3, :]
            ct0 = jnp.sum(qt * small_ref[h, 3:4, :], axis=1, keepdims=True)
            ct1 = jnp.sum(qt * small_ref[h, 4:5, :], axis=1, keepdims=True)
            diff = (ct1 - ct0) * scale
            base = ct0 * scale + diff * (1.0 - typed)
            tilt = diff * (2.0 * typed - 1.0)
            base_hi = base.astype(bf16).astype(f32)
            tilt_hi = tilt.astype(bf16).astype(f32)
            extra = jnp.where(
                lane == 64,
                base_hi,
                jnp.where(
                    lane == 65,
                    base - base_hi,
                    jnp.where(lane == 66, tilt_hi, jnp.where(lane == 67, tilt - tilt_hi, qmeta)),
                ),
            )
            qc = (q + small_ref[h, 0:1, :]) * scale
            qa[h, at, :] = jnp.where(lane < 64, qc, extra).astype(bf16)
            qr[h, at, :] = low_half((q + small_ref[h, 1:2, :]) * scale).astype(bf16)
        return carry

    def poll(*steppers):
        for stepper in steppers:
            stepper.step()

    if ring_on:
        spread_o.step()
    x_b.wait_recv()
    x_f.wait_recv()
    lax.fori_loop(0, members, project, 0)
    if ring_on:
        poll(spread_o)
        spread_i.begin()

    wide = seq + rows

    def attend(o, between=None):
        at = pl.ds(pl.multiple_of(o * rows, rows), rows)
        window = pl.ds(pl.multiple_of((members - 1 - o) * rows, rows), wide)

        def one_head(h, carry):
            s = mm(qa[h, at, :], ka[h], NT)
            g = mm(qr[h, at, :], rel[h, window, :], NT)
            g = pltpu.roll(g, wide + 1 - rows, 1, stride=1, stride_axis=0)
            s = s + g[:, :seq]
            top = jnp.max(s, axis=1, keepdims=True)
            e = jnp.exp(s - top).astype(bf16)
            es[h, at, :] = e
            o_full = mm(e, va[h], NN)
            inv = 1.0 / o_full[:, 64:65]
            a32[h, at, :] = jnp.where(lane_of(rows) < 64, o_full * inv, inv)
            return carry

        if between:
            lax.fori_loop(0, 1, one_head, 0)
            between()
        lax.fori_loop(1 if between else 0, heads, one_head, 0)
        first = low_half(a32[0, at, :]) + swap(low_half(a32[1, at, :]))
        attnp[at, :128] = first.astype(bf16)
        attnp[at, 128:] = low_half(a32[2, at, :]).astype(bf16)

    def branch_of(o):
        return mm(attnp[pl.ds(pl.multiple_of(o * rows, rows), rows), :], whole(wog), NT)

    class Scatter:
        def __init__(self, part, r1, r2, sx):
            self.part, self.r1, self.r2, self.sx = part, r1, r2, sx
            self.far, self.near, self.over = [None, None], [None, None], [None, None]

        def give_diag(self, x, value):
            self.part[diag, halves[x]] = value.astype(bf16)
            self.far[x] = links.start(self.part.at[diag, halves[x]], self.r1.at[1 - side, halves[x]], to_mate)

        def give_across(self, x, value):
            self.part[across, halves[x]] = value.astype(bf16)

        def give_mate(self, x, value):
            self.part[mate, halves[x]] = value.astype(bf16)
            self.near[x] = links.start(self.part.at[mate, halves[x]], self.r1.at[side, halves[x]], to_mate)

        def give_own(self, x, value):
            own_f[halves[x]] = value

        def give_near(self, x, pair):
            self.give_mate(x, jnp.where(core == 0, pair[1], pair[0]))
            self.give_own(x, jnp.where(core == 0, pair[0], pair[1]))

        def give_far(self, x, pair):
            self.give_diag(x, jnp.where(core == 0, pair[1], pair[0]))
            self.give_across(x, jnp.where(core == 0, pair[0], pair[1]))

        def pass_on(self, x):
            self.far[x].wait_recv()
            both = self.part[across, halves[x]].astype(f32) + self.r1[1 - side, halves[x]].astype(f32)
            self.sx[halves[x]] = both.astype(bf16)
            self.over[x] = links.start(self.sx.at[halves[x]], self.r2.at[halves[x]], to_across)

        def release(self):
            links.drain(self.far + self.near + self.over)

        def take(self, x):
            self.near[x].wait_recv()
            near = own_f[halves[x]] + self.r1[side, halves[x]].astype(f32)
            self.over[x].wait_recv()
            return near + self.r2[halves[x]].astype(f32)

    def split(value):
        return value[:part_rows], value[part_rows:]

    first_red = red = Scatter(part_a, r1a, r2a, sxa)
    attend(diag)
    if ring_on:
        poll(spread_o, spread_i)
        spread_u.begin()
    attend(across)
    if ring_on:
        spread_o.finish()
    for x, (there, here) in enumerate(zip(split(branch_of(diag)), split(branch_of(across)))):
        red.give_diag(x, there)
        red.give_across(x, here)
    if ring_on:
        poll(spread_i, spread_u)

    def first_pass():
        red.pass_on(0)
        red.pass_on(1)

    attend(mate, first_pass)
    for x, value in enumerate(split(branch_of(mate))):
        red.give_mate(x, value)
    if ring_on:
        poll(spread_i, spread_u)
    attend(me)
    for x, value in enumerate(split(branch_of(me))):
        red.give_own(x, value)
    vec_ref[...] = jnp.zeros((8, width), f32)
    hs_ref[...] = jnp.zeros(hs_ref.shape, f32)

    def first_norm(x):
        at = halves[x]
        summed = x_ref[at, :].astype(f32) + first_red.take(x) + ln_ref[0:1, :]
        normed, inv_std = norm_stats(summed)
        n1[at, :] = normed
        inv1[at, :] = jnp.broadcast_to(inv_std, (part_rows, 128))
        h1[at, :] = normed * ln_ref[1:2, :] + ln_ref[2:3, :]
        hb[me, at] = h1[at, :].astype(bf16)
        return Gather(hb, x)

    def ffn(pair, x):
        inner = mm(hb[pair, halves[x]].reshape(rows, width), whole(wig), NN) + ibs[0:1, :]
        square = inner * inner
        t = jnp.tanh(0.7978845608028654 * (inner + 0.044715 * square * inner))
        made = (0.5 * inner * (1.0 + t)).astype(bf16)
        act[pair, halves[x]] = made.reshape(2, part_rows, hidden)
        steep = (
            0.5 * (1.0 + t)
            + 0.5 * inner * (1.0 - t * t) * 0.7978845608028654 * (1.0 + 3.0 * 0.044715 * square)
        ).astype(bf16)
        slope[pair, halves[x]] = steep.reshape(2, part_rows, hidden)
        return mm(made, whole(wug), NT).reshape(2, part_rows, width)

    def stage(start, block, reducer, ready=None):
        moves = [start(0), start(1)]
        if ready:
            ready()
        for x in (0, 1):
            moves[x].beside.wait_recv()
            reducer.give_near(x, block(near_pair, x))
        moves[0].forward()
        moves[0].last.wait_recv()
        reducer.give_far(0, block(far_pair, 0))
        moves[1].forward()
        reducer.pass_on(0)
        moves[1].last.wait_recv()
        reducer.give_far(1, block(far_pair, 1))
        reducer.pass_on(1)

    def weights_ready():
        spread_i.finish()
        spread_u.finish()

    if ring_on:
        poll(spread_i, spread_u)
    second_red = red = Scatter(part_b, r1b, r2b, sxb)
    stage(first_norm, ffn, second_red, weights_ready if ring_on else None)

    def second_norm(x):
        at = halves[x]
        summed = h1[at, :] + second_red.take(x) + ln_ref[3:4, :]
        normed, inv_std = norm_stats(summed)
        out_ref[at, :] = (normed * ln_ref[4:5, :] + ln_ref[5:6, :]).astype(bf16)
        grad = og_ref[at, :].astype(f32)
        back = norm_back(grad, normed, inv_std, ln_ref[4:5, :])
        e2[at, :] = back
        eb2[me, at] = back.astype(bf16)
        move = Gather(eb2, x)
        vec_ref[4:5, :] += col_sum(grad * normed)
        vec_ref[5:6, :] += col_sum(grad)
        vec_ref[1:2, :] += col_sum(back)
        return move

    def ffn_back(pair, x):
        steep = slope[pair, halves[x]].reshape(rows, hidden).astype(f32)
        grad_inner = (mm(eb2[pair, halves[x]].reshape(rows, width), whole(wug), NN) * steep).astype(bf16)
        igr[pair, halves[x]] = grad_inner.reshape(2, part_rows, hidden)
        vec_ref[6:7, :hidden] += col_sum(grad_inner.astype(f32))
        return mm(grad_inner, whole(wig), NT).reshape(2, part_rows, width)

    third_red = Scatter(part_a, r1a, r2a, sxa)
    stage(second_norm, ffn_back, third_red, first_red.release)
    flat = lambda ref: ref[...].reshape(seq, ref.shape[2])

    def put(ref, value):
        ref[...] = value.astype(bf16).reshape(ref.shape)

    def third_norm(x):
        at = halves[x]
        grad = e2[at, :] + third_red.take(x)
        back = norm_back(grad, n1[at, :], inv1[at, :1], ln_ref[1:2, :])
        e1[at, :] = back
        eb1[me, at] = back.astype(bf16)
        move = Gather(eb1, x)
        vec_ref[2:3, :] += col_sum(grad * n1[at, :])
        vec_ref[3:4, :] += col_sum(grad)
        vec_ref[0:1, :] += col_sum(back)
        return move

    put(dwu, mm(flat(eb2), flat(act), TN))
    if ring_on:
        collect_u = Collect(links, ring, [dwu], [r["gwu"]])
        collect_u.begin()
    g_0 = third_norm(0)
    put(dwi, mm(flat(hb), flat(igr), TN))
    if ring_on:
        collect_i = Collect(links, ring, [dwi], [r["gwi"]])
        collect_i.begin()
    g_1 = third_norm(1)
    if ring_on:
        vec_all, vec_mp = r["vec_all"], r["vec_mp"]
        vec_all[mine] = vec_ref[...]
        spread_4 = Spread(links, ring, [vec_all])
        spread_4.begin()

    dkv[...] = jnp.zeros(dkv.shape, f32)
    drt[...] = jnp.zeros(drt.shape, f32)

    def attend_back(o):
        at = pl.ds(pl.multiple_of(o * rows, rows), rows)
        lo = pl.multiple_of((members - 1 - o) * rows, rows)
        window = pl.ds(lo, wide)
        d_all = mm(eb1[o], whole(wog), NN).astype(bf16).astype(f32)
        lane = lane_of(rows)
        typed = qmeta_ref[at, :].astype(f32)[:, 64:65]
        per_head[0] = d_all[:, :128]
        per_head[1] = swap(d_all[:, :128])
        per_head[2] = d_all[:, 128:]

        def one_head(h, carry):
            d_out = per_head[h]
            kept = a32[h, at, :]
            d_out = low_half(d_out * kept[:, 64:65]).astype(bf16).astype(f32)
            d_row = -jnp.sum(d_out * kept, axis=1, keepdims=True)
            d_hi = d_row.astype(bf16).astype(f32)
            d_aug = jnp.where(lane == 64, d_hi, jnp.where(lane == 65, d_row - d_hi, d_out)).astype(bf16)
            e = es[h, at, :]
            ds = (e.astype(f32) * mm(d_aug, va[h], NT)).astype(bf16)
            dkv[h, 64:128, :] += mm(d_aug, e, TN)[:64]
            dkv[h, 0:64, :] += mm(qa[h, at, :], ds, TN)[:64]
            dq = mm(ds, ka[h], NN) * scale
            turned = mm(flip[...], ds, NN)
            turned = jnp.concatenate([turned, jnp.zeros((rows, rows), f32)], axis=1)
            dg = pltpu.roll(turned, 0, 1, stride=1, stride_axis=0).astype(bf16)
            dqr = mm(dg, rel[h, window, :], NN) * scale
            qr_turned = mm(flip[...], qr[h, at, :], NN).astype(bf16)
            drt[pl.ds(pl.multiple_of(64 * h + 64, 64), 64), window] += mm(qr_turned, dg, TN)[:64]
            hs_ref[h, 1:2, :] += col_sum(dqr)
            dqr_hi = dqr.astype(bf16)
            dqr_lo = (dqr - dqr_hi.astype(f32)).astype(bf16)
            dqr = mm(flip[...], dqr_hi, NN) + mm(flip[...], dqr_lo, NN)
            total = dq[:, 64:65]
            ones = dq[:, 66:67]
            same = jnp.where(typed > 0.5, ones, total - ones)
            other = total - same
            dqt = other * small_ref[h, 3:4, :] + same * small_ref[h, 4:5, :]
            qt = q32[h, at, :] + small_ref[h, 2:3, :]
            hs_ref[h, 0:1, :] += col_sum(dq)
            hs_ref[h, 2:3, :] += col_sum(dqt)
            hs_ref[h, 3:4, :] += col_sum(other * qt)
            hs_ref[h, 4:5, :] += col_sum(same * qt)
            per_head[h] = low_half(dq + dqr + dqt)
            return carry

        lax.fori_loop(0, heads, one_head, 0)
        dqkv[at, 384:512] = (per_head[0] + swap(per_head[1])).astype(bf16)
        dqkv[at, 512:640] = per_head[2].astype(bf16)

    attend_back(me)
    g_0.beside.wait_recv()
    g_1.beside.wait_recv()
    g_0.forward()
    g_1.forward()
    if ring_on:
        poll(spread_4, collect_u, collect_i)
    attend_back(mate)
    if ring_on:
        poll(spread_4, collect_u, collect_i)
    attend_back(across)
    g_0.last.wait_recv()
    g_1.last.wait_recv()
    put(dwo, mm(flat(eb1), attnp[...], TN))
    if ring_on:
        spread_4.finish()
        total = vec_all[0]
        for i in range(1, ring.count):
            total = total + vec_all[i]
        vec_mp[me] = total
        v_a, v_b = gather_start(vec_mp)
        poll(collect_u, collect_i)
        collect_2 = Collect(links, ring, [dwo], [r["gwo"]])
        collect_2.begin()
    attend_back(diag)
    if ring_on:
        poll(collect_u, collect_i, collect_2)
        v_b.wait_recv()
        v_f = gather_forward(vec_mp, v_a)

    for h in range(heads):
        turned = jnp.transpose(dkv[h], (1, 0)).astype(bf16)
        dqkv[:, 128 * h : 128 * h + 128] = turned
        hs_ref[h, 5:6, :] = swap(col_sum(turned.astype(f32)))
    put(dwa, mm(flat(xs), dqkv[:, :512], TN))
    if ring_on:
        hs_all = r["hs_all"]
        hs_all[mine] = hs_ref[...].reshape(8 * heads, 128)
        spread_5 = Spread(links, ring, [hs_all])
        spread_5.begin()
        collect_3 = Collect(links, ring, [dwa], [r["gwa"]])
        collect_3.begin()

    def input_back(o):
        at = pl.ds(pl.multiple_of(o * rows, rows), rows)
        return mm(dqkv[at, :], w1g[:, :, :640].reshape(width, 640), NT)

    second_red.release()
    red = Scatter(part_b, r1b, r2b, sxb)
    for x, value in enumerate(split(input_back(diag))):
        red.give_diag(x, value)
    for x, value in enumerate(split(input_back(across))):
        red.give_across(x, value)
    tail = mm(flat(xs), dqkv[:, 512:640], TN)
    d_pos = jnp.transpose(mm(drt[...].astype(bf16), table[...], NN), (1, 0))
    put(dwb, jnp.concatenate([tail + d_pos[:, :128], d_pos[:, 128:]], axis=1))
    if ring_on:
        collect_4 = Collect(links, ring, [dwb], [r["gwb"]])
        collect_4.begin()
    red.pass_on(0)
    red.pass_on(1)
    if ring_on:
        poll(collect_2, collect_3, spread_5)
    for x, value in enumerate(split(input_back(mate))):
        red.give_mate(x, value)
    for x, value in enumerate(split(input_back(me))):
        red.give_own(x, value)
    if ring_on:
        grad_ref = r["grad_ref"]
        poll(collect_4, collect_3, spread_5)
        collect_u.finish()
        collect_i.finish()
        collect_u.take(0, grad_ref, pl.ds(1024 + hidden, hidden))
        poll(collect_2)
        collect_i.take(0, grad_ref, pl.ds(1024, hidden))
        poll(collect_4, collect_3, spread_5)
        v_f.wait_recv()
        r["vec_ref"][...] = vec_mp[0] + vec_mp[1] + vec_mp[2] + vec_mp[3]
        r["vec_ref"][6:7, :] = vec_mp[me][6:7, :]
        collect_2.finish()
        collect_2.take(0, grad_ref, pl.ds(768, 256))
        poll(collect_4, collect_3, spread_5)
    for x in (0, 1):
        ig_ref[halves[x], :] = (e1[halves[x], :] + red.take(x)).astype(bf16)
    if ring_on:
        spread_5.finish()
        total = hs_all[0]
        for i in range(1, ring.count):
            total = total + hs_all[i]
        r["hs_ref"][...] = total
        collect_3.finish()
        collect_3.take(0, grad_ref, pl.ds(0, 512))
        collect_4.finish()
        collect_4.take(0, grad_ref, pl.ds(512, 256))
    else:
        r["vec_ref"][...] = vec_ref[...]
        r["hs_ref"][...] = hs_ref[...].reshape(8 * heads, 128)
    links.drain()


SCRATCH = (
    "xs", "hb", "eb2", "eb1", "part_a", "part_b", "r1a", "r1b", "r2a", "r2b", "sxa", "sxb", "own_f", "table", "rel",
    "qa", "qr", "ka", "va", "q32", "es", "a32", "attnp", "act", "slope", "igr", "h1", "n1", "e2", "inv1", "e1", "dkv",
    "drt", "dqkv", "flip", "qmeta", "kmeta", "small", "per_head", "ln", "ibs", "send_sems", "recv_sems",
)


def finish_kernel(
    out_ref, ig_ref, grad_ref, vec_ref, hs_ref,
    out, in_grad, wq, wk, wv, wp, wo, wi, wu, cb, pb, tbias, vb, te, ib, ab, fb, ag, ash, fg, fs, turn,
):
    out[...] = out_ref[...]
    in_grad[...] = ig_ref[...]
    shard, hidden = wi.shape
    t = [grad_ref[:, 128 * i : 128 * i + 128].astype(f32) for i in range(6)]
    low = lane_of(shard) < 64
    wk[:, :128] = jnp.where(low, t[0], swap(t[1]))
    wk[:, 128:] = t[2][:, :64]
    wv[:, :128] = jnp.where(low, swap(t[0]), t[1])
    wv[:, 128:] = swap(t[2])[:, :64]
    wq[:, :128] = t[3]
    wq[:, 128:] = t[4][:, :64]
    wp[:, :128] = jnp.where(low, swap(t[4]), swap(t[5]))
    wp[:, 128:] = swap(t[5])[:, :64]
    turn[...] = jnp.zeros(turn.shape, f32)
    turn[:shard, :] = grad_ref[:, 768:1024].astype(f32)
    wo[...] = jnp.transpose(turn[...], (1, 0))[: wo.shape[0], :shard]
    wi[...] = grad_ref[:, 1024 : 1024 + hidden].astype(f32)
    wu[...] = grad_ref[:, 1024 + hidden :].astype(f32)
    for h in range(cb.shape[0]):
        for i, ref in ((0, cb), (1, pb), (2, tbias), (5, vb)):
            ref[h : h + 1, :] = hs_ref[8 * h + i : 8 * h + i + 1, :64]
        te[h] = hs_ref[8 * h + 3 : 8 * h + 5, :64]
    ib[...] = vec_ref[6:7, :hidden].reshape(hidden)
    for i, ref in enumerate((ab, fb, ag, ash, fg, fs)):
        ref[...] = vec_ref[i : i + 1, :].reshape(ref.shape[0])


def angle_tables(seq, width):
    half = width // 2
    freq = 1.0 / 10000.0 ** (np.arange(half, dtype=np.float64) * (2.0 / width))
    steps = 32
    coarse = (seq - 1 - steps * np.arange(2 * seq // steps, dtype=np.float64))[:, None] * freq[None, :]
    fine = np.arange(steps, dtype=np.float64)[:, None] * freq[None, :]
    return (
        np.stack([np.sin(coarse), np.cos(coarse)]).astype(np.float32),
        np.stack([np.sin(fine), np.cos(fine)]).astype(np.float32),
    )


def per_device(
    layer_input, doc_ids, type_ids, positions, query_weight, key_weight, value_weight, pos_kernel,
    out_weight, inner_weight, outer_weight, content_bias, pos_bias, type_bias, value_bias, type_embed,
    inner_bias, attn_bias, ffn_bias, attn_gain, attn_shift, ffn_gain, ffn_shift, out_grad,
):
    rows, width = layer_input.shape
    seq = doc_ids.shape[0]
    heads, depth = content_bias.shape
    hidden = inner_weight.shape[1]
    shard = query_weight.shape[0]
    members = seq // rows
    count = width // shard
    cols = heads * depth
    ring_on = shard % 16 == 0 and count % 2 == 0 and count > 2

    type_rows = jnp.transpose(type_embed, (1, 0, 2))
    ta, tb = angle_tables(seq, width)
    given = [
        layer_input, out_grad, doc_ids, type_ids, content_bias, pos_bias, type_bias, value_bias, type_rows, inner_bias,
        attn_bias, ffn_bias, attn_gain, attn_shift, ffn_gain, ffn_shift, ta, tb,
    ]
    sds = jax.ShapeDtypeStruct
    vm = pltpu.VMEM
    blocks = count if ring_on else 1
    deep = width // blocks
    full = {
        "w1g": 768, "wog": 256, "wig": hidden, "wug": hidden,
        "dwa": 512, "dwb": 256, "dwo": 256, "dwi": hidden, "dwu": hidden,
    }
    outs = {
        "out_ref": sds((rows, width), bf16), "ig_ref": sds((rows, width), bf16),
        "vec_ref": sds((8, width), f32), "hs_ref": sds((8 * heads, 128), f32),
    }
    extra = {"vec": vm((8, width), f32), "hs": vm((heads, 8, 128), f32)}
    if ring_on:
        given += [query_weight, key_weight, value_weight, pos_kernel, out_weight, inner_weight, outer_weight.T]
        names = IN_BOTH + IN_RING
        outs["grad_ref"] = sds((shard, 1024 + 2 * hidden), f32)
        extra |= {name: vm((blocks, deep, wide), bf16) for name, wide in full.items()}
        for name in OUT_WHOLE:
            extra["g" + name[1:]] = vm((blocks - 1, deep, full[name]), bf16)
        extra["vec_all"] = vm((blocks, 8, width), f32)
        extra["vec_mp"] = vm((members, 8, width), f32)
        extra["hs_all"] = vm((blocks, 8 * heads, 128), f32)
    else:
        q3, k3, v3 = (w.reshape(shard, heads, depth) for w in (query_weight, key_weight, value_weight))
        kv = jnp.stack([k3, v3], axis=2).reshape(shard, 2 * cols)
        out_t = jnp.pad(out_weight.T, ((0, 0), (0, 256 - cols)))
        mine = jnp.concatenate([kv, query_weight, pos_kernel, out_t, inner_weight, outer_weight.T], axis=1)
        gathered = lax.all_gather(mine, "dp", axis=0, tiled=True)[None]
        bounds = np.cumsum([0] + [full[name] for name in IN_WHOLE])
        given += [gathered[:, :, lo:hi] for lo, hi in zip(bounds[:-1], bounds[1:])]
        names = IN_BOTH + IN_WHOLE
        outs |= {name: sds((1, width, full[name]), bf16) for name in OUT_WHOLE}

    block = (members, rows, width)
    per_head = (heads, seq, 128)
    scratch = {
        "xs": vm(block, bf16), "hb": vm(block, bf16), "eb2": vm(block, bf16), "eb1": vm(block, bf16),
        "part_a": vm(block, bf16), "part_b": vm(block, bf16),
        "r1a": vm((2, rows, width), bf16), "r1b": vm((2, rows, width), bf16),
        "r2a": vm((rows, width), bf16), "r2b": vm((rows, width), bf16),
        "sxa": vm((rows, width), bf16), "sxb": vm((rows, width), bf16),
        "own_f": vm((rows, width), f32), "table": vm((2 * seq, width), bf16), "rel": vm((heads, 2 * seq, 128), bf16),
        "qa": vm(per_head, bf16), "qr": vm(per_head, bf16), "ka": vm(per_head, bf16), "va": vm(per_head, bf16),
        "q32": vm(per_head, f32), "es": vm((heads, seq, seq), bf16), "a32": vm(per_head, f32),
        "attnp": vm((seq, 256), bf16), "act": vm((members, rows, hidden), bf16),
        "slope": vm((members, rows, hidden), bf16), "igr": vm((members, rows, hidden), bf16),
        "h1": vm((rows, width), f32), "n1": vm((rows, width), f32), "e2": vm((rows, width), f32),
        "inv1": vm((rows, 128), f32), "e1": vm((rows, width), f32), "dkv": vm((heads, 128, seq), f32),
        "drt": vm((256, 2 * seq), f32), "dqkv": vm((seq, 640), bf16), "flip": vm((rows, rows), bf16),
        "qmeta": vm((seq, 128), bf16), "kmeta": vm((seq, 128), bf16), "small": vm((heads, 8, 128), f32), "per_head": vm((heads, rows, 128), f32),
        "ln": vm((8, width), f32), "ibs": vm((8, hidden), f32),
        "send_sems": pltpu.SemaphoreType.DMA((192,)), "recv_sems": pltpu.SemaphoreType.DMA((192,)),
    }
    scratch |= extra
    inside = pl.BlockSpec(memory_space=pltpu.VMEM)
    made = pl.pallas_call(
        functools.partial(layer_kernel, ring_on, [*names, *outs, *scratch]),
        out_shape=list(outs.values()),
        in_specs=[inside] * len(given),
        out_specs=[inside] * len(outs),
        scratch_shapes=list(scratch.values()),
        compiler_params=pltpu.CompilerParams(collective_id=0, has_side_effects=True, vmem_limit_bytes=67043328),
        name="layer",
    )(*given)
    made = dict(zip(outs, made))

    if ring_on:
        grads, vec, hs = made["grad_ref"], made["vec_ref"], made["hs_ref"]
    else:
        grads = jnp.concatenate([made[name][0] for name in ("dwa", "dwb", "dwo", "dwi", "dwu")], axis=1)
        grads = lax.psum_scatter(grads, "dp", scatter_dimension=0, tiled=True).astype(f32)
        vec, hs = lax.psum((made["vec_ref"], made["hs_ref"]), "dp")
        vec = jnp.concatenate([lax.psum(vec[:6], "mp"), vec[6:]], axis=0)
    small = sds((heads, depth), f32)
    line = sds((width,), f32)
    results = pl.pallas_call(
        finish_kernel,
        out_shape=[
            made["out_ref"], made["ig_ref"], *[sds((shard, cols), f32)] * 4, sds((cols, shard), f32),
            sds((shard, hidden), f32), sds((shard, hidden), f32), *[small] * 4, sds((heads, 2, depth), f32),
            sds((hidden,), f32), *[line] * 6,
        ],
        in_specs=[inside] * 5,
        out_specs=[inside] * 21,
        scratch_shapes=[vm((128, 256), f32)],
        name="finish",
    )(made["out_ref"], made["ig_ref"], grads, vec, hs)
    results = list(results)
    results[8] = results[8].T
    results[13] = jnp.transpose(results[13], (1, 0, 2))
    return tuple(results)


def solution(mesh):
    rows = P(("dp", "mp"), None)
    token = P("dp")
    placed = (
        (rows, token, token, token)
        + (P("dp", "mp"),) * 4
        + (P("mp", "dp"), P("dp", "mp"), P("mp", "dp"))
        + (P("mp", None),) * 4
        + (P(None, "mp", None), P("mp"))
        + (P(),) * 6
        + (rows,)
    )
    given = (
        (rows, rows)
        + (P("dp", "mp"),) * 4
        + (P("mp", "dp"), P("dp", "mp"), P("mp", "dp"))
        + (P("mp", None),) * 4
        + (P(None, "mp", None), P("mp"))
        + (P(),) * 6
    )
    return jax.shard_map(per_device, mesh=mesh, in_specs=placed, out_specs=given, check_vma=False)
```

```python
import functools
import math

import jax
import jax.numpy as jnp
import numpy as np
from jax import lax
from jax.experimental import pallas as pl
from jax.experimental.pallas import tpu as pltpu
from jax.sharding import PartitionSpec as P

f32 = jnp.float32
bf16 = jnp.bfloat16
MESH = pl.DeviceIdType.MESH
MASK = -1e30
DOC_LEAST = 60
NN = (((1,), (0,)), ((), ()))
NT = (((1,), (1,)), ((), ()))
TN = (((0,), (0,)), ((), ()))


def mm(a, b, dims):
    return lax.dot_general(a, b, dims, preferred_element_type=f32)


def lane_of(rows):
    return lax.broadcasted_iota(jnp.int32, (rows, 128), 1)


def low_half(value):
    return jnp.where(lane_of(value.shape[0]) < 64, value, 0.0)


def swap(value):
    return pltpu.roll(value, 64, 1)


class Move:
    def __init__(self, src, dst, send_sem, recv_sem, where):
        self.src, self.dst, self.where = src, dst, where
        self.send_sem, self.recv_sem = send_sem, recv_sem

    def described(self):
        return pltpu.make_async_remote_copy(
            src_ref=self.src() if callable(self.src) else self.src,
            dst_ref=self.dst() if callable(self.dst) else self.dst,
            send_sem=self.send_sem(),
            recv_sem=self.recv_sem(),
            device_id=self.where,
            device_id_type=MESH,
        )

    def start(self):
        self.described().start()

    def wait_send(self):
        self.described().wait_send()

    def wait_recv(self):
        self.described().wait_recv()


class Links:
    def __init__(self, send_sems, recv_sems):
        self.send_sems = send_sems
        self.recv_sems = recv_sems
        self.used = 0
        self.sent = []

    def start(self, src, dst, where):
        used = self.used
        copy = Move(src, dst, lambda: self.send_sems.at[used], lambda: self.recv_sems.at[used], where)
        self.used += 1
        self.sent.append(copy)
        copy.start()
        return copy

    def drain(self, some=None):
        for copy in some or self.sent:
            copy.wait_send()
            self.sent = [other for other in self.sent if other is not copy]


def norm_stats(summed):
    center = summed - jnp.mean(summed, axis=-1, keepdims=True)
    spread = jnp.mean(center * center, axis=-1, keepdims=True)
    inv_std = lax.rsqrt(spread + 1e-06)
    return center * inv_std, inv_std


def norm_back(grad, normed, inv_std, gain):
    scaled = grad * gain
    return inv_std * (
        scaled
        - jnp.mean(scaled, axis=-1, keepdims=True)
        - normed * jnp.mean(scaled * normed, axis=-1, keepdims=True)
    )


def col_sum(value):
    return jnp.sum(value, axis=0, keepdims=True)


class Ring:
    def __init__(self, count):
        mine = lax.axis_index("dp")
        row = lax.rem(mine, 2)
        along = lax.div(mine, 2)
        self.count = count
        self.place = (1 - row) * along + row * (count - 1 - along)
        self.places = {offset: self.find(offset) for offset in range(-(count // 2), count // 2 + 1)}

    def at(self, offset):
        return self.places[offset]

    def find(self, offset):
        place = lax.rem(self.place + (offset + self.count), self.count)
        back = lax.div(place, self.count // 2)
        return (1 - back) * 2 * place + back * (2 * (self.count - 1 - place) + 1)


class Flow:
    def __init__(self, sign, hops, rows, slot):
        self.sign, self.hops, self.rows, self.slot = sign, hops, rows, slot


def flows_of(count, rows):
    near = count // 2 - 1
    if rows % 32:
        return [Flow(1, near + 1, pl.ds(0, rows), 0), Flow(-1, near, pl.ds(0, rows), near + 1)]
    first, second = pl.ds(0, rows // 2), pl.ds(rows // 2, rows // 2)
    return [
        Flow(1, near + 1, first, 0),
        Flow(-1, near + 1, second, near),
        Flow(-1, near, first, near + 1),
        Flow(1, near, second, 0),
    ]


def part_of(ref, *index):
    return ref.at[index]


class Spread:
    def __init__(self, links, ring, bufs):
        self.links, self.ring, self.bufs = links, ring, bufs
        self.done = 0
        self.last = max(f.hops for f in flows_of(ring.count, bufs[0].shape[1]))
        self.moves = {}

    def begin(self):
        self.send(0)

    def send(self, s):
        for b, buf in enumerate(self.bufs):
            for f, flow in enumerate(flows_of(self.ring.count, buf.shape[1])):
                if s > 0 and s <= flow.hops:
                    self.moves[b, f].wait_recv()
                if s < flow.hops:
                    ref = functools.partial(part_of, buf, self.ring.at(-flow.sign * s), flow.rows)
                    self.moves[b, f] = self.links.start(ref, ref, {"dp": self.ring.at(flow.sign)})

    def step(self):
        if self.done < self.last:
            self.done += 1
            self.send(self.done)

    def finish(self):
        while self.done < self.last:
            self.step()


class Collect:
    def __init__(self, links, ring, bufs, gots):
        self.links, self.ring = links, ring
        self.bufs, self.gots = bufs, gots
        self.done = 0
        self.last = max(f.hops for f in flows_of(ring.count, bufs[0].shape[1]))
        self.moves = {}

    def begin(self):
        self.send(0)

    def send(self, s):
        for b, (buf, got) in enumerate(zip(self.bufs, self.gots)):
            for f, flow in enumerate(flows_of(self.ring.count, buf.shape[1])):
                if s > 0 and s <= flow.hops:
                    self.moves[b, f].wait_recv()
                if s < flow.hops:
                    owner = self.ring.at(flow.sign * (flow.hops - s))
                    if s > 0:
                        both = buf[owner, flow.rows].astype(f32) + got[flow.slot + s - 1, flow.rows].astype(f32)
                        buf[owner, flow.rows] = both.astype(bf16)
                    self.moves[b, f] = self.links.start(
                        functools.partial(part_of, buf, owner, flow.rows),
                        functools.partial(part_of, got, flow.slot + s, flow.rows),
                        {"dp": self.ring.at(flow.sign)},
                    )

    def step(self):
        if self.done < self.last:
            self.done += 1
            self.send(self.done)

    def finish(self):
        while self.done < self.last:
            self.step()

    def take(self, b, out_ref, columns):
        buf, got = self.bufs[b], self.gots[b]
        mine = self.ring.at(0)
        flows = flows_of(self.ring.count, buf.shape[1])
        for start in sorted({flow.rows.start for flow in flows}):
            total = None
            for flow in flows:
                if flow.rows.start == start:
                    part = got[flow.slot + flow.hops - 1, flow.rows].astype(f32)
                    total = buf[mine, flow.rows].astype(f32) + part if total is None else total + part
                    rows = flow.rows
            out_ref[rows, columns] = total


IN_BOTH = (
    "x_ref", "og_ref", "doc_ref", "kind_ref", "cb_ref", "pb_ref", "tbias_ref", "vb_ref", "te_ref", "ib_ref", "ab_ref",
    "fb_ref", "ag_ref", "as_ref", "fg_ref", "fs_ref", "ta_ref", "tb_ref",
)
IN_RING = (
    "wq_ref", "wk_ref", "wv_ref", "wp_ref", "wo_ref", "wi_ref", "wu_ref",
)
IN_WHOLE = (
    "w1g", "wog", "wig", "wug",
)
OUT_WHOLE = (
    "dwa", "dwb", "dwo", "dwi", "dwu",
)


def layer_kernel(ring_on, names, *refs):
    r = dict(zip(names, refs, strict=True))
    (x_ref, og_ref, doc_ref, kind_ref, cb_ref, pb_ref, tbias_ref, vb_ref, te_ref, ib_ref,
     ab_ref, fb_ref, ag_ref, as_ref, fg_ref, fs_ref, ta_ref, tb_ref) = (r[n] for n in IN_BOTH)
    w1g, wog, wig, wug = (r[n] for n in IN_WHOLE)
    dwa, dwb, dwo, dwi, dwu = (r[n] for n in OUT_WHOLE)
    out_ref, ig_ref = r["out_ref"], r["ig_ref"]
    vec_ref, hs_ref = r["vec"], r["hs"]
    (xs, hb, eb2, eb1, part_a, part_b, r1a, r1b, r2a, r2b, sxa, sxb, own_f,
     table, rel, qa, qr, ka, va, q32, es, a32, attnp, act, slope, igr,
     h1, n1, e2, inv1, e1, dkv, drt, dqkv, flip, qmeta_ref, kmeta_ref, small_ref, per_head, ln_ref, ibs,
     send_sems, recv_sems) = (r[n] for n in SCRATCH)
    rows = x_ref.shape[0]
    width = x_ref.shape[1]
    hidden = wig.shape[2]
    members = xs.shape[0]
    seq = members * rows
    heads = es.shape[0]
    half = width // 2
    scale = 0.125
    me = lax.axis_index("mp")
    core = lax.rem(me, 2)
    side = lax.div(me, 2)
    mate = me + 1 - 2 * core
    across = lax.rem(me + 2, 4)
    diag = lax.rem(mate + 2, 4)
    links = Links(send_sems, recv_sems)
    to_mate = {"mp": mate}
    to_across = {"mp": across}

    barrier = pltpu.get_barrier_semaphore()
    peers = [to_mate, to_across]
    if ring_on:
        ring = Ring(w1g.shape[0])
        peers += [{"dp": ring.at(1)}, {"dp": ring.at(-1)}]
    for where in peers:
        pl.semaphore_signal(barrier, inc=1, device_id=where, device_id_type=MESH)
    pl.semaphore_wait(barrier, len(peers))

    def whole(ref):
        return ref[...].reshape(width, ref.shape[2])

    def gather_start(buf):
        a = links.start(buf.at[me], buf.at[me], to_across)
        b = links.start(buf.at[me], buf.at[me], to_mate)
        return a, b

    def gather_forward(buf, first):
        first.wait_recv()
        return links.start(buf.at[across], buf.at[across], to_mate)

    part_rows = rows // 2
    halves = [pl.ds(0, part_rows), pl.ds(part_rows, part_rows)]
    near_pair, far_pair = pl.ds(2 * side, 2), pl.ds(2 * (1 - side), 2)

    class Gather:
        def __init__(self, buf, x):
            self.buf, self.x = buf, x
            mine_x = buf.at[me, halves[x]]
            self.over = links.start(mine_x, mine_x, to_across)
            self.beside = links.start(mine_x, mine_x, to_mate)

        def forward(self):
            self.over.wait_recv()
            theirs = self.buf.at[across, halves[self.x]]
            self.last = links.start(theirs, theirs, to_mate)

    xs[me] = x_ref[...]
    x_a, x_b = gather_start(xs)

    if ring_on:
        shard = w1g.shape[1]
        mine = ring.at(0)
        own_f[...] = jnp.zeros(own_f.shape, f32)
        tiles = []
        for i, name in enumerate(IN_RING[:4]):
            r0, c0 = 128 * (i // 2), 256 * (i % 2)
            own_f[r0 : r0 + shard, c0 : c0 + r[name].shape[1]] = r[name][...].astype(f32)
            tiles.append((own_f[r0 : r0 + shard, c0 : c0 + 128], own_f[r0 : r0 + shard, c0 + 128 : c0 + 256]))
        (qx, qy), (kx, ky), (vx, vy), (px, py) = tiles
        low = lane_of(shard) < 64
        joined = [
            jnp.where(low, kx, swap(vx)),
            jnp.where(low, swap(kx), vx),
            jnp.where(low, ky, swap(vy)),
            qx,
            jnp.where(low, qy, swap(px)),
            jnp.where(low, swap(px), swap(py)),
        ]
        for i, tile in enumerate(joined):
            w1g[mine, :, 128 * i : 128 * i + 128] = tile.astype(bf16)
        spread_1 = Spread(links, ring, [w1g])
        spread_1.begin()
        wo_ref = r["wo_ref"]
        own_f[:, :128] = jnp.zeros((256, 128), f32)
        own_f[: wo_ref.shape[0], :shard] = wo_ref[...].astype(f32)
        wog[mine] = jnp.transpose(own_f[:, :128], (1, 0))[:shard].astype(bf16)
        wig[mine] = r["wi_ref"][...]
        wug[mine] = r["wu_ref"][...]
        spread_o, spread_i, spread_u = (Spread(links, ring, [ref]) for ref in (wog, wig, wug))

    small_ref[...] = jnp.zeros(small_ref.shape, f32)
    for h in range(heads):
        for i, ref in enumerate((cb_ref, pb_ref, tbias_ref)):
            small_ref[h, i : i + 1, 0:64] = ref[h : h + 1, :]
        small_ref[h, 3:5, 0:64] = te_ref[h]
        small_ref[h, 5:6, 0:64] = vb_ref[h : h + 1, :]
    for i, ref in enumerate((ab_ref, ag_ref, as_ref, fb_ref, fg_ref, fs_ref)):
        ln_ref[i : i + 1, :] = ref[...].reshape(1, width)
    ibs[0:1, :] = ib_ref[...].reshape(1, hidden)

    slots = seq // DOC_LEAST + 2
    ends = (doc_ref[...].reshape(1, seq) - lax.axis_index("dp") * seq).astype(f32)
    slot = jnp.where(ends > seq - 1.5, slots - 1.0, jnp.floor((ends + 0.5) * (1.0 / DOC_LEAST)))
    slot = jnp.transpose(jnp.broadcast_to(slot, (128, seq)), (1, 0))
    kind = jnp.transpose(jnp.broadcast_to(kind_ref[...].reshape(1, seq).astype(f32), (128, seq)), (1, 0))
    lane = lane_of(seq)
    hit = jnp.abs(slot + 68.0 - lane.astype(f32)) < 0.5
    qmeta_ref[...] = jnp.where(lane == 64, kind, jnp.where(hit, 1.0, 0.0)).astype(bf16)
    miss = jnp.where(hit, 0.0, MASK)
    kmeta_ref[...] = jnp.where(
        lane < 66, 1.0, jnp.where(lane < 68, kind, jnp.where(lane < 68 + slots, miss, 0.0))
    ).astype(bf16)
    x_f = gather_forward(xs, x_a)
    if ring_on:
        spread_1.step()

    steps = tb_ref.shape[1]

    def table_step(u, carry):
        sa = ta_ref[0, pl.ds(u, 1), :]
        ca = ta_ref[1, pl.ds(u, 1), :]
        at = pl.multiple_of(u * steps, steps)
        table[pl.ds(at, steps), :half] = (sa * tb_ref[1] - ca * tb_ref[0]).astype(bf16)
        table[pl.ds(at, steps), half:] = (ca * tb_ref[1] + sa * tb_ref[0]).astype(bf16)
        return carry

    lax.fori_loop(0, ta_ref.shape[1] // 2, table_step, 0)
    if ring_on:
        spread_1.step()
    lax.fori_loop(ta_ref.shape[1] // 2, ta_ref.shape[1], table_step, 0)

    ri = lax.broadcasted_iota(jnp.int32, (rows, rows), 0)
    ci = lax.broadcasted_iota(jnp.int32, (rows, rows), 1)
    flip[...] = jnp.where(ri + ci == rows - 1, 1.0, 0.0).astype(bf16)
    if ring_on:
        spread_1.step()
        spread_o.begin()
        spread_1.finish()

    def rel_step(i, carry):
        at = pl.ds(pl.multiple_of(i * 256, 256), 256)
        got = mm(table[at, :], w1g[:, :, 512:768].reshape(width, 256), NN)
        rel[0, at, :] = low_half(swap(got[:, :128])).astype(bf16)
        rel[1, at, :] = low_half(got[:, 128:]).astype(bf16)
        rel[2, at, :] = low_half(swap(got[:, 128:])).astype(bf16)
        return carry

    lax.fori_loop(0, 2 * seq // 256, rel_step, 0)

    def project(o, carry):
        at = pl.ds(pl.multiple_of(o * rows, rows), rows)
        got = mm(xs[o], w1g[:, :, :640].reshape(width, 640), NN)
        lane = lane_of(rows)
        qmeta = qmeta_ref[at, :].astype(f32)
        kmeta = kmeta_ref[at, :].astype(f32)
        typed = qmeta[:, 64:65]
        for h in range(heads):
            kv = got[:, 128 * h : 128 * h + 128]
            ka[h, at, :] = jnp.where(lane < 64, kv, kmeta).astype(bf16)
            vrow = swap(kv) + small_ref[h, 5:6, :]
            va[h, at, :] = jnp.where(lane < 64, vrow, jnp.where(lane < 66, 1.0, 0.0)).astype(bf16)
            q = got[:, 384:512] if h < 2 else got[:, 512:640]
            if h == 1:
                q = swap(q)
            q = low_half(q)
            q32[h, at, :] = q
            qt = q + small_ref[h, 2:3, :]
            ct0 = jnp.sum(qt * small_ref[h, 3:4, :], axis=1, keepdims=True)
            ct1 = jnp.sum(qt * small_ref[h, 4:5, :], axis=1, keepdims=True)
            diff = (ct1 - ct0) * scale
            base = ct0 * scale + diff * (1.0 - typed)
            tilt = diff * (2.0 * typed - 1.0)
            base_hi = base.astype(bf16).astype(f32)
            tilt_hi = tilt.astype(bf16).astype(f32)
            extra = jnp.where(
                lane == 64,
                base_hi,
                jnp.where(
                    lane == 65,
                    base - base_hi,
                    jnp.where(lane == 66, tilt_hi, jnp.where(lane == 67, tilt - tilt_hi, qmeta)),
                ),
            )
            qc = (q + small_ref[h, 0:1, :]) * scale
            qa[h, at, :] = jnp.where(lane < 64, qc, extra).astype(bf16)
            qr[h, at, :] = low_half((q + small_ref[h, 1:2, :]) * scale).astype(bf16)
        return carry

    def poll(*steppers):
        for stepper in steppers:
            stepper.step()

    if ring_on:
        spread_o.step()
        spread_i.begin()
    x_b.wait_recv()
    x_f.wait_recv()
    lax.fori_loop(0, members, project, 0)
    if ring_on:
        poll(spread_o)
        spread_u.begin()

    wide = seq + rows

    def hooked(hooks, h):
        for when, hook in (hooks or {}).items():
            pl.when(h == when)(hook)

    def attend(o, hooks=None):
        at = pl.ds(pl.multiple_of(o * rows, rows), rows)
        window = pl.ds(pl.multiple_of((members - 1 - o) * rows, rows), wide)

        def one_head(h, carry):
            hooked(hooks, h)
            s = mm(qa[h, at, :], ka[h], NT)
            g = mm(qr[h, at, :], rel[h, window, :], NT)
            g = pltpu.roll(g, wide + 1 - rows, 1, stride=1, stride_axis=0)
            s = s + g[:, :seq]
            top = jnp.max(s, axis=1, keepdims=True)
            e = jnp.exp(s - top).astype(bf16)
            es[h, at, :] = e
            o_full = mm(e, va[h], NN)
            inv = 1.0 / o_full[:, 64:65]
            a32[h, at, :] = jnp.where(lane_of(rows) < 64, o_full * inv, inv)
            return carry

        lax.fori_loop(0, heads, one_head, 0)
        first = low_half(a32[0, at, :]) + swap(low_half(a32[1, at, :]))
        attnp[at, :128] = first.astype(bf16)
        attnp[at, 128:] = low_half(a32[2, at, :]).astype(bf16)

    def branch_of(o):
        return mm(attnp[pl.ds(pl.multiple_of(o * rows, rows), rows), :], whole(wog), NT)

    class Scatter:
        def __init__(self, part, r1, r2, sx):
            self.part, self.r1, self.r2, self.sx = part, r1, r2, sx
            self.far, self.near, self.over = [None, None], [None, None], [None, None]

        def give_diag(self, x, value):
            self.part[diag, halves[x]] = value.astype(bf16)
            self.far[x] = links.start(self.part.at[diag, halves[x]], self.r1.at[1 - side, halves[x]], to_mate)

        def give_across(self, x, value):
            self.part[across, halves[x]] = value.astype(bf16)

        def give_mate(self, x, value):
            self.part[mate, halves[x]] = value.astype(bf16)
            self.near[x] = links.start(self.part.at[mate, halves[x]], self.r1.at[side, halves[x]], to_mate)

        def give_own(self, x, value):
            own_f[halves[x]] = value

        def give_near(self, x, pair):
            self.give_mate(x, jnp.where(core == 0, pair[1], pair[0]))
            self.give_own(x, jnp.where(core == 0, pair[0], pair[1]))

        def give_far(self, x, pair):
            self.give_diag(x, jnp.where(core == 0, pair[1], pair[0]))
            self.give_across(x, jnp.where(core == 0, pair[0], pair[1]))

        def pass_on(self, x):
            self.far[x].wait_recv()
            both = self.part[across, halves[x]].astype(f32) + self.r1[1 - side, halves[x]].astype(f32)
            self.sx[halves[x]] = both.astype(bf16)
            self.over[x] = links.start(
                functools.partial(part_of, self.sx, halves[x]), functools.partial(part_of, self.r2, halves[x]), to_across
            )

        def release(self):
            links.drain(self.far + self.near + self.over)

        def take(self, x):
            self.near[x].wait_recv()
            near = own_f[halves[x]] + self.r1[side, halves[x]].astype(f32)
            self.over[x].wait_recv()
            return near + self.r2[halves[x]].astype(f32)

    def split(value):
        return value[:part_rows], value[part_rows:]

    first_red = red = Scatter(part_a, r1a, r2a, sxa)

    def first_pass():
        red.pass_on(0)
        red.pass_on(1)

    def polls(**at):
        return {int(when[1:]): functools.partial(poll, *steppers) for when, steppers in at.items()}

    attend(diag, polls(h2=(spread_o, spread_i)) if ring_on else None)
    attend(across, polls(h1=(spread_u,), h2=(spread_o,)) if ring_on else None)
    if ring_on:
        spread_o.finish()
        poll(spread_i)
    for x, (there, here) in enumerate(zip(split(branch_of(diag)), split(branch_of(across)))):
        red.give_diag(x, there)
        red.give_across(x, here)
    attend(mate, {1: first_pass} | (polls(h2=(spread_u,)) if ring_on else {}))
    for x, value in enumerate(split(branch_of(mate))):
        red.give_mate(x, value)
    if ring_on:
        poll(spread_i)
    attend(me, polls(h2=(spread_u,)) if ring_on else None)
    for x, value in enumerate(split(branch_of(me))):
        red.give_own(x, value)
    vec_ref[...] = jnp.zeros((8, width), f32)
    hs_ref[...] = jnp.zeros(hs_ref.shape, f32)

    def first_norm(x):
        at = halves[x]
        summed = x_ref[at, :].astype(f32) + first_red.take(x) + ln_ref[0:1, :]
        normed, inv_std = norm_stats(summed)
        n1[at, :] = normed
        inv1[at, :] = jnp.broadcast_to(inv_std, (part_rows, 128))
        h1[at, :] = normed * ln_ref[1:2, :] + ln_ref[2:3, :]
        hb[me, at] = h1[at, :].astype(bf16)
        return Gather(hb, x)

    def ffn(pair, x):
        inner = mm(hb[pair, halves[x]].reshape(rows, width), whole(wig), NN) + ibs[0:1, :]
        square = inner * inner
        t = jnp.tanh(0.7978845608028654 * (inner + 0.044715 * square * inner))
        made = (0.5 * inner * (1.0 + t)).astype(bf16)
        act[pair, halves[x]] = made.reshape(2, part_rows, hidden)
        steep = (
            0.5 * (1.0 + t)
            + 0.5 * inner * (1.0 - t * t) * 0.7978845608028654 * (1.0 + 3.0 * 0.044715 * square)
        ).astype(bf16)
        slope[pair, halves[x]] = steep.reshape(2, part_rows, hidden)
        return mm(made, whole(wug), NT).reshape(2, part_rows, width)

    def stage(start, block, reducer, ready=None):
        moves = [start(0), start(1)]
        if ready:
            ready()
        for x in (0, 1):
            moves[x].beside.wait_recv()
            reducer.give_near(x, block(near_pair, x))
        moves[0].forward()
        moves[0].last.wait_recv()
        reducer.give_far(0, block(far_pair, 0))
        moves[1].forward()
        reducer.pass_on(0)
        moves[1].last.wait_recv()
        reducer.give_far(1, block(far_pair, 1))
        reducer.pass_on(1)

    def weights_ready():
        spread_i.finish()
        spread_u.finish()

    second_red = red = Scatter(part_b, r1b, r2b, sxb)
    stage(first_norm, ffn, second_red, weights_ready if ring_on else None)

    def second_norm(x):
        at = halves[x]
        summed = h1[at, :] + second_red.take(x) + ln_ref[3:4, :]
        normed, inv_std = norm_stats(summed)
        out_ref[at, :] = (normed * ln_ref[4:5, :] + ln_ref[5:6, :]).astype(bf16)
        grad = og_ref[at, :].astype(f32)
        back = norm_back(grad, normed, inv_std, ln_ref[4:5, :])
        e2[at, :] = back
        eb2[me, at] = back.astype(bf16)
        move = Gather(eb2, x)
        vec_ref[4:5, :] += col_sum(grad * normed)
        vec_ref[5:6, :] += col_sum(grad)
        vec_ref[1:2, :] += col_sum(back)
        return move

    def ffn_back(pair, x):
        steep = slope[pair, halves[x]].reshape(rows, hidden).astype(f32)
        grad_inner = (mm(eb2[pair, halves[x]].reshape(rows, width), whole(wug), NN) * steep).astype(bf16)
        igr[pair, halves[x]] = grad_inner.reshape(2, part_rows, hidden)
        vec_ref[6:7, :hidden] += col_sum(grad_inner.astype(f32))
        return mm(grad_inner, whole(wig), NT).reshape(2, part_rows, width)

    third_red = Scatter(part_a, r1a, r2a, sxa)
    stage(second_norm, ffn_back, third_red, first_red.release)
    flat = lambda ref: ref[...].reshape(seq, ref.shape[2])

    def put(ref, value):
        ref[...] = value.astype(bf16).reshape(ref.shape)

    def third_norm(x):
        at = halves[x]
        grad = e2[at, :] + third_red.take(x)
        back = norm_back(grad, n1[at, :], inv1[at, :1], ln_ref[1:2, :])
        e1[at, :] = back
        eb1[me, at] = back.astype(bf16)
        move = Gather(eb1, x)
        vec_ref[2:3, :] += col_sum(grad * n1[at, :])
        vec_ref[3:4, :] += col_sum(grad)
        vec_ref[0:1, :] += col_sum(back)
        return move

    put(dwu, mm(flat(eb2), flat(act), TN))
    if ring_on:
        collect_u = Collect(links, ring, [dwu], [r["gwu"]])
        collect_u.begin()
    g_0 = third_norm(0)
    put(dwi, mm(flat(hb), flat(igr), TN))
    if ring_on:
        collect_i = Collect(links, ring, [dwi], [r["gwi"]])
        collect_i.begin()
    g_1 = third_norm(1)
    if ring_on:
        vec_all, vec_mp = r["vec_all"], r["vec_mp"]
        vec_all[mine] = vec_ref[...]
        spread_4 = Spread(links, ring, [vec_all])
        spread_4.begin()

    dkv[...] = jnp.zeros(dkv.shape, f32)
    drt[...] = jnp.zeros(drt.shape, f32)

    def attend_back(o, hooks=None):
        at = pl.ds(pl.multiple_of(o * rows, rows), rows)
        lo = pl.multiple_of((members - 1 - o) * rows, rows)
        window = pl.ds(lo, wide)
        d_all = mm(eb1[o], whole(wog), NN).astype(bf16).astype(f32)
        lane = lane_of(rows)
        typed = qmeta_ref[at, :].astype(f32)[:, 64:65]
        per_head[0] = d_all[:, :128]
        per_head[1] = swap(d_all[:, :128])
        per_head[2] = d_all[:, 128:]

        def one_head(h, carry):
            hooked(hooks, h)
            d_out = per_head[h]
            kept = a32[h, at, :]
            d_out = low_half(d_out * kept[:, 64:65]).astype(bf16).astype(f32)
            d_row = -jnp.sum(d_out * kept, axis=1, keepdims=True)
            d_hi = d_row.astype(bf16).astype(f32)
            d_aug = jnp.where(lane == 64, d_hi, jnp.where(lane == 65, d_row - d_hi, d_out)).astype(bf16)
            e = es[h, at, :]
            ds = (e.astype(f32) * mm(d_aug, va[h], NT)).astype(bf16)
            dkv[h, 64:128, :] += mm(d_aug, e, TN)[:64]
            dkv[h, 0:64, :] += mm(qa[h, at, :], ds, TN)[:64]
            dq = mm(ds, ka[h], NN) * scale
            turned = mm(flip[...], ds, NN)
            turned = jnp.concatenate([turned, jnp.zeros((rows, rows), f32)], axis=1)
            dg = pltpu.roll(turned, 0, 1, stride=1, stride_axis=0).astype(bf16)
            dqr = mm(dg, rel[h, window, :], NN) * scale
            qr_turned = mm(flip[...], qr[h, at, :], NN).astype(bf16)
            drt[pl.ds(pl.multiple_of(64 * h + 64, 64), 64), window] += mm(qr_turned, dg, TN)[:64]
            hs_ref[h, 1:2, :] += col_sum(dqr)
            dqr_hi = dqr.astype(bf16)
            dqr_lo = (dqr - dqr_hi.astype(f32)).astype(bf16)
            dqr = mm(flip[...], dqr_hi, NN) + mm(flip[...], dqr_lo, NN)
            total = dq[:, 64:65]
            ones = dq[:, 66:67]
            same = jnp.where(typed > 0.5, ones, total - ones)
            other = total - same
            dqt = other * small_ref[h, 3:4, :] + same * small_ref[h, 4:5, :]
            qt = q32[h, at, :] + small_ref[h, 2:3, :]
            hs_ref[h, 0:1, :] += col_sum(dq)
            hs_ref[h, 2:3, :] += col_sum(dqt)
            hs_ref[h, 3:4, :] += col_sum(other * qt)
            hs_ref[h, 4:5, :] += col_sum(same * qt)
            per_head[h] = low_half(dq + dqr + dqt)
            return carry

        lax.fori_loop(0, heads, one_head, 0)
        dqkv[at, 384:512] = (per_head[0] + swap(per_head[1])).astype(bf16)
        dqkv[at, 512:640] = per_head[2].astype(bf16)

    attend_back(me, polls(h2=(collect_u,)) if ring_on else None)
    g_0.beside.wait_recv()
    g_1.beside.wait_recv()
    g_0.forward()
    g_1.forward()
    if ring_on:
        poll(spread_4, collect_i)
    attend_back(mate, polls(h1=(spread_4,), h2=(collect_u,)) if ring_on else None)
    if ring_on:
        poll(spread_4, collect_i)
    attend_back(across, polls(h1=(collect_u,), h2=(collect_i,)) if ring_on else None)
    g_0.last.wait_recv()
    g_1.last.wait_recv()
    put(dwo, mm(flat(eb1), attnp[...], TN))
    if ring_on:
        spread_4.finish()
        total = vec_all[0]
        for i in range(1, ring.count):
            total = total + vec_all[i]
        vec_mp[me] = total
        v_a, v_b = gather_start(vec_mp)
        collect_2 = Collect(links, ring, [dwo], [r["gwo"]])
        collect_2.begin()
    attend_back(diag, polls(h2=(collect_2,)) if ring_on else None)
    if ring_on:
        poll(collect_2)
        v_b.wait_recv()
        v_f = gather_forward(vec_mp, v_a)

    for h in range(heads):
        turned = jnp.transpose(dkv[h], (1, 0)).astype(bf16)
        dqkv[:, 128 * h : 128 * h + 128] = turned
        hs_ref[h, 5:6, :] = swap(col_sum(turned.astype(f32)))
    put(dwa, mm(flat(xs), dqkv[:, :512], TN))
    if ring_on:
        hs_all = r["hs_all"]
        hs_all[mine] = hs_ref[...].reshape(8 * heads, 128)
        spread_5 = Spread(links, ring, [hs_all])
        spread_5.begin()
        collect_3 = Collect(links, ring, [dwa], [r["gwa"]])
        collect_3.begin()

    def input_back(o):
        at = pl.ds(pl.multiple_of(o * rows, rows), rows)
        return mm(dqkv[at, :], w1g[:, :, :640].reshape(width, 640), NT)

    second_red.release()
    red = Scatter(part_b, r1b, r2b, sxb)
    for x, value in enumerate(split(input_back(diag))):
        red.give_diag(x, value)
    for x, value in enumerate(split(input_back(across))):
        red.give_across(x, value)
    tail = mm(flat(xs), dqkv[:, 512:640], TN)
    d_pos = jnp.transpose(mm(drt[...].astype(bf16), table[...], NN), (1, 0))
    put(dwb, jnp.concatenate([tail + d_pos[:, :128], d_pos[:, 128:]], axis=1))
    if ring_on:
        collect_4 = Collect(links, ring, [dwb], [r["gwb"]])
        collect_4.begin()
    red.pass_on(0)
    red.pass_on(1)
    if ring_on:
        poll(collect_2, collect_3, spread_5)
    for x, value in enumerate(split(input_back(mate))):
        red.give_mate(x, value)
    for x, value in enumerate(split(input_back(me))):
        red.give_own(x, value)
    if ring_on:
        grad_ref = r["grad_ref"]
        poll(collect_4, collect_3, spread_5)
        collect_u.finish()
        collect_i.finish()
        collect_u.take(0, grad_ref, pl.ds(1024 + hidden, hidden))
        poll(collect_2)
        collect_i.take(0, grad_ref, pl.ds(1024, hidden))
        poll(collect_4, collect_3, spread_5)
        v_f.wait_recv()
        r["vec_ref"][...] = vec_mp[0] + vec_mp[1] + vec_mp[2] + vec_mp[3]
        r["vec_ref"][6:7, :] = vec_mp[me][6:7, :]
        collect_2.finish()
        collect_2.take(0, grad_ref, pl.ds(768, 256))
        poll(collect_4, collect_3, spread_5)
    for x in (0, 1):
        ig_ref[halves[x], :] = (e1[halves[x], :] + red.take(x)).astype(bf16)
    if ring_on:
        spread_5.finish()
        total = hs_all[0]
        for i in range(1, ring.count):
            total = total + hs_all[i]
        r["hs_ref"][...] = total
        collect_3.finish()
        collect_3.take(0, grad_ref, pl.ds(0, 512))
        collect_4.finish()
        collect_4.take(0, grad_ref, pl.ds(512, 256))
    else:
        r["vec_ref"][...] = vec_ref[...]
        r["hs_ref"][...] = hs_ref[...].reshape(8 * heads, 128)
    links.drain()


SCRATCH = (
    "xs", "hb", "eb2", "eb1", "part_a", "part_b", "r1a", "r1b", "r2a", "r2b", "sxa", "sxb", "own_f", "table", "rel",
    "qa", "qr", "ka", "va", "q32", "es", "a32", "attnp", "act", "slope", "igr", "h1", "n1", "e2", "inv1", "e1", "dkv",
    "drt", "dqkv", "flip", "qmeta", "kmeta", "small", "per_head", "ln", "ibs", "send_sems", "recv_sems",
)


def finish_kernel(
    out_ref, ig_ref, grad_ref, vec_ref, hs_ref,
    out, in_grad, wq, wk, wv, wp, wo, wi, wu, cb, pb, tbias, vb, te, ib, ab, fb, ag, ash, fg, fs, turn,
):
    out[...] = out_ref[...]
    in_grad[...] = ig_ref[...]
    shard, hidden = wi.shape
    t = [grad_ref[:, 128 * i : 128 * i + 128].astype(f32) for i in range(6)]
    low = lane_of(shard) < 64
    wk[:, :128] = jnp.where(low, t[0], swap(t[1]))
    wk[:, 128:] = t[2][:, :64]
    wv[:, :128] = jnp.where(low, swap(t[0]), t[1])
    wv[:, 128:] = swap(t[2])[:, :64]
    wq[:, :128] = t[3]
    wq[:, 128:] = t[4][:, :64]
    wp[:, :128] = jnp.where(low, swap(t[4]), swap(t[5]))
    wp[:, 128:] = swap(t[5])[:, :64]
    turn[...] = jnp.zeros(turn.shape, f32)
    turn[:shard, :] = grad_ref[:, 768:1024].astype(f32)
    wo[...] = jnp.transpose(turn[...], (1, 0))[: wo.shape[0], :shard]
    wi[...] = grad_ref[:, 1024 : 1024 + hidden].astype(f32)
    wu[...] = grad_ref[:, 1024 + hidden :].astype(f32)
    for h in range(cb.shape[0]):
        for i, ref in ((0, cb), (1, pb), (2, tbias), (5, vb)):
            ref[h : h + 1, :] = hs_ref[8 * h + i : 8 * h + i + 1, :64]
        te[h] = hs_ref[8 * h + 3 : 8 * h + 5, :64]
    ib[...] = vec_ref[6:7, :hidden].reshape(hidden)
    for i, ref in enumerate((ab, fb, ag, ash, fg, fs)):
        ref[...] = vec_ref[i : i + 1, :].reshape(ref.shape[0])


def angle_tables(seq, width):
    half = width // 2
    freq = 1.0 / 10000.0 ** (np.arange(half, dtype=np.float64) * (2.0 / width))
    steps = 32
    coarse = (seq - 1 - steps * np.arange(2 * seq // steps, dtype=np.float64))[:, None] * freq[None, :]
    fine = np.arange(steps, dtype=np.float64)[:, None] * freq[None, :]
    return (
        np.stack([np.sin(coarse), np.cos(coarse)]).astype(np.float32),
        np.stack([np.sin(fine), np.cos(fine)]).astype(np.float32),
    )


def per_device(
    layer_input, doc_ids, type_ids, positions, query_weight, key_weight, value_weight, pos_kernel,
    out_weight, inner_weight, outer_weight, content_bias, pos_bias, type_bias, value_bias, type_embed,
    inner_bias, attn_bias, ffn_bias, attn_gain, attn_shift, ffn_gain, ffn_shift, out_grad,
):
    rows, width = layer_input.shape
    seq = doc_ids.shape[0]
    heads, depth = content_bias.shape
    hidden = inner_weight.shape[1]
    shard = query_weight.shape[0]
    members = seq // rows
    count = width // shard
    cols = heads * depth
    ring_on = shard % 16 == 0 and count % 2 == 0 and count > 2

    type_rows = jnp.transpose(type_embed, (1, 0, 2))
    ta, tb = angle_tables(seq, width)
    given = [
        layer_input, out_grad, doc_ids, type_ids, content_bias, pos_bias, type_bias, value_bias, type_rows, inner_bias,
        attn_bias, ffn_bias, attn_gain, attn_shift, ffn_gain, ffn_shift, ta, tb,
    ]
    sds = jax.ShapeDtypeStruct
    vm = pltpu.VMEM
    blocks = count if ring_on else 1
    deep = width // blocks
    full = {
        "w1g": 768, "wog": 256, "wig": hidden, "wug": hidden,
        "dwa": 512, "dwb": 256, "dwo": 256, "dwi": hidden, "dwu": hidden,
    }
    outs = {
        "out_ref": sds((rows, width), bf16), "ig_ref": sds((rows, width), bf16),
        "vec_ref": sds((8, width), f32), "hs_ref": sds((8 * heads, 128), f32),
    }
    extra = {"vec": vm((8, width), f32), "hs": vm((heads, 8, 128), f32)}
    if ring_on:
        given += [query_weight, key_weight, value_weight, pos_kernel, out_weight, inner_weight, outer_weight.T]
        names = IN_BOTH + IN_RING
        outs["grad_ref"] = sds((shard, 1024 + 2 * hidden), f32)
        extra |= {name: vm((blocks, deep, wide), bf16) for name, wide in full.items()}
        for name in OUT_WHOLE:
            extra["g" + name[1:]] = vm((blocks - 1, deep, full[name]), bf16)
        extra["vec_all"] = vm((blocks, 8, width), f32)
        extra["vec_mp"] = vm((members, 8, width), f32)
        extra["hs_all"] = vm((blocks, 8 * heads, 128), f32)
    else:
        q3, k3, v3 = (w.reshape(shard, heads, depth) for w in (query_weight, key_weight, value_weight))
        kv = jnp.stack([k3, v3], axis=2).reshape(shard, 2 * cols)
        out_t = jnp.pad(out_weight.T, ((0, 0), (0, 256 - cols)))
        mine = jnp.concatenate([kv, query_weight, pos_kernel, out_t, inner_weight, outer_weight.T], axis=1)
        gathered = lax.all_gather(mine, "dp", axis=0, tiled=True)[None]
        bounds = np.cumsum([0] + [full[name] for name in IN_WHOLE])
        given += [gathered[:, :, lo:hi] for lo, hi in zip(bounds[:-1], bounds[1:])]
        names = IN_BOTH + IN_WHOLE
        outs |= {name: sds((1, width, full[name]), bf16) for name in OUT_WHOLE}

    block = (members, rows, width)
    per_head = (heads, seq, 128)
    scratch = {
        "xs": vm(block, bf16), "hb": vm(block, bf16), "eb2": vm(block, bf16), "eb1": vm(block, bf16),
        "part_a": vm(block, bf16), "part_b": vm(block, bf16),
        "r1a": vm((2, rows, width), bf16), "r1b": vm((2, rows, width), bf16),
        "r2a": vm((rows, width), bf16), "r2b": vm((rows, width), bf16),
        "sxa": vm((rows, width), bf16), "sxb": vm((rows, width), bf16),
        "own_f": vm((rows, width), f32), "table": vm((2 * seq, width), bf16), "rel": vm((heads, 2 * seq, 128), bf16),
        "qa": vm(per_head, bf16), "qr": vm(per_head, bf16), "ka": vm(per_head, bf16), "va": vm(per_head, bf16),
        "q32": vm(per_head, f32), "es": vm((heads, seq, seq), bf16), "a32": vm(per_head, f32),
        "attnp": vm((seq, 256), bf16), "act": vm((members, rows, hidden), bf16),
        "slope": vm((members, rows, hidden), bf16), "igr": vm((members, rows, hidden), bf16),
        "h1": vm((rows, width), f32), "n1": vm((rows, width), f32), "e2": vm((rows, width), f32),
        "inv1": vm((rows, 128), f32), "e1": vm((rows, width), f32), "dkv": vm((heads, 128, seq), f32),
        "drt": vm((256, 2 * seq), f32), "dqkv": vm((seq, 640), bf16), "flip": vm((rows, rows), bf16),
        "qmeta": vm((seq, 128), bf16), "kmeta": vm((seq, 128), bf16), "small": vm((heads, 8, 128), f32), "per_head": vm((heads, rows, 128), f32),
        "ln": vm((8, width), f32), "ibs": vm((8, hidden), f32),
        "send_sems": pltpu.SemaphoreType.DMA((192,)), "recv_sems": pltpu.SemaphoreType.DMA((192,)),
    }
    scratch |= extra
    inside = pl.BlockSpec(memory_space=pltpu.VMEM)
    made = pl.pallas_call(
        functools.partial(layer_kernel, ring_on, [*names, *outs, *scratch]),
        out_shape=list(outs.values()),
        in_specs=[inside] * len(given),
        out_specs=[inside] * len(outs),
        scratch_shapes=list(scratch.values()),
        compiler_params=pltpu.CompilerParams(collective_id=0, has_side_effects=True, vmem_limit_bytes=67043328),
        name="layer",
    )(*given)
    made = dict(zip(outs, made))

    if ring_on:
        grads, vec, hs = made["grad_ref"], made["vec_ref"], made["hs_ref"]
    else:
        grads = jnp.concatenate([made[name][0] for name in ("dwa", "dwb", "dwo", "dwi", "dwu")], axis=1)
        grads = lax.psum_scatter(grads, "dp", scatter_dimension=0, tiled=True).astype(f32)
        vec, hs = lax.psum((made["vec_ref"], made["hs_ref"]), "dp")
        vec = jnp.concatenate([lax.psum(vec[:6], "mp"), vec[6:]], axis=0)
    small = sds((heads, depth), f32)
    line = sds((width,), f32)
    results = pl.pallas_call(
        finish_kernel,
        out_shape=[
            made["out_ref"], made["ig_ref"], *[sds((shard, cols), f32)] * 4, sds((cols, shard), f32),
            sds((shard, hidden), f32), sds((shard, hidden), f32), *[small] * 4, sds((heads, 2, depth), f32),
            sds((hidden,), f32), *[line] * 6,
        ],
        in_specs=[inside] * 5,
        out_specs=[inside] * 21,
        scratch_shapes=[vm((128, 256), f32)],
        name="finish",
    )(made["out_ref"], made["ig_ref"], grads, vec, hs)
    results = list(results)
    results[8] = results[8].T
    results[13] = jnp.transpose(results[13], (1, 0, 2))
    return tuple(results)


def solution(mesh):
    rows = P(("dp", "mp"), None)
    token = P("dp")
    placed = (
        (rows, token, token, token)
        + (P("dp", "mp"),) * 4
        + (P("mp", "dp"), P("dp", "mp"), P("mp", "dp"))
        + (P("mp", None),) * 4
        + (P(None, "mp", None), P("mp"))
        + (P(),) * 6
        + (rows,)
    )
    given = (
        (rows, rows)
        + (P("dp", "mp"),) * 4
        + (P("mp", "dp"), P("dp", "mp"), P("mp", "dp"))
        + (P("mp", None),) * 4
        + (P(None, "mp", None), P("mp"))
        + (P(),) * 6
    )
    return jax.shard_map(per_device, mesh=mesh, in_specs=placed, out_specs=given, check_vma=False)
```

```python
import functools
import math

import jax
import jax.numpy as jnp
import numpy as np
from jax import lax
from jax.experimental import pallas as pl
from jax.experimental.pallas import tpu as pltpu
from jax.sharding import PartitionSpec as P

f32 = jnp.float32
bf16 = jnp.bfloat16
MESH = pl.DeviceIdType.MESH
MASK = -1e30
DOC_LEAST = 60
NN = (((1,), (0,)), ((), ()))
NT = (((1,), (1,)), ((), ()))
TN = (((0,), (0,)), ((), ()))


def mm(a, b, dims):
    return lax.dot_general(a, b, dims, preferred_element_type=f32)


def lane_of(rows):
    return lax.broadcasted_iota(jnp.int32, (rows, 128), 1)


def low_half(value):
    return jnp.where(lane_of(value.shape[0]) < 64, value, 0.0)


def swap(value):
    return pltpu.roll(value, 64, 1)


class Move:
    def __init__(self, src, dst, send_sem, recv_sem, where):
        self.src, self.dst, self.where = src, dst, where
        self.send_sem, self.recv_sem = send_sem, recv_sem

    def described(self):
        return pltpu.make_async_remote_copy(
            src_ref=self.src() if callable(self.src) else self.src,
            dst_ref=self.dst() if callable(self.dst) else self.dst,
            send_sem=self.send_sem(),
            recv_sem=self.recv_sem(),
            device_id=self.where,
            device_id_type=MESH,
        )

    def start(self):
        self.described().start()

    def wait_send(self):
        self.described().wait_send()

    def wait_recv(self):
        self.described().wait_recv()


class Links:
    def __init__(self, send_sems, recv_sems):
        self.send_sems = send_sems
        self.recv_sems = recv_sems
        self.used = 0
        self.sent = []

    def start(self, src, dst, where):
        used = self.used
        copy = Move(src, dst, lambda: self.send_sems.at[used], lambda: self.recv_sems.at[used], where)
        self.used += 1
        self.sent.append(copy)
        copy.start()
        return copy

    def drain(self, some=None):
        for copy in some or self.sent:
            copy.wait_send()
            self.sent = [other for other in self.sent if other is not copy]


def norm_stats(summed):
    center = summed - jnp.mean(summed, axis=-1, keepdims=True)
    spread = jnp.mean(center * center, axis=-1, keepdims=True)
    inv_std = lax.rsqrt(spread + 1e-06)
    return center * inv_std, inv_std


def norm_back(grad, normed, inv_std, gain):
    scaled = grad * gain
    return inv_std * (
        scaled
        - jnp.mean(scaled, axis=-1, keepdims=True)
        - normed * jnp.mean(scaled * normed, axis=-1, keepdims=True)
    )


def col_sum(value):
    return jnp.sum(value, axis=0, keepdims=True)


class Ring:
    def __init__(self, count):
        mine = lax.axis_index("dp")
        row = lax.rem(mine, 2)
        along = lax.div(mine, 2)
        self.count = count
        self.place = (1 - row) * along + row * (count - 1 - along)
        self.places = {offset: self.find(offset) for offset in range(-(count // 2), count // 2 + 1)}

    def at(self, offset):
        return self.places[offset]

    def find(self, offset):
        place = lax.rem(self.place + (offset + self.count), self.count)
        back = lax.div(place, self.count // 2)
        return (1 - back) * 2 * place + back * (2 * (self.count - 1 - place) + 1)


class Flow:
    def __init__(self, sign, hops, rows, slot):
        self.sign, self.hops, self.rows, self.slot = sign, hops, rows, slot


def flows_of(count, rows):
    near = count // 2 - 1
    if rows % 32:
        return [Flow(1, near + 1, pl.ds(0, rows), 0), Flow(-1, near, pl.ds(0, rows), near + 1)]
    first, second = pl.ds(0, rows // 2), pl.ds(rows // 2, rows // 2)
    return [
        Flow(1, near + 1, first, 0),
        Flow(-1, near + 1, second, near),
        Flow(-1, near, first, near + 1),
        Flow(1, near, second, 0),
    ]


def part_of(ref, *index):
    return ref.at[index]


class Spread:
    def __init__(self, links, ring, bufs):
        self.links, self.ring, self.bufs = links, ring, bufs
        self.done = 0
        self.last = max(f.hops for f in flows_of(ring.count, bufs[0].shape[1]))
        self.moves = {}

    def begin(self):
        self.send(0)

    def send(self, s):
        for b, buf in enumerate(self.bufs):
            for f, flow in enumerate(flows_of(self.ring.count, buf.shape[1])):
                if s > 0 and s <= flow.hops:
                    self.moves[b, f].wait_recv()
                if s < flow.hops:
                    ref = functools.partial(part_of, buf, self.ring.at(-flow.sign * s), flow.rows)
                    self.moves[b, f] = self.links.start(ref, ref, {"dp": self.ring.at(flow.sign)})

    def step(self):
        if self.done < self.last:
            self.done += 1
            self.send(self.done)

    def finish(self):
        while self.done < self.last:
            self.step()


class Collect:
    def __init__(self, links, ring, bufs, gots):
        self.links, self.ring = links, ring
        self.bufs, self.gots = bufs, gots
        self.done = 0
        self.last = max(f.hops for f in flows_of(ring.count, bufs[0].shape[1]))
        self.moves = {}

    def begin(self):
        self.send(0)

    def send(self, s):
        for b, (buf, got) in enumerate(zip(self.bufs, self.gots)):
            for f, flow in enumerate(flows_of(self.ring.count, buf.shape[1])):
                if s > 0 and s <= flow.hops:
                    self.moves[b, f].wait_recv()
                if s < flow.hops:
                    owner = self.ring.at(flow.sign * (flow.hops - s))
                    if s > 0:
                        both = buf[owner, flow.rows].astype(f32) + got[flow.slot + s - 1, flow.rows].astype(f32)
                        buf[owner, flow.rows] = both.astype(bf16)
                    self.moves[b, f] = self.links.start(
                        functools.partial(part_of, buf, owner, flow.rows),
                        functools.partial(part_of, got, flow.slot + s, flow.rows),
                        {"dp": self.ring.at(flow.sign)},
                    )

    def step(self):
        if self.done < self.last:
            self.done += 1
            self.send(self.done)

    def finish(self):
        while self.done < self.last:
            self.step()

    def take(self, b, out_ref, columns):
        buf, got = self.bufs[b], self.gots[b]
        mine = self.ring.at(0)
        flows = flows_of(self.ring.count, buf.shape[1])
        for start in sorted({flow.rows.start for flow in flows}):
            total = None
            for flow in flows:
                if flow.rows.start == start:
                    part = got[flow.slot + flow.hops - 1, flow.rows].astype(f32)
                    total = buf[mine, flow.rows].astype(f32) + part if total is None else total + part
                    rows = flow.rows
            out_ref[rows, columns] = total


IN_BOTH = (
    "x_ref", "og_ref", "doc_ref", "kind_ref", "cb_ref", "pb_ref", "tbias_ref", "vb_ref", "te_ref", "ib_ref", "ab_ref",
    "fb_ref", "ag_ref", "as_ref", "fg_ref", "fs_ref", "ta_ref", "tb_ref",
)
IN_RING = (
    "wq_ref", "wk_ref", "wv_ref", "wp_ref", "wo_ref", "wi_ref", "wu_ref",
)
IN_WHOLE = (
    "w1g", "wog", "wig", "wug",
)
OUT_WHOLE = (
    "dwa", "dwb", "dwo", "dwi", "dwu",
)


def layer_kernel(ring_on, names, *refs):
    r = dict(zip(names, refs, strict=True))
    (x_ref, og_ref, doc_ref, kind_ref, cb_ref, pb_ref, tbias_ref, vb_ref, te_ref, ib_ref,
     ab_ref, fb_ref, ag_ref, as_ref, fg_ref, fs_ref, ta_ref, tb_ref) = (r[n] for n in IN_BOTH)
    w1g, wog, wig, wug = (r[n] for n in IN_WHOLE)
    dwa, dwb, dwo, dwi, dwu = (r[n] for n in OUT_WHOLE)
    out_ref, ig_ref = r["out_ref"], r["ig_ref"]
    vec_ref, hs_ref = r["vec"], r["hs"]
    (xs, hb, eb2, eb1, part_a, part_b, r1a, r1b, r2a, r2b, sxa, sxb, own_f,
     table, rel, qa, qr, ka, va, q32, es, a32, attnp, act, slope, igr,
     h1, n1, e2, inv1, e1, dkv, drt, dqkv, flip, qmeta_ref, kmeta_ref, small_ref, per_head, ln_ref, ibs,
     send_sems, recv_sems) = (r[n] for n in SCRATCH)
    rows = x_ref.shape[0]
    width = x_ref.shape[1]
    hidden = wig.shape[2]
    members = xs.shape[0]
    seq = members * rows
    heads = es.shape[0]
    half = width // 2
    scale = 0.125
    me = lax.axis_index("mp")
    core = lax.rem(me, 2)
    side = lax.div(me, 2)
    mate = me + 1 - 2 * core
    across = lax.rem(me + 2, 4)
    diag = lax.rem(mate + 2, 4)
    links = Links(send_sems, recv_sems)
    to_mate = {"mp": mate}
    to_across = {"mp": across}

    barrier = pltpu.get_barrier_semaphore()
    peers = [to_mate, to_across]
    if ring_on:
        ring = Ring(w1g.shape[0])
        peers += [{"dp": ring.at(1)}, {"dp": ring.at(-1)}]
    for where in peers:
        pl.semaphore_signal(barrier, inc=1, device_id=where, device_id_type=MESH)
    pl.semaphore_wait(barrier, len(peers))

    def whole(ref):
        return ref[...].reshape(width, ref.shape[2])

    def gather_start(buf):
        a = links.start(buf.at[me], buf.at[me], to_across)
        b = links.start(buf.at[me], buf.at[me], to_mate)
        return a, b

    def gather_forward(buf, first):
        first.wait_recv()
        return links.start(buf.at[across], buf.at[across], to_mate)

    part_rows = rows // 2
    halves = [pl.ds(0, part_rows), pl.ds(part_rows, part_rows)]
    near_pair, far_pair = pl.ds(2 * side, 2), pl.ds(2 * (1 - side), 2)

    class Gather:
        def __init__(self, buf, x):
            self.buf, self.x = buf, x
            mine_x = buf.at[me, halves[x]]
            self.over = links.start(mine_x, mine_x, to_across)
            self.beside = links.start(mine_x, mine_x, to_mate)

        def forward(self):
            self.over.wait_recv()
            theirs = self.buf.at[across, halves[self.x]]
            self.last = links.start(theirs, theirs, to_mate)

    xs[me] = x_ref[...]
    x_a, x_b = gather_start(xs)

    if ring_on:
        shard = w1g.shape[1]
        mine = ring.at(0)
        own_f[...] = jnp.zeros(own_f.shape, f32)
        tiles = []
        for i, name in enumerate(IN_RING[:4]):
            r0, c0 = 128 * (i // 2), 256 * (i % 2)
            own_f[r0 : r0 + shard, c0 : c0 + r[name].shape[1]] = r[name][...].astype(f32)
            tiles.append((own_f[r0 : r0 + shard, c0 : c0 + 128], own_f[r0 : r0 + shard, c0 + 128 : c0 + 256]))
        (qx, qy), (kx, ky), (vx, vy), (px, py) = tiles
        low = lane_of(shard) < 64
        joined = [
            jnp.where(low, kx, swap(vx)),
            jnp.where(low, swap(kx), vx),
            jnp.where(low, ky, swap(vy)),
            qx,
            jnp.where(low, qy, swap(px)),
            jnp.where(low, swap(px), swap(py)),
        ]
        for i, tile in enumerate(joined):
            w1g[mine, :, 128 * i : 128 * i + 128] = tile.astype(bf16)
        spread_1 = Spread(links, ring, [w1g])
        spread_1.begin()
        wo_ref = r["wo_ref"]
        own_f[:, :128] = jnp.zeros((256, 128), f32)
        own_f[: wo_ref.shape[0], :shard] = wo_ref[...].astype(f32)
        wog[mine] = jnp.transpose(own_f[:, :128], (1, 0))[:shard].astype(bf16)
        wig[mine] = r["wi_ref"][...]
        wug[mine] = r["wu_ref"][...]
        spread_o, spread_i, spread_u = (Spread(links, ring, [ref]) for ref in (wog, wig, wug))

    small_ref[...] = jnp.zeros(small_ref.shape, f32)
    for h in range(heads):
        for i, ref in enumerate((cb_ref, pb_ref, tbias_ref)):
            small_ref[h, i : i + 1, 0:64] = ref[h : h + 1, :]
        small_ref[h, 3:5, 0:64] = te_ref[h]
        small_ref[h, 5:6, 0:64] = vb_ref[h : h + 1, :]
    for i, ref in enumerate((ab_ref, ag_ref, as_ref, fb_ref, fg_ref, fs_ref)):
        ln_ref[i : i + 1, :] = ref[...].reshape(1, width)
    ibs[0:1, :] = ib_ref[...].reshape(1, hidden)

    slots = seq // DOC_LEAST + 2
    ends = (doc_ref[...].reshape(1, seq) - lax.axis_index("dp") * seq).astype(f32)
    slot = jnp.where(ends > seq - 1.5, slots - 1.0, jnp.floor((ends + 0.5) * (1.0 / DOC_LEAST)))
    slot = jnp.transpose(jnp.broadcast_to(slot, (128, seq)), (1, 0))
    kind = jnp.transpose(jnp.broadcast_to(kind_ref[...].reshape(1, seq).astype(f32), (128, seq)), (1, 0))
    lane = lane_of(seq)
    hit = jnp.abs(slot + 68.0 - lane.astype(f32)) < 0.5
    qmeta_ref[...] = jnp.where(lane == 64, kind, jnp.where(hit, 1.0, 0.0)).astype(bf16)
    miss = jnp.where(hit, 0.0, MASK)
    kmeta_ref[...] = jnp.where(
        lane < 66, 1.0, jnp.where(lane < 68, kind, jnp.where(lane < 68 + slots, miss, 0.0))
    ).astype(bf16)
    if ring_on:
        spread_1.step()

    steps = tb_ref.shape[1]

    def table_step(u, carry):
        sa = ta_ref[0, pl.ds(u, 1), :]
        ca = ta_ref[1, pl.ds(u, 1), :]
        at = pl.multiple_of(u * steps, steps)
        table[pl.ds(at, steps), :half] = (sa * tb_ref[1] - ca * tb_ref[0]).astype(bf16)
        table[pl.ds(at, steps), half:] = (ca * tb_ref[1] + sa * tb_ref[0]).astype(bf16)
        return carry

    lax.fori_loop(0, ta_ref.shape[1] // 2, table_step, 0)
    if ring_on:
        spread_1.step()
    x_f = gather_forward(xs, x_a)
    lax.fori_loop(ta_ref.shape[1] // 2, ta_ref.shape[1], table_step, 0)

    ri = lax.broadcasted_iota(jnp.int32, (rows, rows), 0)
    ci = lax.broadcasted_iota(jnp.int32, (rows, rows), 1)
    flip[...] = jnp.where(ri + ci == rows - 1, 1.0, 0.0).astype(bf16)
    if ring_on:
        spread_1.step()
        spread_o.begin()
        spread_1.finish()

    def rel_step(i, carry):
        at = pl.ds(pl.multiple_of(i * 256, 256), 256)
        got = mm(table[at, :], w1g[:, :, 512:768].reshape(width, 256), NN)
        rel[0, at, :] = low_half(swap(got[:, :128])).astype(bf16)
        rel[1, at, :] = low_half(got[:, 128:]).astype(bf16)
        rel[2, at, :] = low_half(swap(got[:, 128:])).astype(bf16)
        return carry

    lax.fori_loop(0, 2 * seq // 256, rel_step, 0)

    def project(o, carry):
        at = pl.ds(pl.multiple_of(o * rows, rows), rows)
        got = mm(xs[o], w1g[:, :, :640].reshape(width, 640), NN)
        lane = lane_of(rows)
        qmeta = qmeta_ref[at, :].astype(f32)
        kmeta = kmeta_ref[at, :].astype(f32)
        typed = qmeta[:, 64:65]
        for h in range(heads):
            kv = got[:, 128 * h : 128 * h + 128]
            ka[h, at, :] = jnp.where(lane < 64, kv, kmeta).astype(bf16)
            vrow = swap(kv) + small_ref[h, 5:6, :]
            va[h, at, :] = jnp.where(lane < 64, vrow, jnp.where(lane < 66, 1.0, 0.0)).astype(bf16)
            q = got[:, 384:512] if h < 2 else got[:, 512:640]
            if h == 1:
                q = swap(q)
            q = low_half(q)
            q32[h, at, :] = q
            qt = q + small_ref[h, 2:3, :]
            ct0 = jnp.sum(qt * small_ref[h, 3:4, :], axis=1, keepdims=True)
            ct1 = jnp.sum(qt * small_ref[h, 4:5, :], axis=1, keepdims=True)
            diff = (ct1 - ct0) * scale
            base = ct0 * scale + diff * (1.0 - typed)
            tilt = diff * (2.0 * typed - 1.0)
            base_hi = base.astype(bf16).astype(f32)
            tilt_hi = tilt.astype(bf16).astype(f32)
            extra = jnp.where(
                lane == 64,
                base_hi,
                jnp.where(
                    lane == 65,
                    base - base_hi,
                    jnp.where(lane == 66, tilt_hi, jnp.where(lane == 67, tilt - tilt_hi, qmeta)),
                ),
            )
            qc = (q + small_ref[h, 0:1, :]) * scale
            qa[h, at, :] = jnp.where(lane < 64, qc, extra).astype(bf16)
            qr[h, at, :] = low_half((q + small_ref[h, 1:2, :]) * scale).astype(bf16)
        return carry

    def poll(*steppers):
        for stepper in steppers:
            stepper.step()

    if ring_on:
        spread_o.step()
        spread_i.begin()
    x_b.wait_recv()
    x_f.wait_recv()
    lax.fori_loop(0, members, project, 0)
    if ring_on:
        poll(spread_o)
        spread_u.begin()

    wide = seq + rows

    def hooked(hooks, h):
        for when, hook in (hooks or {}).items():
            pl.when(h == when)(hook)

    def attend(o, hooks=None):
        at = pl.ds(pl.multiple_of(o * rows, rows), rows)
        window = pl.ds(pl.multiple_of((members - 1 - o) * rows, rows), wide)

        def one_head(h, carry):
            hooked(hooks, h)
            s = mm(qa[h, at, :], ka[h], NT)
            g = mm(qr[h, at, :], rel[h, window, :], NT)
            g = pltpu.roll(g, wide + 1 - rows, 1, stride=1, stride_axis=0)
            s = s + g[:, :seq]
            top = jnp.max(s, axis=1, keepdims=True)
            e = jnp.exp(s - top).astype(bf16)
            es[h, at, :] = e
            o_full = mm(e, va[h], NN)
            inv = 1.0 / o_full[:, 64:65]
            a32[h, at, :] = jnp.where(lane_of(rows) < 64, o_full * inv, inv)
            return carry

        lax.fori_loop(0, heads, one_head, 0)
        first = low_half(a32[0, at, :]) + swap(low_half(a32[1, at, :]))
        attnp[at, :128] = first.astype(bf16)
        attnp[at, 128:] = low_half(a32[2, at, :]).astype(bf16)

    def branch_of(o):
        return mm(attnp[pl.ds(pl.multiple_of(o * rows, rows), rows), :], whole(wog), NT)

    class Scatter:
        def __init__(self, part, r1, r2, sx):
            self.part, self.r1, self.r2, self.sx = part, r1, r2, sx
            self.far, self.near, self.over = [None, None], [None, None], [None, None]

        def give_diag(self, x, value):
            self.part[diag, halves[x]] = value.astype(bf16)
            self.far[x] = links.start(self.part.at[diag, halves[x]], self.r1.at[1 - side, halves[x]], to_mate)

        def give_across(self, x, value):
            self.part[across, halves[x]] = value.astype(bf16)

        def give_mate(self, x, value):
            self.part[mate, halves[x]] = value.astype(bf16)
            self.near[x] = links.start(self.part.at[mate, halves[x]], self.r1.at[side, halves[x]], to_mate)

        def give_own(self, x, value):
            own_f[halves[x]] = value

        def give_near(self, x, pair):
            self.give_mate(x, jnp.where(core == 0, pair[1], pair[0]))
            self.give_own(x, jnp.where(core == 0, pair[0], pair[1]))

        def give_far(self, x, pair):
            self.give_diag(x, jnp.where(core == 0, pair[1], pair[0]))
            self.give_across(x, jnp.where(core == 0, pair[0], pair[1]))

        def pass_on(self, x):
            self.far[x].wait_recv()
            both = self.part[across, halves[x]].astype(f32) + self.r1[1 - side, halves[x]].astype(f32)
            self.sx[halves[x]] = both.astype(bf16)
            self.over[x] = links.start(
                functools.partial(part_of, self.sx, halves[x]), functools.partial(part_of, self.r2, halves[x]), to_across
            )

        def release(self):
            links.drain(self.far + self.near + self.over)

        def take(self, x):
            self.near[x].wait_recv()
            near = own_f[halves[x]] + self.r1[side, halves[x]].astype(f32)
            self.over[x].wait_recv()
            return near + self.r2[halves[x]].astype(f32)

    def split(value):
        return value[:part_rows], value[part_rows:]

    first_red = red = Scatter(part_a, r1a, r2a, sxa)

    def first_pass():
        red.pass_on(0)
        red.pass_on(1)

    def polls(**at):
        return {int(when[1:]): functools.partial(poll, *steppers) for when, steppers in at.items()}

    attend(diag, polls(h2=(spread_o, spread_i)) if ring_on else None)
    attend(across, polls(h1=(spread_u,), h2=(spread_o,)) if ring_on else None)
    if ring_on:
        spread_o.finish()
        poll(spread_i)
    for x, (there, here) in enumerate(zip(split(branch_of(diag)), split(branch_of(across)))):
        red.give_diag(x, there)
        red.give_across(x, here)
    attend(mate, {1: first_pass} | (polls(h2=(spread_u,)) if ring_on else {}))
    for x, value in enumerate(split(branch_of(mate))):
        red.give_mate(x, value)
    if ring_on:
        poll(spread_i)
    attend(me, polls(h2=(spread_u,)) if ring_on else None)
    for x, value in enumerate(split(branch_of(me))):
        red.give_own(x, value)
    vec_ref[...] = jnp.zeros((8, width), f32)
    hs_ref[...] = jnp.zeros(hs_ref.shape, f32)

    def first_norm(x):
        at = halves[x]
        summed = x_ref[at, :].astype(f32) + first_red.take(x) + ln_ref[0:1, :]
        normed, inv_std = norm_stats(summed)
        n1[at, :] = normed
        inv1[at, :] = jnp.broadcast_to(inv_std, (part_rows, 128))
        h1[at, :] = normed * ln_ref[1:2, :] + ln_ref[2:3, :]
        hb[me, at] = h1[at, :].astype(bf16)
        return Gather(hb, x)

    def ffn(pair, x):
        inner = mm(hb[pair, halves[x]].reshape(rows, width), whole(wig), NN) + ibs[0:1, :]
        square = inner * inner
        t = jnp.tanh(0.7978845608028654 * (inner + 0.044715 * square * inner))
        made = (0.5 * inner * (1.0 + t)).astype(bf16)
        act[pair, halves[x]] = made.reshape(2, part_rows, hidden)
        steep = (
            0.5 * (1.0 + t)
            + 0.5 * inner * (1.0 - t * t) * 0.7978845608028654 * (1.0 + 3.0 * 0.044715 * square)
        ).astype(bf16)
        slope[pair, halves[x]] = steep.reshape(2, part_rows, hidden)
        return mm(made, whole(wug), NT).reshape(2, part_rows, width)

    def stage(start, block, reducer, ready=None):
        moves = [start(0), start(1)]
        if ready:
            ready()
        for x in (0, 1):
            moves[x].beside.wait_recv()
            reducer.give_near(x, block(near_pair, x))
        moves[0].forward()
        moves[0].last.wait_recv()
        reducer.give_far(0, block(far_pair, 0))
        moves[1].forward()
        reducer.pass_on(0)
        moves[1].last.wait_recv()
        reducer.give_far(1, block(far_pair, 1))
        reducer.pass_on(1)

    def weights_ready():
        spread_i.finish()
        spread_u.finish()

    second_red = red = Scatter(part_b, r1b, r2b, sxb)
    stage(first_norm, ffn, second_red, weights_ready if ring_on else None)

    def second_norm(x):
        at = halves[x]
        summed = h1[at, :] + second_red.take(x) + ln_ref[3:4, :]
        normed, inv_std = norm_stats(summed)
        out_ref[at, :] = (normed * ln_ref[4:5, :] + ln_ref[5:6, :]).astype(bf16)
        grad = og_ref[at, :].astype(f32)
        back = norm_back(grad, normed, inv_std, ln_ref[4:5, :])
        e2[at, :] = back
        eb2[me, at] = back.astype(bf16)
        move = Gather(eb2, x)
        vec_ref[4:5, :] += col_sum(grad * normed)
        vec_ref[5:6, :] += col_sum(grad)
        vec_ref[1:2, :] += col_sum(back)
        return move

    def ffn_back(pair, x):
        steep = slope[pair, halves[x]].reshape(rows, hidden).astype(f32)
        grad_inner = (mm(eb2[pair, halves[x]].reshape(rows, width), whole(wug), NN) * steep).astype(bf16)
        igr[pair, halves[x]] = grad_inner.reshape(2, part_rows, hidden)
        vec_ref[6:7, :hidden] += col_sum(grad_inner.astype(f32))
        return mm(grad_inner, whole(wig), NT).reshape(2, part_rows, width)

    third_red = Scatter(part_a, r1a, r2a, sxa)
    stage(second_norm, ffn_back, third_red, first_red.release)
    flat = lambda ref: ref[...].reshape(seq, ref.shape[2])

    def put(ref, value):
        ref[...] = value.astype(bf16).reshape(ref.shape)

    def third_norm(x):
        at = halves[x]
        grad = e2[at, :] + third_red.take(x)
        back = norm_back(grad, n1[at, :], inv1[at, :1], ln_ref[1:2, :])
        e1[at, :] = back
        eb1[me, at] = back.astype(bf16)
        move = Gather(eb1, x)
        vec_ref[2:3, :] += col_sum(grad * n1[at, :])
        vec_ref[3:4, :] += col_sum(grad)
        vec_ref[0:1, :] += col_sum(back)
        return move

    put(dwu, mm(flat(eb2), flat(act), TN))
    if ring_on:
        collect_u = Collect(links, ring, [dwu], [r["gwu"]])
        collect_u.begin()
    g_0 = third_norm(0)
    put(dwi, mm(flat(hb), flat(igr), TN))
    if ring_on:
        collect_i = Collect(links, ring, [dwi], [r["gwi"]])
        collect_i.begin()
    g_1 = third_norm(1)
    if ring_on:
        vec_all, vec_mp = r["vec_all"], r["vec_mp"]
        vec_all[mine] = vec_ref[...]
        spread_4 = Spread(links, ring, [vec_all])
        spread_4.begin()

    dkv[...] = jnp.zeros(dkv.shape, f32)
    drt[...] = jnp.zeros(drt.shape, f32)

    def attend_back(o, hooks=None):
        at = pl.ds(pl.multiple_of(o * rows, rows), rows)
        lo = pl.multiple_of((members - 1 - o) * rows, rows)
        window = pl.ds(lo, wide)
        d_all = mm(eb1[o], whole(wog), NN).astype(bf16).astype(f32)
        lane = lane_of(rows)
        typed = qmeta_ref[at, :].astype(f32)[:, 64:65]
        per_head[0] = d_all[:, :128]
        per_head[1] = swap(d_all[:, :128])
        per_head[2] = d_all[:, 128:]

        def one_head(h, carry):
            hooked(hooks, h)
            d_out = per_head[h]
            kept = a32[h, at, :]
            d_out = low_half(d_out * kept[:, 64:65]).astype(bf16).astype(f32)
            d_row = -jnp.sum(d_out * kept, axis=1, keepdims=True)
            d_hi = d_row.astype(bf16).astype(f32)
            d_aug = jnp.where(lane == 64, d_hi, jnp.where(lane == 65, d_row - d_hi, d_out)).astype(bf16)
            e = es[h, at, :]
            ds = (e.astype(f32) * mm(d_aug, va[h], NT)).astype(bf16)
            dkv[h, 64:128, :] += mm(d_aug, e, TN)[:64]
            dkv[h, 0:64, :] += mm(qa[h, at, :], ds, TN)[:64]
            dq = mm(ds, ka[h], NN) * scale
            turned = mm(flip[...], ds, NN)
            turned = jnp.concatenate([turned, jnp.zeros((rows, rows), f32)], axis=1)
            dg = pltpu.roll(turned, 0, 1, stride=1, stride_axis=0).astype(bf16)
            dqr = mm(dg, rel[h, window, :], NN) * scale
            qr_turned = mm(flip[...], qr[h, at, :], NN).astype(bf16)
            drt[pl.ds(pl.multiple_of(64 * h + 64, 64), 64), window] += mm(qr_turned, dg, TN)[:64]
            hs_ref[h, 1:2, :] += col_sum(dqr)
            dqr_hi = dqr.astype(bf16)
            dqr_lo = (dqr - dqr_hi.astype(f32)).astype(bf16)
            dqr = mm(flip[...], dqr_hi, NN) + mm(flip[...], dqr_lo, NN)
            total = dq[:, 64:65]
            ones = dq[:, 66:67]
            same = jnp.where(typed > 0.5, ones, total - ones)
            other = total - same
            dqt = other * small_ref[h, 3:4, :] + same * small_ref[h, 4:5, :]
            qt = q32[h, at, :] + small_ref[h, 2:3, :]
            hs_ref[h, 0:1, :] += col_sum(dq)
            hs_ref[h, 2:3, :] += col_sum(dqt)
            hs_ref[h, 3:4, :] += col_sum(other * qt)
            hs_ref[h, 4:5, :] += col_sum(same * qt)
            per_head[h] = low_half(dq + dqr + dqt)
            return carry

        lax.fori_loop(0, heads, one_head, 0)
        dqkv[at, 384:512] = (per_head[0] + swap(per_head[1])).astype(bf16)
        dqkv[at, 512:640] = per_head[2].astype(bf16)

    attend_back(me, polls(h2=(collect_u,)) if ring_on else None)
    g_0.beside.wait_recv()
    g_1.beside.wait_recv()
    g_0.forward()
    g_1.forward()
    if ring_on:
        poll(spread_4, collect_i)
    attend_back(mate, polls(h1=(spread_4,), h2=(collect_u,)) if ring_on else None)
    if ring_on:
        poll(spread_4, collect_i)
    attend_back(across, polls(h1=(collect_u,), h2=(collect_i,)) if ring_on else None)
    g_0.last.wait_recv()
    g_1.last.wait_recv()
    put(dwo, mm(flat(eb1), attnp[...], TN))
    if ring_on:
        spread_4.finish()
        total = vec_all[0]
        for i in range(1, ring.count):
            total = total + vec_all[i]
        vec_mp[me] = total
        v_a, v_b = gather_start(vec_mp)
        collect_2 = Collect(links, ring, [dwo], [r["gwo"]])
        collect_2.begin()
    attend_back(diag, polls(h2=(collect_2,)) if ring_on else None)
    if ring_on:
        poll(collect_2)
        v_b.wait_recv()
        v_f = gather_forward(vec_mp, v_a)

    for h in range(heads):
        turned = jnp.transpose(dkv[h], (1, 0)).astype(bf16)
        dqkv[:, 128 * h : 128 * h + 128] = turned
        hs_ref[h, 5:6, :] = swap(col_sum(turned.astype(f32)))
    put(dwa, mm(flat(xs), dqkv[:, :512], TN))
    if ring_on:
        hs_all = r["hs_all"]
        hs_all[mine] = hs_ref[...].reshape(8 * heads, 128)
        spread_5 = Spread(links, ring, [hs_all])
        spread_5.begin()
        collect_3 = Collect(links, ring, [dwa], [r["gwa"]])
        collect_3.begin()

    def input_back(o):
        at = pl.ds(pl.multiple_of(o * rows, rows), rows)
        return mm(dqkv[at, :], w1g[:, :, :640].reshape(width, 640), NT)

    second_red.release()
    red = Scatter(part_b, r1b, r2b, sxb)
    for x, value in enumerate(split(input_back(diag))):
        red.give_diag(x, value)
    for x, value in enumerate(split(input_back(across))):
        red.give_across(x, value)
    tail = mm(flat(xs), dqkv[:, 512:640], TN)
    d_pos = jnp.transpose(mm(drt[...].astype(bf16), table[...], NN), (1, 0))
    put(dwb, jnp.concatenate([tail + d_pos[:, :128], d_pos[:, 128:]], axis=1))
    if ring_on:
        collect_4 = Collect(links, ring, [dwb], [r["gwb"]])
        collect_4.begin()
    red.pass_on(0)
    red.pass_on(1)
    if ring_on:
        poll(collect_2, collect_3, spread_5)
    for x, value in enumerate(split(input_back(mate))):
        red.give_mate(x, value)
    for x, value in enumerate(split(input_back(me))):
        red.give_own(x, value)
    if ring_on:
        grad_ref = r["grad_ref"]
        poll(collect_4, collect_3, spread_5)
        collect_u.finish()
        collect_i.finish()
        collect_u.take(0, grad_ref, pl.ds(1024 + hidden, hidden))
        poll(collect_2)
        collect_i.take(0, grad_ref, pl.ds(1024, hidden))
        poll(collect_4, collect_3, spread_5)
        v_f.wait_recv()
        r["vec_ref"][...] = vec_mp[0] + vec_mp[1] + vec_mp[2] + vec_mp[3]
        r["vec_ref"][6:7, :] = vec_mp[me][6:7, :]
        collect_2.finish()
        collect_2.take(0, grad_ref, pl.ds(768, 256))
        poll(collect_4, collect_3, spread_5)
    for x in (0, 1):
        ig_ref[halves[x], :] = (e1[halves[x], :] + red.take(x)).astype(bf16)
    if ring_on:
        spread_5.finish()
        total = hs_all[0]
        for i in range(1, ring.count):
            total = total + hs_all[i]
        r["hs_ref"][...] = total
        collect_3.finish()
        collect_3.take(0, grad_ref, pl.ds(0, 512))
        collect_4.finish()
        collect_4.take(0, grad_ref, pl.ds(512, 256))
    else:
        r["vec_ref"][...] = vec_ref[...]
        r["hs_ref"][...] = hs_ref[...].reshape(8 * heads, 128)
    links.drain()


SCRATCH = (
    "xs", "hb", "eb2", "eb1", "part_a", "part_b", "r1a", "r1b", "r2a", "r2b", "sxa", "sxb", "own_f", "table", "rel",
    "qa", "qr", "ka", "va", "q32", "es", "a32", "attnp", "act", "slope", "igr", "h1", "n1", "e2", "inv1", "e1", "dkv",
    "drt", "dqkv", "flip", "qmeta", "kmeta", "small", "per_head", "ln", "ibs", "send_sems", "recv_sems",
)


def finish_kernel(
    out_ref, ig_ref, grad_ref, vec_ref, hs_ref,
    out, in_grad, wq, wk, wv, wp, wo, wi, wu, cb, pb, tbias, vb, te, ib, ab, fb, ag, ash, fg, fs, turn,
):
    out[...] = out_ref[...]
    in_grad[...] = ig_ref[...]
    shard, hidden = wi.shape
    t = [grad_ref[:, 128 * i : 128 * i + 128].astype(f32) for i in range(6)]
    low = lane_of(shard) < 64
    wk[:, :128] = jnp.where(low, t[0], swap(t[1]))
    wk[:, 128:] = t[2][:, :64]
    wv[:, :128] = jnp.where(low, swap(t[0]), t[1])
    wv[:, 128:] = swap(t[2])[:, :64]
    wq[:, :128] = t[3]
    wq[:, 128:] = t[4][:, :64]
    wp[:, :128] = jnp.where(low, swap(t[4]), swap(t[5]))
    wp[:, 128:] = swap(t[5])[:, :64]
    turn[...] = jnp.zeros(turn.shape, f32)
    turn[:shard, :] = grad_ref[:, 768:1024].astype(f32)
    wo[...] = jnp.transpose(turn[...], (1, 0))[: wo.shape[0], :shard]
    wi[...] = grad_ref[:, 1024 : 1024 + hidden].astype(f32)
    wu[...] = grad_ref[:, 1024 + hidden :].astype(f32)
    for h in range(cb.shape[0]):
        for i, ref in ((0, cb), (1, pb), (2, tbias), (5, vb)):
            ref[h : h + 1, :] = hs_ref[8 * h + i : 8 * h + i + 1, :64]
        te[h] = hs_ref[8 * h + 3 : 8 * h + 5, :64]
    ib[...] = vec_ref[6:7, :hidden].reshape(hidden)
    for i, ref in enumerate((ab, fb, ag, ash, fg, fs)):
        ref[...] = vec_ref[i : i + 1, :].reshape(ref.shape[0])


def angle_tables(seq, width):
    half = width // 2
    freq = 1.0 / 10000.0 ** (np.arange(half, dtype=np.float64) * (2.0 / width))
    steps = 32
    coarse = (seq - 1 - steps * np.arange(2 * seq // steps, dtype=np.float64))[:, None] * freq[None, :]
    fine = np.arange(steps, dtype=np.float64)[:, None] * freq[None, :]
    return (
        np.stack([np.sin(coarse), np.cos(coarse)]).astype(np.float32),
        np.stack([np.sin(fine), np.cos(fine)]).astype(np.float32),
    )


def per_device(
    layer_input, doc_ids, type_ids, positions, query_weight, key_weight, value_weight, pos_kernel,
    out_weight, inner_weight, outer_weight, content_bias, pos_bias, type_bias, value_bias, type_embed,
    inner_bias, attn_bias, ffn_bias, attn_gain, attn_shift, ffn_gain, ffn_shift, out_grad,
):
    rows, width = layer_input.shape
    seq = doc_ids.shape[0]
    heads, depth = content_bias.shape
    hidden = inner_weight.shape[1]
    shard = query_weight.shape[0]
    members = seq // rows
    count = width // shard
    cols = heads * depth
    ring_on = shard % 16 == 0 and count % 2 == 0 and count > 2

    type_rows = jnp.transpose(type_embed, (1, 0, 2))
    ta, tb = angle_tables(seq, width)
    given = [
        layer_input, out_grad, doc_ids, type_ids, content_bias, pos_bias, type_bias, value_bias, type_rows, inner_bias,
        attn_bias, ffn_bias, attn_gain, attn_shift, ffn_gain, ffn_shift, ta, tb,
    ]
    sds = jax.ShapeDtypeStruct
    vm = pltpu.VMEM
    blocks = count if ring_on else 1
    deep = width // blocks
    full = {
        "w1g": 768, "wog": 256, "wig": hidden, "wug": hidden,
        "dwa": 512, "dwb": 256, "dwo": 256, "dwi": hidden, "dwu": hidden,
    }
    outs = {
        "out_ref": sds((rows, width), bf16), "ig_ref": sds((rows, width), bf16),
        "vec_ref": sds((8, width), f32), "hs_ref": sds((8 * heads, 128), f32),
    }
    extra = {"vec": vm((8, width), f32), "hs": vm((heads, 8, 128), f32)}
    if ring_on:
        given += [query_weight, key_weight, value_weight, pos_kernel, out_weight, inner_weight, outer_weight.T]
        names = IN_BOTH + IN_RING
        outs["grad_ref"] = sds((shard, 1024 + 2 * hidden), f32)
        extra |= {name: vm((blocks, deep, wide), bf16) for name, wide in full.items()}
        for name in OUT_WHOLE:
            extra["g" + name[1:]] = vm((blocks - 1, deep, full[name]), bf16)
        extra["vec_all"] = vm((blocks, 8, width), f32)
        extra["vec_mp"] = vm((members, 8, width), f32)
        extra["hs_all"] = vm((blocks, 8 * heads, 128), f32)
    else:
        q3, k3, v3 = (w.reshape(shard, heads, depth) for w in (query_weight, key_weight, value_weight))
        kv = jnp.stack([k3, v3], axis=2).reshape(shard, 2 * cols)
        out_t = jnp.pad(out_weight.T, ((0, 0), (0, 256 - cols)))
        mine = jnp.concatenate([kv, query_weight, pos_kernel, out_t, inner_weight, outer_weight.T], axis=1)
        gathered = lax.all_gather(mine, "dp", axis=0, tiled=True)[None]
        bounds = np.cumsum([0] + [full[name] for name in IN_WHOLE])
        given += [gathered[:, :, lo:hi] for lo, hi in zip(bounds[:-1], bounds[1:])]
        names = IN_BOTH + IN_WHOLE
        outs |= {name: sds((1, width, full[name]), bf16) for name in OUT_WHOLE}

    block = (members, rows, width)
    per_head = (heads, seq, 128)
    scratch = {
        "xs": vm(block, bf16), "hb": vm(block, bf16), "eb2": vm(block, bf16), "eb1": vm(block, bf16),
        "part_a": vm(block, bf16), "part_b": vm(block, bf16),
        "r1a": vm((2, rows, width), bf16), "r1b": vm((2, rows, width), bf16),
        "r2a": vm((rows, width), bf16), "r2b": vm((rows, width), bf16),
        "sxa": vm((rows, width), bf16), "sxb": vm((rows, width), bf16),
        "own_f": vm((rows, width), f32), "table": vm((2 * seq, width), bf16), "rel": vm((heads, 2 * seq, 128), bf16),
        "qa": vm(per_head, bf16), "qr": vm(per_head, bf16), "ka": vm(per_head, bf16), "va": vm(per_head, bf16),
        "q32": vm(per_head, f32), "es": vm((heads, seq, seq), bf16), "a32": vm(per_head, f32),
        "attnp": vm((seq, 256), bf16), "act": vm((members, rows, hidden), bf16),
        "slope": vm((members, rows, hidden), bf16), "igr": vm((members, rows, hidden), bf16),
        "h1": vm((rows, width), f32), "n1": vm((rows, width), f32), "e2": vm((rows, width), f32),
        "inv1": vm((rows, 128), f32), "e1": vm((rows, width), f32), "dkv": vm((heads, 128, seq), f32),
        "drt": vm((256, 2 * seq), f32), "dqkv": vm((seq, 640), bf16), "flip": vm((rows, rows), bf16),
        "qmeta": vm((seq, 128), bf16), "kmeta": vm((seq, 128), bf16), "small": vm((heads, 8, 128), f32), "per_head": vm((heads, rows, 128), f32),
        "ln": vm((8, width), f32), "ibs": vm((8, hidden), f32),
        "send_sems": pltpu.SemaphoreType.DMA((192,)), "recv_sems": pltpu.SemaphoreType.DMA((192,)),
    }
    scratch |= extra
    inside = pl.BlockSpec(memory_space=pltpu.VMEM)
    made = pl.pallas_call(
        functools.partial(layer_kernel, ring_on, [*names, *outs, *scratch]),
        out_shape=list(outs.values()),
        in_specs=[inside] * len(given),
        out_specs=[inside] * len(outs),
        scratch_shapes=list(scratch.values()),
        compiler_params=pltpu.CompilerParams(collective_id=0, has_side_effects=True, vmem_limit_bytes=67043328),
        name="layer",
    )(*given)
    made = dict(zip(outs, made))

    if ring_on:
        grads, vec, hs = made["grad_ref"], made["vec_ref"], made["hs_ref"]
    else:
        grads = jnp.concatenate([made[name][0] for name in ("dwa", "dwb", "dwo", "dwi", "dwu")], axis=1)
        grads = lax.psum_scatter(grads, "dp", scatter_dimension=0, tiled=True).astype(f32)
        vec, hs = lax.psum((made["vec_ref"], made["hs_ref"]), "dp")
        vec = jnp.concatenate([lax.psum(vec[:6], "mp"), vec[6:]], axis=0)
    small = sds((heads, depth), f32)
    line = sds((width,), f32)
    results = pl.pallas_call(
        finish_kernel,
        out_shape=[
            made["out_ref"], made["ig_ref"], *[sds((shard, cols), f32)] * 4, sds((cols, shard), f32),
            sds((shard, hidden), f32), sds((shard, hidden), f32), *[small] * 4, sds((heads, 2, depth), f32),
            sds((hidden,), f32), *[line] * 6,
        ],
        in_specs=[inside] * 5,
        out_specs=[inside] * 21,
        scratch_shapes=[vm((128, 256), f32)],
        name="finish",
    )(made["out_ref"], made["ig_ref"], grads, vec, hs)
    results = list(results)
    results[8] = results[8].T
    results[13] = jnp.transpose(results[13], (1, 0, 2))
    return tuple(results)


def solution(mesh):
    rows = P(("dp", "mp"), None)
    token = P("dp")
    placed = (
        (rows, token, token, token)
        + (P("dp", "mp"),) * 4
        + (P("mp", "dp"), P("dp", "mp"), P("mp", "dp"))
        + (P("mp", None),) * 4
        + (P(None, "mp", None), P("mp"))
        + (P(),) * 6
        + (rows,)
    )
    given = (
        (rows, rows)
        + (P("dp", "mp"),) * 4
        + (P("mp", "dp"), P("dp", "mp"), P("mp", "dp"))
        + (P("mp", None),) * 4
        + (P(None, "mp", None), P("mp"))
        + (P(),) * 6
    )
    return jax.shard_map(per_device, mesh=mesh, in_specs=placed, out_specs=given, check_vma=False)
```
